32 devices in a mesh: groups: 2 (over x), height: 16 (over z, y, core).
Axes of the slice: x: 2, y: 2, z: 4, core: 2. Of those that a mesh axis runs over, the one named last changes fastest.
Arguments:
- frames: bfloat16 [4, 128, 32, 128], P('groups', 'height'), parts along dimension 0, may hold values from -6 to 6
- weight_a: bfloat16 [3, 3, 3, 128, 128], replicated, may hold values from -0.109375 to 0.109375
- weight_b: bfloat16 [3, 3, 3, 128, 256], replicated, may hold values from -0.109375 to 0.109375
- cotangent: bfloat16 [4, 64, 16, 256], P('groups', 'height'), parts along dimension 0, may hold values from -6 to 6
Outputs:
- encoded: bfloat16 [4, 64, 16, 256], P('groups', 'height'), parts along dimension 0
- frames_grad: bfloat16 [4, 128, 32, 128], P('groups', 'height'), parts along dimension 0
- weight_a_grad: bfloat16 [6, 3, 3, 128, 128], P('groups'), parts along dimension 0
- weight_b_grad: bfloat16 [6, 3, 3, 128, 256], P('groups'), parts along dimension 0
The draws below stay inside these ranges and needn't reach their ends.
There are 2 independent parts, one for each index of `groups`. The reference program is written for one: setup_inputs(seed, part) draws one part's arguments, and reference() takes and returns one part's arrays. A program takes and returns all parts, laid end to end along the dimension named above; an argument that names none is the same for every part. Nothing has to cross between parts.
All inputs are finite; a program needn't handle non-finite values.
Results may differ from the reference program's by a relative error of at most 0.0053.
Values may be sent and summed in bfloat16 or wider, within the bound.
No kernel may reach another device: no remote copies, remote signals or barrier semaphores. Data moves between devices by JAX's collectives and lax.ppermute only.
A program may use at most 64 MiB of HBM per device.

```python
import jax
import jax.numpy as jnp
from jax import lax

C = 128
C2 = 256
F = 2
W = 32
HEIGHT = 128


def shard_levels(key, extent, split, least, top_value):
    def one(position, parts):
        draws = jax.random.uniform(jax.random.fold_in(jax.random.fold_in(key, 6), position), (parts,), jnp.float32, least / len(split), top_value / len(split))
        return jnp.repeat(jnp.exp(draws), extent[position] // parts).reshape((-1,) + (1,) * (len(extent) - position - 1))

    level = one(*split[0])
    for cut in split[1:]:
        level = level * one(*cut)
    return level


def bell_draw(rng, extent, scale, most, pieces=(), dtype=jnp.bfloat16):
    values = scale * jax.random.normal(rng, extent, jnp.float32)
    if pieces:
        values = values * shard_levels(rng, extent, pieces, -0.22, 0.18)
    return jnp.clip(values, -most, most).astype(dtype)


def setup_inputs(seed: int = 0, part: int = 0) -> dict:
    arg_keys = jax.random.split(jax.random.key(seed), 5)
    part_keys = jax.random.split(jax.random.fold_in(arg_keys[4], part), 5)
    return {
        "frames": bell_draw(part_keys[0], (F, HEIGHT, W, C), 1.0, 6.0, ((1, 16),)),
        "weight_a": bell_draw(arg_keys[1], (3, 3, 3, C, C), (27 * C) ** -0.5, 0.109375),
        "weight_b": bell_draw(arg_keys[2], (3, 3, 3, C, C2), (27 * C) ** -0.5, 0.109375),
        "cotangent": bell_draw(part_keys[3], (F, HEIGHT // 2, W // 2, C2), 1.0, 6.0, ((1, 16),)),
    }


def pad_time(field):
    return jnp.concatenate([field[:1], field[:1], field], axis=0)


def fold_time(grads):
    return grads[2:].at[0].add(grads[0] + grads[1])


def widen_full(field):
    padded = pad_time(field)
    zero_col = jnp.zeros_like(padded[:, :, :1])
    padded = jnp.concatenate([zero_col, padded, zero_col], axis=2)
    width = field.shape[2]
    return jnp.concatenate([padded[:, :, 0:width], padded[:, :, 1:width + 1], padded[:, :, 2:width + 2]], axis=3)


def widen_half(field):
    padded = pad_time(field)
    zero_col = jnp.zeros_like(padded[:, :, :1])
    padded = jnp.concatenate([zero_col, padded], axis=2)
    width = field.shape[2]
    return jnp.concatenate([padded[:, :, k:k + width - 1:2] for k in range(3)], axis=3)


def forward_a(stacked, kernel, rows):
    frames = stacked.shape[0] - 2
    width = stacked.shape[2]
    total = jnp.zeros((frames * rows * width, kernel.shape[-1]), jnp.float32)
    for kt in range(3):
        for kh in range(3):
            piece = stacked[kt:kt + frames, kh:kh + rows]
            total = total + jnp.dot(piece.reshape(-1, piece.shape[-1]), kernel[kt, kh], preferred_element_type=jnp.float32)
    return total.reshape(frames, rows, width, kernel.shape[-1])


def forward_b(stacked, kernel, rows):
    frames = stacked.shape[0] - 2
    width = stacked.shape[2]
    total = jnp.zeros((frames * rows * width, kernel.shape[-1]), jnp.float32)
    for kt in range(3):
        for kh in range(3):
            piece = stacked[kt:kt + frames, kh:kh + 2 * rows - 1:2]
            total = total + jnp.dot(piece.reshape(-1, piece.shape[-1]), kernel[kt, kh], preferred_element_type=jnp.float32)
    return total.reshape(frames, rows, width, kernel.shape[-1])


def backward_a(stacked, kernel, grad, rows):
    frames = stacked.shape[0] - 2
    width = stacked.shape[2]
    chans = grad.shape[-1]
    flat = grad.reshape(-1, chans)
    wgrad = []
    dstack = jnp.zeros(stacked.shape, jnp.float32)
    for kt in range(3):
        for kh in range(3):
            piece = stacked[kt:kt + frames, kh:kh + rows]
            wgrad.append(lax.dot_general(piece.reshape(-1, piece.shape[-1]), flat, (((0,), (0,)), ((), ())), preferred_element_type=jnp.float32))
            back = lax.dot_general(flat, kernel[kt, kh], (((1,), (1,)), ((), ())), preferred_element_type=jnp.float32)
            dstack = dstack.at[kt:kt + frames, kh:kh + rows].add(back.reshape(frames, rows, width, -1))
    return jnp.stack(wgrad).reshape(kernel.shape), dstack


def backward_b(stacked, kernel, grad, rows):
    frames = stacked.shape[0] - 2
    width = stacked.shape[2]
    flat = grad.reshape(-1, grad.shape[-1])
    wgrad = []
    dstack = jnp.zeros(stacked.shape, jnp.float32)
    for kt in range(3):
        for kh in range(3):
            piece = stacked[kt:kt + frames, kh:kh + 2 * rows - 1:2]
            wgrad.append(lax.dot_general(piece.reshape(-1, piece.shape[-1]), flat, (((0,), (0,)), ((), ())), preferred_element_type=jnp.float32))
            back = lax.dot_general(flat, kernel[kt, kh], (((1,), (1,)), ((), ())), preferred_element_type=jnp.float32)
            dstack = dstack.at[kt:kt + frames, kh:kh + 2 * rows - 1:2].add(back.reshape(frames, rows, width, -1))
    return jnp.stack(wgrad).reshape(kernel.shape), dstack


def unstack_full(dstack, chans):
    width = dstack.shape[2]
    shape = (dstack.shape[0], dstack.shape[1], width + 2, chans)
    total = jnp.zeros(shape, jnp.float32)
    for k in range(3):
        total = total.at[:, :, k:k + width].add(dstack[..., k * chans:(k + 1) * chans])
    return fold_time(total[:, :, 1:width + 1])


def unstack_half(dstack, chans, width):
    shape = (dstack.shape[0], dstack.shape[1], width + 1, chans)
    total = jnp.zeros(shape, jnp.float32)
    for k in range(3):
        total = total.at[:, :, k:k + width - 1:2].add(dstack[..., k * chans:(k + 1) * chans])
    return fold_time(total[:, :, 1:])


def reference(frames, weight_a, weight_b, cotangent):
    chans = frames.shape[-1]
    rows = frames.shape[1]
    width = frames.shape[2]
    kernel_a = weight_a.reshape(3, 3, 3 * chans, chans)
    kernel_b = weight_b.reshape(3, 3, 3 * chans, weight_b.shape[-1])
    zero_row = jnp.zeros_like(frames[:, :1])
    rows_ext = jnp.concatenate([zero_row, frames, zero_row], axis=1)
    stacked_a = widen_full(rows_ext)
    pre = frames.astype(jnp.float32) + forward_a(stacked_a, kernel_a, rows)
    sig = jax.nn.sigmoid(pre)
    act = (pre * sig).astype(jnp.bfloat16)
    act_ext = jnp.concatenate([jnp.zeros_like(act[:, :1]), act], axis=1)
    stacked_b = widen_half(act_ext)
    encoded = forward_b(stacked_b, kernel_b, rows // 2).astype(jnp.bfloat16)
    wgrad_b, dstack_b = backward_b(stacked_b, kernel_b, cotangent, rows // 2)
    act_grad = unstack_half(dstack_b, chans, width)[:, 1:]
    pre_grad = (act_grad * sig * (1.0 + pre * (1.0 - sig))).astype(jnp.bfloat16)
    wgrad_a, dstack_a = backward_a(stacked_a, kernel_a, pre_grad, rows)
    field_grad = unstack_full(dstack_a, chans)
    frames_grad = (pre_grad.astype(jnp.float32) + field_grad[:, 1:rows + 1]).astype(jnp.bfloat16)
    scale = (F * HEIGHT * W) ** -0.5
    weight_a_grad = (wgrad_a * scale).astype(jnp.bfloat16).reshape(weight_a.shape)
    weight_b_grad = (wgrad_b * scale).astype(jnp.bfloat16).reshape(weight_b.shape)
    return encoded, frames_grad, weight_a_grad, weight_b_grad
```

```python
import jax
import jax.numpy as jnp
from jax import lax
from jax.experimental import pallas as pl
from jax.experimental.pallas import tpu as pltpu
from jax.sharding import PartitionSpec as P

F32 = jnp.float32
BF16 = jnp.bfloat16
AXIS = "height"
VMEM_LIMIT = 48 * 1024 * 1024


def position():
    index = lax.axis_index(AXIS)
    return (index % 2, (index // 2) % 2, index // 4)


def mm(a, b):
    return lax.dot_general(a, b, (((1,), (0,)), ((), ())), preferred_element_type=F32)


def mm_nt(a, b):
    return lax.dot_general(a, b, (((1,), (1,)), ((), ())), preferred_element_type=F32)


def mm_tn(a, b):
    return lax.dot_general(a, b, (((0,), (0,)), ((), ())), preferred_element_type=F32)


def shifted(field, by, half):
    rows, _, chans = field.shape
    flat = field.reshape(rows * half, chans)
    column = lax.broadcasted_iota(jnp.int32, flat.shape, 0) % half
    moved = pltpu.roll(flat, by % (rows * half), axis=0)
    edge = 0 if by > 0 else half - 1
    return jnp.where(column == edge, 0.0, moved).reshape(field.shape)


def wide_pair(even, odd, half):
    before = shifted(odd, 1, half).astype(BF16)
    after = shifted(even, -1, half).astype(BF16)
    even, odd = (even.astype(BF16), odd.astype(BF16))
    return (
        jnp.concatenate([before, even, odd], axis=-1),
        jnp.concatenate([even, odd, after], axis=-1),
    )


def forward_kernel(
    own_f, other_f, halo_1f, halo_2f, own_g, other_g, halo_1g, halo_2g, weight_a,
    keep_b, send_b, pre_ref, stacked_a, stacked_b, cot_ref, flat,
):
    core, side, plane = position()
    frames, rows, width, chans = own_f.shape
    half = width // 2
    ext = 2 * rows + 4
    block = rows * width
    for t in range(frames):
        base = t * ext * width
        top = jnp.where(core == 0, halo_1f[t].astype(F32), halo_2f[t].astype(F32))
        low = jnp.where(core == 0, halo_2f[t].astype(F32), halo_1f[t].astype(F32))
        flat[base : base + 2 * width] = top.reshape(2 * width, chans)
        flat[base + (ext - 2) * width : base + ext * width] = low.reshape(2 * width, chans)
        at = pl.multiple_of(base + 2 * width + core * block, 2 * width)
        flat[pl.ds(at, block)] = own_f[t].astype(F32).reshape(block, chans)
        at = pl.multiple_of(base + 2 * width + (1 - core) * block, 2 * width)
        flat[pl.ds(at, block)] = other_f[t].astype(F32).reshape(block, chans)
        cot_ref[t, 0] = jnp.where(core == 0, halo_1g[t, 0], halo_2g[t, 0])
        cot_ref[t, rows + 1] = jnp.where(core == 0, halo_2g[t, 0], halo_1g[t, 0])
        cot_ref[t, pl.ds(1 + core * (rows // 2), rows // 2)] = own_g[t]
        cot_ref[t, pl.ds(1 + (1 - core) * (rows // 2), rows // 2)] = other_g[t]
    count = frames * ext
    even = flat[pl.ds(0, count * half, stride=2), :].reshape(count, half, chans)
    odd = flat[pl.ds(1, count * half, stride=2), :].reshape(count, half, chans)
    taps_even, taps_odd = wide_pair(even, odd, half)
    stacked_a[:, :, 0:half] = taps_even.reshape(frames, ext, half, 3 * chans)
    stacked_a[:, :, half:width] = taps_odd.reshape(frames, ext, half, 3 * chans)

    inner = ext - 2
    shared = jnp.zeros((inner * width, chans), F32)
    latest = [jnp.zeros((inner * width, chans), F32) for _ in range(2)]
    for kh in range(3):
        first = stacked_a[0, kh : kh + inner].reshape(inner * width, 3 * chans)
        second = stacked_a[1, kh : kh + inner].reshape(inner * width, 3 * chans)
        shared += mm(first, weight_a[0, kh]) + mm(first, weight_a[1, kh])
        latest[0] += mm(first, weight_a[2, kh])
        latest[1] += mm(second, weight_a[2, kh])
    even = even.reshape(frames, ext, half, chans)
    odd = odd.reshape(frames, ext, half, chans)
    outside = (plane == 0) & (side == 0)
    row = lax.broadcasted_iota(jnp.int32, (inner, half, chans), 0)
    hidden = outside & (row == 0)
    for t in range(frames):
        conv = (shared + latest[t]).reshape(inner, 2, half, chans)
        pre_even = even[t, 1 : ext - 1] + conv[:, 0]
        pre_odd = odd[t, 1 : ext - 1] + conv[:, 1]
        pre_ref[t, :, 0:half] = pre_even
        pre_ref[t, :, half:width] = pre_odd
        act_even = jnp.where(hidden, 0.0, pre_even * jax.nn.sigmoid(pre_even))
        act_odd = jnp.where(hidden, 0.0, pre_odd * jax.nn.sigmoid(pre_odd))
        stacked_b[t] = jnp.concatenate(
            [
                shifted(act_odd, 1, half).astype(BF16),
                act_even.astype(BF16),
                act_odd.astype(BF16),
            ],
            axis=-1,
        ).reshape(inner // 2, 2, half, 3 * chans)
    wide = own_g.shape[-1]
    grads = [cot_ref[t, 1 : rows + 1].reshape(rows * half, wide) for t in range(frames)]
    grad = jnp.concatenate(grads, axis=0)
    part = chans // 2
    for kh in range(3):
        lo, parity = divmod(kh, 2)
        piece = [
            stacked_b[t, lo : lo + rows, parity].reshape(rows * half, 3 * chans)
            for t in (0, core)
        ]
        total = mm_tn(jnp.concatenate(piece, axis=0), grad)
        for kw in range(3):
            upper = total[kw * chans : kw * chans + part].astype(BF16)
            lower = total[kw * chans + part : (kw + 1) * chans].astype(BF16)
            keep_b[kh * 3 + kw] = jnp.where(side == 0, upper, lower)
            send_b[kh * 3 + kw] = jnp.where(side == 0, lower, upper)


def backward_kernel(last, cot_ref, pre_ref, stacked_a, weight_b, keep_a, send_a, pre_grad):
    core, side, plane = position()
    frames, ext_g, half, wide = cot_ref.shape
    chans = weight_b.shape[3]
    inner = pre_ref.shape[1]
    width = 2 * half
    mid = inner // 2
    cot = cot_ref[...].reshape(frames * ext_g, half, wide)
    ahead = shifted(cot.astype(F32), -1, half).astype(BF16)
    both = jnp.concatenate([cot, ahead], axis=-1).reshape(frames, ext_g, half, 2 * wide)
    later = both[:, 1:].reshape(frames * mid * half, 2 * wide)
    sooner = both[:, :-1].reshape(frames * mid * half, 2 * wide)
    zero = jnp.zeros((chans, wide), BF16)

    def taps(kt, kh):
        return jnp.concatenate(
            [
                jnp.concatenate([weight_b[kt, kh, 1], zero], axis=1),
                jnp.concatenate([weight_b[kt, kh, 2], weight_b[kt, kh, 0]], axis=1),
            ],
            axis=0,
        )

    def rows_of(kt):
        even = mm_nt(later, taps(kt, 1))
        odd = mm_nt(later, taps(kt, 0)) + mm_nt(sooner, taps(kt, 2))
        shape = (frames, mid, half, 2 * chans)
        return (even.reshape(shape), odd.reshape(shape))

    copies = [rows_of(kt) for kt in range(3)]
    outside_low = (plane == 0) & (side == 0)
    outside_high = (plane == last // 2) & (side == last % 2)
    row = lax.broadcasted_iota(jnp.int32, (inner, half, chans), 0)
    hidden = (outside_low & (row == 0)) | (outside_high & (row == inner - 1))
    for t in range(frames):
        sums = []
        for parity in range(2):
            total = copies[2][parity][t]
            if t == 0:
                total = total + (copies[0][parity][0] + copies[1][parity][0])
                total = total + (copies[0][parity][1] + copies[1][parity][1])
            sums.append(total)
        grad = jnp.stack([sums[1], sums[0]], axis=1).reshape(inner, half, 2 * chans)
        for parity in range(2):
            act_grad = grad[:, :, parity * chans : (parity + 1) * chans]
            pre = pre_ref[t, :, parity * half : (parity + 1) * half]
            sig = jax.nn.sigmoid(pre)
            value = act_grad * sig * (1.0 + pre * (1.0 - sig))
            value = jnp.where(hidden, 0.0, value).astype(BF16)
            pre_grad[t, :, parity * half : (parity + 1) * half] = value
    rows = inner - 2
    grads = [pre_grad[t, 1 : rows + 1].reshape(rows * width, chans) for t in range(frames)]
    grad = jnp.concatenate(grads, axis=0)
    part = chans // 2
    for kh in range(3):
        piece = [
            stacked_a[t, kh + 1 : kh + 1 + rows].reshape(rows * width, 3 * chans)
            for t in (0, core)
        ]
        total = mm_tn(jnp.concatenate(piece, axis=0), grad)
        for kw in range(3):
            upper = total[kw * chans : kw * chans + part].astype(BF16)
            lower = total[kw * chans + part : (kw + 1) * chans].astype(BF16)
            keep_a[kh * 3 + kw] = jnp.where(side == 0, upper, lower)
            send_a[kh * 3 + kw] = jnp.where(side == 0, lower, upper)


def output_kernel(stacked_b, pre_grad, weight_a, weight_b, encoded, frames_grad, flat):
    core, _, _ = position()
    frames, _, _, half, _ = stacked_b.shape
    rows, width, chans = frames_grad.shape[1:]
    short = rows // 2
    wide = encoded.shape[-1]
    count = short * half
    shared = jnp.zeros((count, wide), F32)
    latest = jnp.zeros((frames * count, wide), F32)
    for kh in range(3):
        lo, parity = divmod(kh, 2)
        piece = [
            stacked_b[t, pl.ds(short * core + lo, short), parity].reshape(count, 3 * chans)
            for t in range(frames)
        ]
        shared += mm(piece[0], weight_b[0, kh]) + mm(piece[0], weight_b[1, kh])
        latest += mm(jnp.concatenate(piece, axis=0), weight_b[2, kh])
    for t in range(frames):
        value = shared + latest[t * count : (t + 1) * count]
        encoded[t] = value.astype(BF16).reshape(short, half, wide)

    ext = rows + 2
    own = pre_grad[:, pl.ds(rows * core, ext)].astype(F32)
    even = own[:, :, 0:half].reshape(frames * ext, half, chans)
    odd = own[:, :, half:width].reshape(frames * ext, half, chans)
    before = shifted(odd, 1, half).astype(BF16)
    after = shifted(even, -1, half).astype(BF16)
    even_16, odd_16 = (even.astype(BF16), odd.astype(BF16))
    stacked = jnp.stack(
        [
            jnp.concatenate([odd_16, even_16, before], axis=-1),
            jnp.concatenate([after, odd_16, even_16], axis=-1),
        ],
        axis=1,
    ).reshape(frames, ext, width, 3 * chans)
    early = jnp.zeros((frames * rows * width, chans), F32)
    late = jnp.zeros((frames * rows * width, chans), F32)
    for kh in range(3):
        piece = stacked[:, 2 - kh : 2 - kh + rows].reshape(frames * rows * width, 3 * chans)
        for kt in range(3):
            taps = jnp.concatenate([weight_a[kt, kh, kw] for kw in range(3)], axis=1)
            if kt == 2:
                late += mm_nt(piece, taps)
            else:
                early += mm_nt(piece, taps)
    early = early.reshape(frames, rows, 2, half, chans)
    late = late.reshape(frames, rows, 2, half, chans)
    even = even.reshape(frames, ext, half, chans)[:, 1 : rows + 1]
    odd = odd.reshape(frames, ext, half, chans)[:, 1 : rows + 1]
    size = rows * half
    for t in range(frames):
        total = late[t]
        if t == 0:
            total = total + (early[0] + early[1])
        for parity, value in ((0, even), (1, odd)):
            summed = value[t] + total[:, parity]
            flat[pl.ds(t * 2 * size + parity, size, stride=2), :] = summed.reshape(size, chans)
    frames_grad[...] = flat[...].reshape(frames_grad.shape).astype(BF16)


def add_kernel(keep, recv, *outs):
    _, _, plane = position()
    planes = len(outs)
    rows = keep.shape[1] // planes
    for step in range(planes):
        at = pl.multiple_of(((plane + step) % planes) * rows, rows)
        value = keep[:, pl.ds(at, rows)].astype(F32) + recv[:, pl.ds(at, rows)].astype(F32)
        outs[step][...] = value.astype(BF16)


def finish_kernel(scale, parts_a, parts_b, out):
    chans = parts_a[0].shape[-1]

    def total(parts):
        value = parts[0][...].astype(F32)
        for part in parts[1:]:
            value = value + part[...].astype(F32)
        return (value * scale).astype(BF16)

    out[:, :, 0:chans] = total(parts_a)
    out[:, :, chans:] = total(parts_b)


def assemble_kernel(planes, *refs):
    pieces, (out_a, out_b) = (refs[:-2], refs[-2:])
    core, side, plane = position()
    chans = out_a.shape[-1]
    rows = pieces[0].shape[1]
    at = 0
    for flip_core in range(2):
        for flip_side in range(2):
            for step in range(planes):
                piece = pieces[at]
                at += 1
                tap = core ^ flip_core
                source = (plane - step + planes) % planes
                start = pl.multiple_of((side ^ flip_side) * (chans // 2) + source * rows, rows)
                for slot in (2 * tap, 1 + tap):
                    out_a[slot, :, pl.ds(start, rows)] = piece[:, :, 0:chans]
                    out_b[slot, :, pl.ds(start, rows)] = piece[:, :, chans:]


def call(body, outs, args, scratch=(), flops=0):
    size = sum(a.size * a.dtype.itemsize for a in args)
    size += sum(o.size * o.dtype.itemsize for o in outs)
    return pl.pallas_call(
        body,
        out_shape=outs,
        scratch_shapes=scratch,
        compiler_params=pltpu.CompilerParams(vmem_limit_bytes=VMEM_LIMIT),
        cost_estimate=pl.CostEstimate(flops=flops, bytes_accessed=size, transcendentals=0),
    )(*args)


def on_device(frames, weight_a, weight_b, cotangent):
    count, rows, width, chans = frames.shape
    assert count == 2
    wide = weight_b.shape[-1]
    half = width // 2
    n = lax.axis_size(AXIS)
    chips = n // 2
    planes = n // 4
    core, side, plane = position()
    shape = jax.ShapeDtypeStruct

    def send(value, pairs):
        return lax.ppermute(value, AXIS, pairs)

    swap_core = [(i, i ^ 1) for i in range(n)]
    swap_side = [(i, i ^ 2) for i in range(n)]
    near = [(2 * k + 1, 2 * k + 2) for k in range(chips - 1)]
    near += [(2 * k + 2, 2 * k + 1) for k in range(chips - 1)]
    far = [(2 * k + 1, 2 * k + 3) for k in range(chips - 1)]
    far += [(2 * k + 2, 2 * k) for k in range(chips - 1)]

    edge_f = lax.dynamic_slice_in_dim(frames, core * (rows - 2), 2, axis=1)
    edge_g = lax.dynamic_slice_in_dim(cotangent, core * (rows // 2 - 1), 1, axis=1)
    edge_g = jnp.concatenate([edge_g[..., :chans], edge_g[..., chans:]], axis=1)
    edge = jnp.concatenate([edge_f, edge_g.reshape(count, 1, width, chans)], axis=1)
    halos = [send(edge, near), send(edge, far)]
    halo_f = [halo[:, 0:2] for halo in halos]
    halo_g = [
        jnp.concatenate([halo[:, 2:3, 0:half], halo[:, 2:3, half:]], axis=-1) for halo in halos
    ]
    other_f = send(frames, swap_core)
    other_g = send(cotangent, swap_core)

    inner = 2 * rows + 2
    kernel_a = weight_a.reshape(3, 3, 3 * chans, chans)
    kernel_b = weight_b.reshape(3, 3, 3 * chans, wide)
    part = chans // 2
    keep_b, send_b, pre, stacked_a, stacked_b, cot = call(
        forward_kernel,
        (
            shape((9, part, wide), BF16),
            shape((9, part, wide), BF16),
            shape((count, inner, width, chans), F32),
            shape((count, inner + 2, width, 3 * chans), BF16),
            shape((count, inner // 2, 2, half, 3 * chans), BF16),
            shape((count, rows + 2, half, wide), BF16),
        ),
        (frames, other_f, *halo_f, cotangent, other_g, *halo_g, kernel_a),
        [pltpu.VMEM((count * (inner + 2) * width, chans), F32)],
        flops=10**9,
    )
    recv_b = send(send_b, swap_side)

    def backward(*refs):
        backward_kernel(chips - 1, *refs)

    keep_a, send_a, pre_grad = call(
        backward,
        (
            shape((9, part, chans), BF16),
            shape((9, part, chans), BF16),
            shape((count, inner, width, chans), BF16),
        ),
        (cot, pre, stacked_a, weight_b),
        flops=10**9,
    )
    recv_a = send(send_a, swap_side)
    encoded, frames_grad = call(
        output_kernel,
        (shape(cotangent.shape, BF16), shape(frames.shape, BF16)),
        (stacked_b, pre_grad, weight_a, kernel_b),
        [pltpu.VMEM((count * rows * width, chans), F32)],
        flops=10**9,
    )

    scale = (count * rows * n * width) ** (-0.5)
    if part % (8 * planes):
        taps = jnp.arange(2)[:, None, None, None, None] == core
        sides = jnp.arange(2)[None, None, :, None, None] == side
        both = []
        for keep, recv in ((keep_a, recv_a), (keep_b, recv_b)):
            value = keep.astype(F32) + recv.astype(F32)
            slots = jnp.where(taps & sides, value[None, :, None], 0.0)
            total = lax.psum(slots, AXIS) * scale
            total = total.astype(BF16).reshape(2, 3, 3, chans, -1)
            both.append(jnp.concatenate([total[:1], total], axis=0))
        return (encoded, frames_grad, both[0], both[1])

    parts = []
    for keep, recv in ((keep_b, recv_b), (keep_a, recv_a)):
        piece = shape((9, part // planes, keep.shape[-1]), BF16)
        pieces = call(add_kernel, (piece,) * planes, (keep, recv))
        got = [pieces[0]]
        for step in range(1, planes):
            to = [(i, (i + 4 * step) % n) for i in range(n)]
            got.append(send(pieces[step], to))
        parts.append(got)

    def finish(*refs):
        finish_kernel(scale, refs[:planes], refs[planes : 2 * planes], refs[-1])

    (own,) = call(
        finish,
        (shape((9, part // planes, chans + wide), BF16),),
        (*parts[1], *parts[0]),
    )
    pieces = [own]
    for step in range(1, planes):
        pieces.append(send(own, [(i, (i + 4 * step) % n) for i in range(n)]))
    pieces += [send(piece, swap_side) for piece in pieces]
    pieces += [send(piece, swap_core) for piece in pieces]

    def assemble(*refs):
        assemble_kernel(planes, *refs)

    grad_a, grad_b = call(
        assemble,
        (shape((3, 9, chans, chans), BF16), shape((3, 9, chans, wide), BF16)),
        pieces,
    )
    return (encoded, frames_grad, grad_a.reshape(weight_a.shape), grad_b.reshape(weight_b.shape))


def solution(mesh):
    in_specs = (P("groups", "height", None, None), P(), P(), P("groups", "height", None, None))
    out_specs = (
        P("groups", "height", None, None),
        P("groups", "height", None, None),
        P("groups", None, None, None, None),
        P("groups", None, None, None, None),
    )
    return jax.shard_map(
        on_device, mesh=mesh, in_specs=in_specs, out_specs=out_specs, check_vma=False
    )
```

```python
import jax
import jax.numpy as jnp
from jax import lax
from jax.experimental import pallas as pl
from jax.experimental.pallas import tpu as pltpu
from jax.sharding import PartitionSpec as P

F32 = jnp.float32
BF16 = jnp.bfloat16
AXIS = "height"
VMEM_LIMIT = 48 * 1024 * 1024


def position():
    index = lax.axis_index(AXIS)
    return (index % 2, (index // 2) % 2, index // 4)


def mm(a, b):
    return lax.dot_general(a, b, (((1,), (0,)), ((), ())), preferred_element_type=F32)


def mm_nt(a, b):
    return lax.dot_general(a, b, (((1,), (1,)), ((), ())), preferred_element_type=F32)


def mm_tn(a, b):
    return lax.dot_general(a, b, (((0,), (0,)), ((), ())), preferred_element_type=F32)


def shifted(field, by, half):
    rows, _, chans = field.shape
    flat = field.reshape(rows * half, chans)
    column = lax.broadcasted_iota(jnp.int32, flat.shape, 0) % half
    moved = pltpu.roll(flat, by % (rows * half), axis=0)
    edge = 0 if by > 0 else half - 1
    return jnp.where(column == edge, 0.0, moved).reshape(field.shape)


def wide_pair(even, odd, half):
    before = shifted(odd, 1, half).astype(BF16)
    after = shifted(even, -1, half).astype(BF16)
    even, odd = (even.astype(BF16), odd.astype(BF16))
    return (
        jnp.concatenate([before, even, odd], axis=-1),
        jnp.concatenate([even, odd, after], axis=-1),
    )


def edge_kernel(frames, cot, edge, sems):
    core, _, _ = position()
    rows, width = frames.shape[1:3]
    short, half = cot.shape[1:3]
    chans = frames.shape[-1]
    first = pl.ds(core * (rows - 2), 2)
    only = pl.ds(core * (short - 1), 1)
    copies = [pltpu.make_async_copy(frames.at[:, first], edge.at[:, 0:2], sems.at[0])]
    for k in range(2):
        source = cot.at[:, only, :, k * chans : (k + 1) * chans]
        target = edge.at[:, 2:3, k * half : (k + 1) * half]
        copies.append(pltpu.make_async_copy(source, target, sems.at[1 + k]))
    for copy in copies:
        copy.start()
    for copy in copies:
        copy.wait()


def stage_kernel(*refs):
    sems = refs[-1]
    count = (len(refs) - 1) // 2
    copies = [
        pltpu.make_async_copy(refs[k], refs[count + k], sems.at[k]) for k in range(count)
    ]
    for copy in copies:
        copy.start()
    for copy in copies:
        copy.wait()


def forward_kernel(
    own_f, other_f, own_g, other_g, near, far, weight_a,
    keep_b, send_b, pre_ref, stacked_a, stacked_b, cot_ref, flat,
):
    core, side, plane = position()
    frames, rows, width, chans = own_f.shape
    half = width // 2
    ext = 2 * rows + 4
    block = rows * width
    for t in range(frames):
        base = t * ext * width
        top = jnp.where(core == 0, near[t].astype(F32), far[t].astype(F32))
        low = jnp.where(core == 0, far[t].astype(F32), near[t].astype(F32))
        top_g = jnp.concatenate([top[2, 0:half], top[2, half:]], axis=-1).astype(BF16)
        low_g = jnp.concatenate([low[2, 0:half], low[2, half:]], axis=-1).astype(BF16)
        flat[base : base + 2 * width] = top[0:2].reshape(2 * width, chans)
        flat[base + (ext - 2) * width : base + ext * width] = low[0:2].reshape(2 * width, chans)
        at = pl.multiple_of(base + 2 * width + core * block, 2 * width)
        flat[pl.ds(at, block)] = own_f[t].astype(F32).reshape(block, chans)
        at = pl.multiple_of(base + 2 * width + (1 - core) * block, 2 * width)
        flat[pl.ds(at, block)] = other_f[t].astype(F32).reshape(block, chans)
        cot_ref[t, 0] = top_g
        cot_ref[t, rows + 1] = low_g
        cot_ref[t, pl.ds(1 + core * (rows // 2), rows // 2)] = own_g[t]
        cot_ref[t, pl.ds(1 + (1 - core) * (rows // 2), rows // 2)] = other_g[t]
    count = frames * ext
    even = flat[pl.ds(0, count * half, stride=2), :].reshape(count, half, chans)
    odd = flat[pl.ds(1, count * half, stride=2), :].reshape(count, half, chans)
    taps_even, taps_odd = wide_pair(even, odd, half)
    stacked_a[:, :, 0:half] = taps_even.reshape(frames, ext, half, 3 * chans)
    stacked_a[:, :, half:width] = taps_odd.reshape(frames, ext, half, 3 * chans)

    inner = ext - 2
    shared = jnp.zeros((inner * width, chans), F32)
    latest = [jnp.zeros((inner * width, chans), F32) for _ in range(2)]
    for kh in range(3):
        first = stacked_a[0, kh : kh + inner].reshape(inner * width, 3 * chans)
        second = stacked_a[1, kh : kh + inner].reshape(inner * width, 3 * chans)
        shared += mm(first, weight_a[0, kh]) + mm(first, weight_a[1, kh])
        latest[0] += mm(first, weight_a[2, kh])
        latest[1] += mm(second, weight_a[2, kh])
    even = even.reshape(frames, ext, half, chans)
    odd = odd.reshape(frames, ext, half, chans)
    outside = (plane == 0) & (side == 0)
    row = lax.broadcasted_iota(jnp.int32, (inner, half, chans), 0)
    hidden = outside & (row == 0)
    for t in range(frames):
        conv = (shared + latest[t]).reshape(inner, 2, half, chans)
        pre_even = even[t, 1 : ext - 1] + conv[:, 0]
        pre_odd = odd[t, 1 : ext - 1] + conv[:, 1]
        pre_ref[t, :, 0:half] = pre_even
        pre_ref[t, :, half:width] = pre_odd
        act_even = jnp.where(hidden, 0.0, pre_even * jax.nn.sigmoid(pre_even))
        act_odd = jnp.where(hidden, 0.0, pre_odd * jax.nn.sigmoid(pre_odd))
        stacked_b[t] = jnp.concatenate(
            [
                shifted(act_odd, 1, half).astype(BF16),
                act_even.astype(BF16),
                act_odd.astype(BF16),
            ],
            axis=-1,
        ).reshape(inner // 2, 2, half, 3 * chans)
    wide = own_g.shape[-1]
    grads = [cot_ref[t, 1 : rows + 1].reshape(rows * half, wide) for t in range(frames)]
    grad = jnp.concatenate(grads, axis=0)
    part = chans // 2
    for kh in range(3):
        lo, parity = divmod(kh, 2)
        piece = [
            stacked_b[t, lo : lo + rows, parity].reshape(rows * half, 3 * chans)
            for t in (0, core)
        ]
        total = mm_tn(jnp.concatenate(piece, axis=0), grad)
        for kw in range(3):
            upper = total[kw * chans : kw * chans + part].astype(BF16)
            lower = total[kw * chans + part : (kw + 1) * chans].astype(BF16)
            keep_b[kh * 3 + kw] = jnp.where(side == 0, upper, lower)
            send_b[kh * 3 + kw] = jnp.where(side == 0, lower, upper)


def backward_kernel(last, cot_ref, pre_ref, stacked_a, weight_b, keep_a, send_a, pre_grad):
    core, side, plane = position()
    frames, ext_g, half, wide = cot_ref.shape
    chans = weight_b.shape[3]
    inner = pre_ref.shape[1]
    width = 2 * half
    mid = inner // 2
    cot = cot_ref[...].reshape(frames * ext_g, half, wide)
    ahead = shifted(cot.astype(F32), -1, half).astype(BF16)
    both = jnp.concatenate([cot, ahead], axis=-1).reshape(frames, ext_g, half, 2 * wide)
    later = both[:, 1:].reshape(frames * mid * half, 2 * wide)
    sooner = both[:, :-1].reshape(frames * mid * half, 2 * wide)
    zero = jnp.zeros((chans, wide), BF16)

    def taps(kt, kh):
        return jnp.concatenate(
            [
                jnp.concatenate([weight_b[kt, kh, 1], zero], axis=1),
                jnp.concatenate([weight_b[kt, kh, 2], weight_b[kt, kh, 0]], axis=1),
            ],
            axis=0,
        )

    def rows_of(kt):
        even = mm_nt(later, taps(kt, 1))
        odd = mm_nt(later, taps(kt, 0)) + mm_nt(sooner, taps(kt, 2))
        shape = (frames, mid, half, 2 * chans)
        return (even.reshape(shape), odd.reshape(shape))

    copies = [rows_of(kt) for kt in range(3)]
    outside_low = (plane == 0) & (side == 0)
    outside_high = (plane == last // 2) & (side == last % 2)
    row = lax.broadcasted_iota(jnp.int32, (inner, half, chans), 0)
    hidden = (outside_low & (row == 0)) | (outside_high & (row == inner - 1))
    for t in range(frames):
        sums = []
        for parity in range(2):
            total = copies[2][parity][t]
            if t == 0:
                total = total + (copies[0][parity][0] + copies[1][parity][0])
                total = total + (copies[0][parity][1] + copies[1][parity][1])
            sums.append(total)
        grad = jnp.stack([sums[1], sums[0]], axis=1).reshape(inner, half, 2 * chans)
        for parity in range(2):
            act_grad = grad[:, :, parity * chans : (parity + 1) * chans]
            pre = pre_ref[t, :, parity * half : (parity + 1) * half]
            sig = jax.nn.sigmoid(pre)
            value = act_grad * sig * (1.0 + pre * (1.0 - sig))
            value = jnp.where(hidden, 0.0, value).astype(BF16)
            pre_grad[t, :, parity * half : (parity + 1) * half] = value
    rows = inner - 2
    grads = [pre_grad[t, 1 : rows + 1].reshape(rows * width, chans) for t in range(frames)]
    grad = jnp.concatenate(grads, axis=0)
    part = chans // 2
    for kh in range(3):
        piece = [
            stacked_a[t, kh + 1 : kh + 1 + rows].reshape(rows * width, 3 * chans)
            for t in (0, core)
        ]
        total = mm_tn(jnp.concatenate(piece, axis=0), grad)
        for kw in range(3):
            upper = total[kw * chans : kw * chans + part].astype(BF16)
            lower = total[kw * chans + part : (kw + 1) * chans].astype(BF16)
            keep_a[kh * 3 + kw] = jnp.where(side == 0, upper, lower)
            send_a[kh * 3 + kw] = jnp.where(side == 0, lower, upper)


def output_kernel(stacked_b, pre_grad, weight_a, weight_b, encoded, frames_grad, flat):
    core, _, _ = position()
    frames, _, _, half, _ = stacked_b.shape
    rows, width, chans = frames_grad.shape[1:]
    short = rows // 2
    wide = encoded.shape[-1]
    count = short * half
    shared = jnp.zeros((count, wide), F32)
    latest = jnp.zeros((frames * count, wide), F32)
    for kh in range(3):
        lo, parity = divmod(kh, 2)
        piece = [
            stacked_b[t, pl.ds(short * core + lo, short), parity].reshape(count, 3 * chans)
            for t in range(frames)
        ]
        shared += mm(piece[0], weight_b[0, kh]) + mm(piece[0], weight_b[1, kh])
        latest += mm(jnp.concatenate(piece, axis=0), weight_b[2, kh])
    for t in range(frames):
        value = shared + latest[t * count : (t + 1) * count]
        encoded[t] = value.astype(BF16).reshape(short, half, wide)

    ext = rows + 2
    own = pre_grad[:, pl.ds(rows * core, ext)].astype(F32)
    even = own[:, :, 0:half].reshape(frames * ext, half, chans)
    odd = own[:, :, half:width].reshape(frames * ext, half, chans)
    before = shifted(odd, 1, half).astype(BF16)
    after = shifted(even, -1, half).astype(BF16)
    even_16, odd_16 = (even.astype(BF16), odd.astype(BF16))
    stacked = jnp.stack(
        [
            jnp.concatenate([odd_16, even_16, before], axis=-1),
            jnp.concatenate([after, odd_16, even_16], axis=-1),
        ],
        axis=1,
    ).reshape(frames, ext, width, 3 * chans)
    early = jnp.zeros((frames * rows * width, chans), F32)
    late = jnp.zeros((frames * rows * width, chans), F32)
    for kh in range(3):
        piece = stacked[:, 2 - kh : 2 - kh + rows].reshape(frames * rows * width, 3 * chans)
        for kt in range(3):
            taps = jnp.concatenate([weight_a[kt, kh, kw] for kw in range(3)], axis=1)
            if kt == 2:
                late += mm_nt(piece, taps)
            else:
                early += mm_nt(piece, taps)
    early = early.reshape(frames, rows, 2, half, chans)
    late = late.reshape(frames, rows, 2, half, chans)
    even = even.reshape(frames, ext, half, chans)[:, 1 : rows + 1]
    odd = odd.reshape(frames, ext, half, chans)[:, 1 : rows + 1]
    size = rows * half
    for t in range(frames):
        total = late[t]
        if t == 0:
            total = total + (early[0] + early[1])
        for parity, value in ((0, even), (1, odd)):
            summed = value[t] + total[:, parity]
            flat[pl.ds(t * 2 * size + parity, size, stride=2), :] = summed.reshape(size, chans)
    frames_grad[...] = flat[...].reshape(frames_grad.shape).astype(BF16)


def add_kernel(keep_a, recv_a, keep_b, recv_b, *outs):
    _, _, plane = position()
    planes = len(outs)
    rows = keep_a.shape[1] // planes
    chans = keep_a.shape[-1]
    for step in range(planes):
        at = pl.multiple_of(((plane + step) % planes) * rows, rows)
        part = pl.ds(at, rows)
        value = keep_a[:, part].astype(F32) + recv_a[:, part].astype(F32)
        outs[step][:, :, 0:chans] = value.astype(BF16)
        value = keep_b[:, part].astype(F32) + recv_b[:, part].astype(F32)
        outs[step][:, :, chans:] = value.astype(BF16)


def finish_kernel(scale, *refs):
    value = refs[0][...].astype(F32)
    for part in refs[1:-1]:
        value = value + part[...].astype(F32)
    refs[-1][...] = (value * scale).astype(BF16)


def assemble_kernel(places, planes, *refs):
    count = len(places)
    pieces, (out_a, out_b), sems = (refs[:count], refs[count : count + 2], refs[-1])
    core, side, plane = position()
    chans = out_a.shape[-1]
    rows = pieces[0].shape[1]

    def copies(piece, place, sem):
        flip_core, flip_side, step = place
        tap = core ^ flip_core
        source = (plane - step + planes) % planes
        at = pl.multiple_of((side ^ flip_side) * (chans // 2) + source * rows, rows)
        for k, slot in enumerate((tap * 2, 1)):
            for part, out in ((slice(0, chans), out_a), (slice(chans, None), out_b)):
                lanes = piece.shape[-1] - chans if part.stop is None else chans
                source_ref = piece.at[:, :, pl.ds(part.start, lanes)]
                target_ref = out.at[slot, :, pl.ds(at, rows), :]
                spot = sem.at[2 * k + (0 if part.stop else 1)]
                yield k, tap, pltpu.make_async_copy(source_ref, target_ref, spot)

    def each(act):
        for index, (piece, place) in enumerate(zip(pieces, places, strict=True)):
            for k, tap, copy in copies(piece, place, sems.at[index]):
                if k == 0:
                    act(copy)
                else:
                    pl.when(tap == 0)(lambda copy=copy: act(copy))

    each(lambda copy: copy.start())
    each(lambda copy: copy.wait())


def call(body, outs, args, scratch=(), flops=0, whole=False):
    size = sum(a.size * a.dtype.itemsize for a in args)
    size += sum(o.size * o.dtype.itemsize for o in outs)
    extra = {}
    if whole:
        extra["in_specs"] = [pl.BlockSpec(memory_space=pl.ANY)] * len(args)
    if whole == "both":
        extra["out_specs"] = (pl.BlockSpec(memory_space=pl.ANY),) * len(outs)
    return pl.pallas_call(
        body,
        out_shape=outs,
        scratch_shapes=scratch,
        compiler_params=pltpu.CompilerParams(vmem_limit_bytes=VMEM_LIMIT),
        cost_estimate=pl.CostEstimate(flops=flops, bytes_accessed=size, transcendentals=0),
        **extra,
    )(*args)


def on_device(frames, weight_a, weight_b, cotangent):
    count, rows, width, chans = frames.shape
    assert count == 2
    wide = weight_b.shape[-1]
    half = width // 2
    n = lax.axis_size(AXIS)
    chips = n // 2
    planes = n // 4
    core, side, plane = position()
    shape = jax.ShapeDtypeStruct

    def send(value, pairs):
        return lax.ppermute(value, AXIS, pairs)

    swap_core = [(i, i ^ 1) for i in range(n)]
    swap_side = [(i, i ^ 2) for i in range(n)]
    near = [(2 * k + 1, 2 * k + 2) for k in range(chips - 1)]
    near += [(2 * k + 2, 2 * k + 1) for k in range(chips - 1)]

    (edge,) = call(
        edge_kernel,
        (shape((count, 3, width, chans), BF16),),
        (frames, cotangent),
        [pltpu.SemaphoreType.DMA((3,))],
        whole=True,
    )
    near_edge = send(edge, near)
    other_f = send(frames, swap_core)
    other_g = send(cotangent, swap_core)
    far_edge = send(near_edge, swap_core)
    inputs = (frames, cotangent, weight_a, weight_b)
    own_f, own_g, weight_a, weight_b = call(
        stage_kernel,
        tuple(shape(x.shape, x.dtype) for x in inputs),
        inputs,
        [pltpu.SemaphoreType.DMA((4,))],
        whole=True,
    )

    inner = 2 * rows + 2
    kernel_a = weight_a.reshape(3, 3, 3 * chans, chans)
    kernel_b = weight_b.reshape(3, 3, 3 * chans, wide)
    part = chans // 2
    keep_b, send_b, pre, stacked_a, stacked_b, cot = call(
        forward_kernel,
        (
            shape((9, part, wide), BF16),
            shape((9, part, wide), BF16),
            shape((count, inner, width, chans), F32),
            shape((count, inner + 2, width, 3 * chans), BF16),
            shape((count, inner // 2, 2, half, 3 * chans), BF16),
            shape((count, rows + 2, half, wide), BF16),
        ),
        (own_f, other_f, own_g, other_g, near_edge, far_edge, kernel_a),
        [pltpu.VMEM((count * (inner + 2) * width, chans), F32)],
        flops=10**9,
    )
    recv_b = send(send_b, swap_side)

    def backward(*refs):
        backward_kernel(chips - 1, *refs)

    keep_a, send_a, pre_grad = call(
        backward,
        (
            shape((9, part, chans), BF16),
            shape((9, part, chans), BF16),
            shape((count, inner, width, chans), BF16),
        ),
        (cot, pre, stacked_a, weight_b),
        flops=10**9,
    )
    recv_a = send(send_a, swap_side)
    encoded, frames_grad = call(
        output_kernel,
        (shape(cotangent.shape, BF16), shape(frames.shape, BF16)),
        (stacked_b, pre_grad, weight_a, kernel_b),
        [pltpu.VMEM((count * rows * width, chans), F32)],
        flops=10**9,
    )

    scale = (count * rows * n * width) ** (-0.5)
    if part % (8 * planes):
        taps = jnp.arange(2)[:, None, None, None, None] == core
        sides = jnp.arange(2)[None, None, :, None, None] == side
        both = []
        for keep, recv in ((keep_a, recv_a), (keep_b, recv_b)):
            value = keep.astype(F32) + recv.astype(F32)
            slots = jnp.where(taps & sides, value[None, :, None], 0.0)
            total = lax.psum(slots, AXIS) * scale
            total = total.astype(BF16).reshape(2, 3, 3, chans, -1)
            both.append(jnp.concatenate([total[:1], total], axis=0))
        return (encoded, frames_grad, both[0], both[1])

    held = (keep_a, keep_b, encoded, frames_grad)
    keep_a, keep_b, encoded, frames_grad = lax.optimization_barrier(held)
    piece = shape((9, part // planes, chans + wide), BF16)
    pieces = call(add_kernel, (piece,) * planes, (keep_a, recv_a, keep_b, recv_b))
    got = [pieces[0]]
    for step in range(1, planes):
        got.append(send(pieces[step], [(i, (i + 4 * step) % n) for i in range(n)]))

    def finish(*refs):
        finish_kernel(scale, *refs)

    (own,) = call(finish, (piece,), got)
    column = {(0, 0, 0): own}
    for step in range(1, planes):
        to = [(i, (i + 4 * step) % n) for i in range(n)]
        column[0, 0, step] = send(own, to)
        if 2 * step == planes and planes > 2:
            column[0, 1, step] = send(own, [(i, j ^ 2) for i, j in to])
    for step in range(planes):
        if (0, 1, step) not in column:
            column[0, 1, step] = send(column[0, 0, step], swap_side)
    for (_, flip, step), value in list(column.items()):
        column[1, flip, step] = send(value, swap_core)
    places = tuple(column)

    def assemble(*refs):
        assemble_kernel(places, planes, *refs)

    grad_a, grad_b = call(
        assemble,
        (shape((3, 9, chans, chans), BF16), shape((3, 9, chans, wide), BF16)),
        tuple(column.values()),
        [pltpu.SemaphoreType.DMA((len(places), 4))],
        whole="both",
    )
    return (encoded, frames_grad, grad_a.reshape(weight_a.shape), grad_b.reshape(weight_b.shape))


def solution(mesh):
    in_specs = (P("groups", "height", None, None), P(), P(), P("groups", "height", None, None))
    out_specs = (
        P("groups", "height", None, None),
        P("groups", "height", None, None),
        P("groups", None, None, None, None),
        P("groups", None, None, None, None),
    )
    return jax.shard_map(
        on_device, mesh=mesh, in_specs=in_specs, out_specs=out_specs, check_vma=False
    )
```

```python
import jax
import jax.numpy as jnp
from jax import lax
from jax.experimental import pallas as pl
from jax.experimental.pallas import tpu as pltpu
from jax.sharding import PartitionSpec as P

F32 = jnp.float32
BF16 = jnp.bfloat16
AXIS = "height"
VMEM_LIMIT = 24 * 1024 * 1024


def position():
    index = lax.axis_index(AXIS)
    return (index % 2, (index // 2) % 2, index // 4)


def emit(total, outs):
    _, side, plane = position()
    part = total.shape[1] // 2
    count = len(outs)
    rows = part // count
    for step, out in enumerate(outs):
        owner = (plane + step) % count if count > 1 else 0
        at = pl.multiple_of(side * part + owner * rows, rows)
        out[...] = total[:, pl.ds(at, rows)].astype(out.dtype)


def mm(a, b):
    return lax.dot_general(a, b, (((1,), (0,)), ((), ())), preferred_element_type=F32)


def mm_nt(a, b):
    return lax.dot_general(a, b, (((1,), (1,)), ((), ())), preferred_element_type=F32)


def mm_tn(a, b):
    return lax.dot_general(a, b, (((0,), (0,)), ((), ())), preferred_element_type=F32)


def shifted(field, by, half):
    rows, _, chans = field.shape
    flat = field.reshape(rows * half, chans)
    column = lax.broadcasted_iota(jnp.int32, flat.shape, 0) % half
    moved = pltpu.roll(flat, by % (rows * half), axis=0)
    edge = 0 if by > 0 else half - 1
    return jnp.where(column == edge, 0.0, moved).reshape(field.shape)


def wide_pair(even, odd, half):
    before = shifted(odd, 1, half).astype(BF16)
    after = shifted(even, -1, half).astype(BF16)
    even, odd = (even.astype(BF16), odd.astype(BF16))
    return (
        jnp.concatenate([before, even, odd], axis=-1),
        jnp.concatenate([even, odd, after], axis=-1),
    )


def edge_kernel(frames, cot, pack, edge, sems):
    core, _, _ = position()
    rows, width = frames.shape[1:3]
    short, half = cot.shape[1:3]
    chans = frames.shape[-1]
    first = pl.ds(core * (rows - 2), 2)
    only = pl.ds(core * (short - 1), 1)
    moves = [(frames.at[:, first], edge.at[:, 0:2]), (frames, pack.at[:, 0:rows])]
    for k in range(2):
        lanes = slice(k * chans, (k + 1) * chans)
        columns = slice(k * half, (k + 1) * half)
        moves.append((cot.at[:, only, :, lanes], edge.at[:, 2:3, columns]))
        moves.append((cot.at[:, :, :, lanes], pack.at[:, rows:, columns]))
    copies = [pltpu.make_async_copy(*move, sems.at[k]) for k, move in enumerate(moves)]
    for copy in copies:
        copy.start()
    for copy in copies:
        copy.wait()


def stage_kernel(*refs):
    sems = refs[-1]
    count = (len(refs) - 1) // 2
    copies = [
        pltpu.make_async_copy(refs[k], refs[count + k], sems.at[k]) for k in range(count)
    ]
    for copy in copies:
        copy.start()
    for copy in copies:
        copy.wait()


def forward_kernel(split, *refs):
    packs, edges, weight_a = (refs[0:4], refs[4:8], refs[8])
    outs, flat, total_b = (refs[9:-2], refs[-2], refs[-1])
    pieces, (pre_ref, stacked_a, stacked_b, cot_ref) = (outs[:split], outs[split:])
    core, side, plane = position()
    place = 2 * side + core
    frames, packed, width, chans = packs[0].shape
    rows = packed // 3 * 2
    short = rows // 2
    half = width // 2
    ext = 4 * rows + 4
    block = rows * width

    def edge(t, index):
        chosen = edges[3][t].astype(F32)
        for k in range(3):
            chosen = jnp.where(index == k, edges[k][t].astype(F32), chosen)
        cot = jnp.concatenate([chosen[2, 0:half], chosen[2, half:]], axis=-1)
        return (chosen[0:2].reshape(2 * width, chans), cot.astype(BF16))

    for t in range(frames):
        base = t * ext * width
        flat[base : base + 2 * width], cot_ref[t, 0] = edge(t, place)
        low = base + (ext - 2) * width
        flat[low : low + 2 * width], cot_ref[t, 4 * short + 1] = edge(t, 3 - place)
        for k in range(4):
            at = pl.multiple_of(base + 2 * width + (place ^ k) * block, 2 * width)
            flat[pl.ds(at, block)] = packs[k][t, 0:rows].astype(F32).reshape(block, chans)
            cot = (packs[k][t, rows:, 0:half], packs[k][t, rows:, half:])
            spot = pl.ds(1 + (place ^ k) * short, short)
            cot_ref[t, spot] = jnp.concatenate(cot, axis=-1)
    count = frames * ext
    even = flat[pl.ds(0, count * half, stride=2), :].reshape(count, half, chans)
    odd = flat[pl.ds(1, count * half, stride=2), :].reshape(count, half, chans)
    taps_even, taps_odd = wide_pair(even, odd, half)
    stacked_a[:, :, 0:half] = taps_even.reshape(frames, ext, half, 3 * chans)
    stacked_a[:, :, half:width] = taps_odd.reshape(frames, ext, half, 3 * chans)

    inner = ext - 2
    shared = jnp.zeros((inner * width, chans), F32)
    latest = [jnp.zeros((inner * width, chans), F32) for _ in range(2)]
    for kh in range(3):
        first = stacked_a[0, kh : kh + inner].reshape(inner * width, 3 * chans)
        second = stacked_a[1, kh : kh + inner].reshape(inner * width, 3 * chans)
        shared += mm(first, weight_a[0, kh]) + mm(first, weight_a[1, kh])
        latest[0] += mm(first, weight_a[2, kh])
        latest[1] += mm(second, weight_a[2, kh])
    even = even.reshape(frames, ext, half, chans)
    odd = odd.reshape(frames, ext, half, chans)
    outside = plane == 0
    row = lax.broadcasted_iota(jnp.int32, (inner, half, chans), 0)
    hidden = outside & (row == 0)
    for t in range(frames):
        conv = (shared + latest[t]).reshape(inner, 2, half, chans)
        pre_even = even[t, 1 : ext - 1] + conv[:, 0]
        pre_odd = odd[t, 1 : ext - 1] + conv[:, 1]
        pre_ref[t, :, 0:half] = pre_even
        pre_ref[t, :, half:width] = pre_odd
        act_even = jnp.where(hidden, 0.0, pre_even * jax.nn.sigmoid(pre_even))
        act_odd = jnp.where(hidden, 0.0, pre_odd * jax.nn.sigmoid(pre_odd))
        stacked_b[t] = jnp.concatenate(
            [
                shifted(act_odd, 1, half).astype(BF16),
                act_even.astype(BF16),
                act_odd.astype(BF16),
            ],
            axis=-1,
        ).reshape(inner // 2, 2, half, 3 * chans)
    wide = cot_ref.shape[-1]
    tall = 4 * short
    grads = [cot_ref[t, 1 : tall + 1].reshape(tall * half, wide) for t in range(frames)]
    grad = jnp.concatenate(grads, axis=0)
    for kh in range(3):
        lo, parity = divmod(kh, 2)
        piece = [
            stacked_b[t, lo : lo + tall, parity].reshape(tall * half, 3 * chans)
            for t in (0, core)
        ]
        total = mm_tn(jnp.concatenate(piece, axis=0), grad)
        total_b[3 * kh : 3 * kh + 3] = total.reshape(3, chans, wide)
    emit(total_b, pieces)


def backward_kernel(last, cot_ref, pre_ref, stacked_a, weight_b, *refs):
    pieces, (pre_grad, total_a) = (refs[:-2], refs[-2:])
    core, side, plane = position()
    frames, ext_g, half, wide = cot_ref.shape
    chans = weight_b.shape[3]
    inner = pre_ref.shape[1]
    width = 2 * half
    mid = inner // 2
    cot = cot_ref[...].reshape(frames * ext_g, half, wide)
    ahead = shifted(cot.astype(F32), -1, half).astype(BF16)
    both = jnp.concatenate([cot, ahead], axis=-1).reshape(frames, ext_g, half, 2 * wide)
    later = both[:, 1:].reshape(frames * mid * half, 2 * wide)
    sooner = both[:, :-1].reshape(frames * mid * half, 2 * wide)
    zero = jnp.zeros((chans, wide), BF16)

    def taps(kt, kh):
        return jnp.concatenate(
            [
                jnp.concatenate([weight_b[kt, kh, 1], zero], axis=1),
                jnp.concatenate([weight_b[kt, kh, 2], weight_b[kt, kh, 0]], axis=1),
            ],
            axis=0,
        )

    def rows_of(kt):
        even = mm_nt(later, taps(kt, 1))
        odd = mm_nt(later, taps(kt, 0)) + mm_nt(sooner, taps(kt, 2))
        shape = (frames, mid, half, 2 * chans)
        return (even.reshape(shape), odd.reshape(shape))

    copies = [rows_of(kt) for kt in range(3)]
    row = lax.broadcasted_iota(jnp.int32, (inner, half, chans), 0)
    hidden = ((plane == 0) & (row == 0)) | ((plane == last) & (row == inner - 1))
    for t in range(frames):
        sums = []
        for parity in range(2):
            total = copies[2][parity][t]
            if t == 0:
                total = total + (copies[0][parity][0] + copies[1][parity][0])
                total = total + (copies[0][parity][1] + copies[1][parity][1])
            sums.append(total)
        grad = jnp.stack([sums[1], sums[0]], axis=1).reshape(inner, half, 2 * chans)
        for parity in range(2):
            act_grad = grad[:, :, parity * chans : (parity + 1) * chans]
            pre = pre_ref[t, :, parity * half : (parity + 1) * half]
            sig = jax.nn.sigmoid(pre)
            value = act_grad * sig * (1.0 + pre * (1.0 - sig))
            value = jnp.where(hidden, 0.0, value).astype(BF16)
            pre_grad[t, :, parity * half : (parity + 1) * half] = value
    rows = inner - 2
    grads = [pre_grad[t, 1 : rows + 1].reshape(rows * width, chans) for t in range(frames)]
    grad = jnp.concatenate(grads, axis=0)
    for kh in range(3):
        piece = [
            stacked_a[t, kh + 1 : kh + 1 + rows].reshape(rows * width, 3 * chans)
            for t in (0, core)
        ]
        total = mm_tn(jnp.concatenate(piece, axis=0), grad)
        total_a[3 * kh : 3 * kh + 3] = total.reshape(3, chans, chans)
    emit(total_a, pieces)


def output_kernel(stacked_b, pre_grad, weight_a, weight_b, encoded, frames_grad, flat):
    core, side, _ = position()
    place = 2 * side + core
    frames, _, _, half, _ = stacked_b.shape
    rows, width, chans = frames_grad.shape[1:]
    short = rows // 2
    wide = encoded.shape[-1]
    count = short * half
    shared = jnp.zeros((count, wide), F32)
    latest = jnp.zeros((frames * count, wide), F32)
    for kh in range(3):
        lo, parity = divmod(kh, 2)
        piece = [
            stacked_b[t, pl.ds(short * place + lo, short), parity].reshape(count, 3 * chans)
            for t in range(frames)
        ]
        shared += mm(piece[0], weight_b[0, kh]) + mm(piece[0], weight_b[1, kh])
        latest += mm(jnp.concatenate(piece, axis=0), weight_b[2, kh])
    for t in range(frames):
        value = shared + latest[t * count : (t + 1) * count]
        encoded[t] = value.astype(BF16).reshape(short, half, wide)

    ext = rows + 2
    own = pre_grad[:, pl.ds(rows * place, ext)].astype(F32)
    even = own[:, :, 0:half].reshape(frames * ext, half, chans)
    odd = own[:, :, half:width].reshape(frames * ext, half, chans)
    before = shifted(odd, 1, half).astype(BF16)
    after = shifted(even, -1, half).astype(BF16)
    even_16, odd_16 = (even.astype(BF16), odd.astype(BF16))
    stacked = jnp.stack(
        [
            jnp.concatenate([odd_16, even_16, before], axis=-1),
            jnp.concatenate([after, odd_16, even_16], axis=-1),
        ],
        axis=1,
    ).reshape(frames, ext, width, 3 * chans)
    early = jnp.zeros((frames * rows * width, chans), F32)
    late = jnp.zeros((frames * rows * width, chans), F32)
    for kh in range(3):
        piece = stacked[:, 2 - kh : 2 - kh + rows].reshape(frames * rows * width, 3 * chans)
        for kt in range(3):
            taps = jnp.concatenate([weight_a[kt, kh, kw] for kw in range(3)], axis=1)
            if kt == 2:
                late += mm_nt(piece, taps)
            else:
                early += mm_nt(piece, taps)
    early = early.reshape(frames, rows, 2, half, chans)
    late = late.reshape(frames, rows, 2, half, chans)
    even = even.reshape(frames, ext, half, chans)[:, 1 : rows + 1]
    odd = odd.reshape(frames, ext, half, chans)[:, 1 : rows + 1]
    size = rows * half
    for t in range(frames):
        total = late[t]
        if t == 0:
            total = total + (early[0] + early[1])
        for parity, value in ((0, even), (1, odd)):
            summed = value[t] + total[:, parity]
            flat[pl.ds(t * 2 * size + parity, size, stride=2), :] = summed.reshape(size, chans)
    frames_grad[...] = flat[...].reshape(frames_grad.shape).astype(BF16)


def finish_kernel(scale, *refs):
    half = len(refs) // 2
    chans = refs[0].shape[-1]

    def total(parts):
        value = parts[0][...].astype(F32)
        for part in parts[1:]:
            value = value + part[...].astype(F32)
        return (value * scale).astype(BF16)

    refs[-1][:, :, 0:chans] = total(refs[:half])
    refs[-1][:, :, chans:] = total(refs[half:-1])


def assemble_kernel(places, planes, *refs):
    pieces, (out_a, out_b) = (refs[:-2], refs[-2:])
    core, side, plane = position()
    chans = out_a.shape[-1]
    rows = pieces[0].shape[1]
    for piece, (flip_core, flip_side, step) in zip(pieces, places, strict=True):
        tap = core ^ flip_core
        source = (plane - step + planes) % planes
        at = pl.multiple_of((side ^ flip_side) * (chans // 2) + source * rows, rows)
        for slot in (2 * tap, 1 + tap):
            out_a[slot, :, pl.ds(at, rows)] = piece[:, :, 0:chans]
            out_b[slot, :, pl.ds(at, rows)] = piece[:, :, chans:]


def call(body, outs, args, scratch=(), flops=0, whole=False, limit=VMEM_LIMIT):
    extra = {}
    if whole:
        extra["in_specs"] = [pl.BlockSpec(memory_space=pl.ANY)] * len(args)
    return pl.pallas_call(
        body,
        out_shape=outs,
        scratch_shapes=scratch,
        compiler_params=pltpu.CompilerParams(vmem_limit_bytes=limit),
        cost_estimate=pl.CostEstimate(flops=flops, bytes_accessed=10**4, transcendentals=0),
        **extra,
    )(*args)


def on_device(frames, weight_a, weight_b, cotangent):
    count, rows, width, chans = frames.shape
    assert count == 2
    wide = weight_b.shape[-1]
    half = width // 2
    n = lax.axis_size(AXIS)
    planes = n // 4
    core, side, plane = position()
    shape = jax.ShapeDtypeStruct

    def send(value, pairs):
        return lax.ppermute(value, AXIS, pairs)

    swap_core = [(i, i ^ 1) for i in range(n)]
    swap_side = [(i, i ^ 2) for i in range(n)]
    near = [(4 * k + 3, 4 * k + 4) for k in range(planes - 1)]
    near += [(4 * k + 4, 4 * k + 3) for k in range(planes - 1)]

    pack, edge = call(
        edge_kernel,
        (
            shape((count, rows + rows // 2, width, chans), BF16),
            shape((count, 3, width, chans), BF16),
        ),
        (frames, cotangent),
        [pltpu.SemaphoreType.DMA((6,))],
        whole=True,
        limit=None,
    )
    packs = [pack, send(pack, swap_core), send(pack, swap_side), None]
    edges = [send(edge, near), None, None, None]
    edges[2] = send(edges[0], swap_side)
    edges[1] = send(edges[0], swap_core)
    packs[2], edges[2] = lax.optimization_barrier((packs[2], edges[2]))
    packs[3] = send(packs[2], swap_core)
    edges[3] = send(edges[2], swap_core)
    inputs = (pack, weight_a, weight_b)
    packs[0], staged_a, staged_b = call(
        stage_kernel,
        tuple(shape(x.shape, x.dtype) for x in inputs),
        inputs,
        [pltpu.SemaphoreType.DMA((3,))],
        whole=True,
    )

    inner = 4 * rows + 2
    kernel_a = staged_a.reshape(3, 3, 3 * chans, chans)
    kernel_b = staged_b.reshape(3, 3, 3 * chans, wide)
    part = chans // 2
    split = planes if part % (8 * planes) == 0 else 1

    def pieces_of(outputs):
        own = (9, part // split, outputs)
        return (shape(own, F32),) + (shape(own, BF16),) * (split - 1)

    def forward(*refs):
        forward_kernel(split, *refs)

    def backward(*refs):
        backward_kernel(planes - 1, *refs)

    *pieces_b, pre, stacked_a, stacked_b, cot = call(
        forward,
        pieces_of(wide)
        + (
            shape((count, inner, width, chans), F32),
            shape((count, inner + 2, width, 3 * chans), BF16),
            shape((count, inner // 2, 2, half, 3 * chans), BF16),
            shape((count, 2 * rows + 2, half, wide), BF16),
        ),
        (*packs, *edges, kernel_a),
        [
            pltpu.VMEM((count * (inner + 2) * width, chans), F32),
            pltpu.VMEM((9, chans, wide), F32),
        ],
        flops=10**7,
    )
    *pieces_a, pre_grad = call(
        backward,
        pieces_of(chans) + (shape((count, inner, width, chans), BF16),),
        (cot, pre, stacked_a, staged_b),
        [pltpu.VMEM((9, chans, chans), F32)],
        flops=10**7,
    )
    encoded, frames_grad = call(
        output_kernel,
        (shape(cotangent.shape, BF16), shape(frames.shape, BF16)),
        (stacked_b, pre_grad, staged_a, kernel_b),
        [pltpu.VMEM((count * rows * width, chans), F32)],
        flops=10**7,
    )

    scale = (count * rows * n * width) ** (-0.5)
    if split != planes:
        taps = jnp.arange(2)[:, None, None, None, None] == core
        sides = jnp.arange(2)[None, None, :, None, None] == side
        both = []
        for value in (pieces_a[0], pieces_b[0]):
            slots = jnp.where(taps & sides, value[None, :, None], 0.0)
            total = lax.psum(slots, AXIS) * scale
            total = total.astype(BF16).reshape(2, 3, 3, chans, -1)
            both.append(jnp.concatenate([total[:1], total], axis=0))
        return (encoded, frames_grad, both[0], both[1])

    rotations = [[(i, (i + 4 * step) % n) for i in range(n)] for step in range(planes)]
    got_b = [send(pieces_b[step], rotations[step]) for step in range(1, planes)]
    gate = lax.optimization_barrier((*got_b[:1], *pieces_a[1:]))
    got_b[:1] = gate[:1]
    pieces_a[1:] = gate[1:]
    got_a = [send(pieces_a[step], rotations[step]) for step in range(1, planes)]
    held = (pieces_a[0], encoded, frames_grad)
    own_a, encoded, frames_grad = lax.optimization_barrier(held)

    def finish(*refs):
        finish_kernel(scale, *refs)

    piece = shape((9, part // planes, chans + wide), BF16)
    (own,) = call(finish, (piece,), (own_a, *got_a, pieces_b[0], *got_b))
    column = {(0, 0, 0): own}
    for step in range(1, planes):
        column[0, 0, step] = send(own, rotations[step])
    for step in range(planes):
        column[0, 1, step] = send(column[0, 0, step], swap_side)
    for (_, flip, step), value in list(column.items()):
        column[1, flip, step] = send(value, swap_core)
    places = tuple(column)

    def assemble(*refs):
        assemble_kernel(places, planes, *refs)

    grad_a, grad_b = call(
        assemble,
        (shape((3, 9, chans, chans), BF16), shape((3, 9, chans, wide), BF16)),
        tuple(column.values()),
    )
    return (encoded, frames_grad, grad_a.reshape(weight_a.shape), grad_b.reshape(weight_b.shape))


def solution(mesh):
    in_specs = (P("groups", "height", None, None), P(), P(), P("groups", "height", None, None))
    out_specs = (
        P("groups", "height", None, None),
        P("groups", "height", None, None),
        P("groups", None, None, None, None),
        P("groups", None, None, None, None),
    )
    return jax.shard_map(
        on_device, mesh=mesh, in_specs=in_specs, out_specs=out_specs, check_vma=False
    )
```

```python
import jax
import jax.numpy as jnp
from jax import lax
from jax.experimental import pallas as pl
from jax.experimental.pallas import tpu as pltpu
from jax.sharding import PartitionSpec as P

F32 = jnp.float32
BF16 = jnp.bfloat16
AXIS = "height"
VMEM_LIMIT = 24 * 1024 * 1024


def position():
    index = lax.axis_index(AXIS)
    return (index % 2, (index // 2) % 2, index // 4)


def emit(total, outs):
    _, side, plane = position()
    part = total.shape[1] // 2
    count = len(outs)
    rows = part // count
    for step, out in enumerate(outs):
        owner = (plane + step) % count if count > 1 else 0
        at = pl.multiple_of(side * part + owner * rows, rows)
        out[...] = total[:, pl.ds(at, rows)].astype(out.dtype)


def mm(a, b):
    return lax.dot_general(a, b, (((1,), (0,)), ((), ())), preferred_element_type=F32)


def mm_nt(a, b):
    return lax.dot_general(a, b, (((1,), (1,)), ((), ())), preferred_element_type=F32)


def mm_tn(a, b):
    return lax.dot_general(a, b, (((0,), (0,)), ((), ())), preferred_element_type=F32)


def shifted(field, by, half):
    rows, _, chans = field.shape
    flat = field.reshape(rows * half, chans)
    column = lax.broadcasted_iota(jnp.int32, flat.shape, 0) % half
    moved = pltpu.roll(flat, by % (rows * half), axis=0)
    edge = 0 if by > 0 else half - 1
    return jnp.where(column == edge, 0.0, moved).reshape(field.shape)


def wide_pair(even, odd, half):
    before = shifted(odd, 1, half).astype(BF16)
    after = shifted(even, -1, half).astype(BF16)
    even, odd = (even.astype(BF16), odd.astype(BF16))
    return (
        jnp.concatenate([before, even, odd], axis=-1),
        jnp.concatenate([even, odd, after], axis=-1),
    )


def edge_kernel(frames, cot, pack, edge, sems):
    core, _, _ = position()
    rows, width = frames.shape[1:3]
    short, half = cot.shape[1:3]
    chans = frames.shape[-1]
    first = pl.ds(core * (rows - 2), 2)
    only = pl.ds(core * (short - 1), 1)
    moves = [(frames.at[:, first], edge.at[:, 0:2]), (frames, pack.at[:, 0:rows])]
    for k in range(2):
        lanes = slice(k * chans, (k + 1) * chans)
        columns = slice(k * half, (k + 1) * half)
        moves.append((cot.at[:, only, :, lanes], edge.at[:, 2:3, columns]))
        moves.append((cot.at[:, :, :, lanes], pack.at[:, rows:, columns]))
    copies = [pltpu.make_async_copy(*move, sems.at[k]) for k, move in enumerate(moves)]
    for copy in copies:
        copy.start()
    for copy in copies:
        copy.wait()


def forward_kernel(split, *refs):
    own_f, own_g, packs, edges, weight_a = (*refs[0:2], refs[2:5], refs[5:7], refs[7])
    outs, flat, total_b = (refs[8:-2], refs[-2], refs[-1])
    pieces, (pre_ref, stacked_a, stacked_b, cot_ref) = (outs[:split], outs[split:])
    core, side, plane = position()
    place = 2 * side + core
    frames, rows, width, chans = own_f.shape
    short = rows // 2
    half = width // 2
    ext = 4 * rows + 4
    block = rows * width

    def edge(t, own):
        chosen = jnp.where(core == own, edges[0][t].astype(F32), edges[1][t].astype(F32))
        cot = jnp.concatenate([chosen[2, 0:half], chosen[2, half:]], axis=-1)
        return (chosen[0:2].reshape(2 * width, chans), cot.astype(BF16))

    for t in range(frames):
        base = t * ext * width
        flat[base : base + 2 * width], cot_ref[t, 0] = edge(t, 0)
        low = base + (ext - 2) * width
        flat[low : low + 2 * width], cot_ref[t, 4 * short + 1] = edge(t, 1)
        for k in range(4):
            at = pl.multiple_of(base + 2 * width + (place ^ k) * block, 2 * width)
            spot = pl.ds(1 + (place ^ k) * short, short)
            if k == 0:
                field, cot = (own_f[t], own_g[t])
            else:
                pack = packs[k - 1]
                cot = (pack[t, rows:, 0:half], pack[t, rows:, half:])
                field, cot = (pack[t, 0:rows], jnp.concatenate(cot, axis=-1))
            flat[pl.ds(at, block)] = field.astype(F32).reshape(block, chans)
            cot_ref[t, spot] = cot
    count = frames * ext
    even = flat[pl.ds(0, count * half, stride=2), :].reshape(count, half, chans)
    odd = flat[pl.ds(1, count * half, stride=2), :].reshape(count, half, chans)
    taps_even, taps_odd = wide_pair(even, odd, half)
    stacked_a[:, :, 0:half] = taps_even.reshape(frames, ext, half, 3 * chans)
    stacked_a[:, :, half:width] = taps_odd.reshape(frames, ext, half, 3 * chans)

    inner = ext - 2
    taps = [
        jnp.concatenate([weight_a[kt, kh] for kh in range(3)], axis=0) for kt in range(3)
    ]
    fields = [
        jnp.concatenate(
            [
                stacked_a[t, kh : kh + inner].reshape(inner * width, 3 * chans)
                for kh in range(3)
            ],
            axis=1,
        )
        for t in range(2)
    ]
    early = mm(fields[0], jnp.concatenate(taps[:2], axis=1))
    shared = early[:, :chans] + early[:, chans:]
    latest = [mm(field, taps[2]) for field in fields]
    even = even.reshape(frames, ext, half, chans)
    odd = odd.reshape(frames, ext, half, chans)
    outside = plane == 0
    row = lax.broadcasted_iota(jnp.int32, (inner, half, chans), 0)
    hidden = outside & (row == 0)
    for t in range(frames):
        conv = (shared + latest[t]).reshape(inner, 2, half, chans)
        pre_even = even[t, 1 : ext - 1] + conv[:, 0]
        pre_odd = odd[t, 1 : ext - 1] + conv[:, 1]
        pre_ref[t, :, 0:half] = pre_even
        pre_ref[t, :, half:width] = pre_odd
        act_even = jnp.where(hidden, 0.0, pre_even * jax.nn.sigmoid(pre_even))
        act_odd = jnp.where(hidden, 0.0, pre_odd * jax.nn.sigmoid(pre_odd))
        stacked_b[t] = jnp.concatenate(
            [
                shifted(act_odd, 1, half).astype(BF16),
                act_even.astype(BF16),
                act_odd.astype(BF16),
            ],
            axis=-1,
        ).reshape(inner // 2, 2, half, 3 * chans)
    wide = cot_ref.shape[-1]
    tall = 4 * short
    grads = [cot_ref[t, 1 : tall + 1].reshape(tall * half, wide) for t in range(frames)]
    grad = jnp.concatenate(grads, axis=0)
    for kh in range(3):
        lo, parity = divmod(kh, 2)
        piece = [
            stacked_b[t, lo : lo + tall, parity].reshape(tall * half, 3 * chans)
            for t in (0, core)
        ]
        total = mm_tn(jnp.concatenate(piece, axis=0), grad)
        total_b[3 * kh : 3 * kh + 3] = total.reshape(3, chans, wide)
    emit(total_b, pieces)


def backward_kernel(last, cot_ref, pre_ref, stacked_a, weight_b, *refs):
    pieces, (pre_grad, total_a) = (refs[:-2], refs[-2:])
    core, side, plane = position()
    frames, ext_g, half, wide = cot_ref.shape
    chans = weight_b.shape[3]
    inner = pre_ref.shape[1]
    width = 2 * half
    mid = inner // 2
    cot = cot_ref[...].reshape(frames * ext_g, half, wide)
    ahead = shifted(cot.astype(F32), -1, half).astype(BF16)
    both = jnp.concatenate([cot, ahead], axis=-1).reshape(frames, ext_g, half, 2 * wide)
    later = both[:, 1:].reshape(frames * mid * half, 2 * wide)
    sooner = both[:, :-1].reshape(frames * mid * half, 2 * wide)
    zero = jnp.zeros((chans, wide), BF16)

    def taps(kt, kh):
        return jnp.concatenate(
            [
                jnp.concatenate([weight_b[kt, kh, 1], zero], axis=1),
                jnp.concatenate([weight_b[kt, kh, 2], weight_b[kt, kh, 0]], axis=1),
            ],
            axis=0,
        )

    def rows_of(kt):
        even = mm_nt(later, taps(kt, 1))
        odd = mm_nt(later, taps(kt, 0)) + mm_nt(sooner, taps(kt, 2))
        shape = (frames, mid, half, 2 * chans)
        return (even.reshape(shape), odd.reshape(shape))

    copies = [rows_of(kt) for kt in range(3)]
    row = lax.broadcasted_iota(jnp.int32, (inner, half, chans), 0)
    hidden = ((plane == 0) & (row == 0)) | ((plane == last) & (row == inner - 1))
    for t in range(frames):
        sums = []
        for parity in range(2):
            total = copies[2][parity][t]
            if t == 0:
                total = total + (copies[0][parity][0] + copies[1][parity][0])
                total = total + (copies[0][parity][1] + copies[1][parity][1])
            sums.append(total)
        grad = jnp.stack([sums[1], sums[0]], axis=1).reshape(inner, half, 2 * chans)
        for parity in range(2):
            act_grad = grad[:, :, parity * chans : (parity + 1) * chans]
            pre = pre_ref[t, :, parity * half : (parity + 1) * half]
            sig = jax.nn.sigmoid(pre)
            value = act_grad * sig * (1.0 + pre * (1.0 - sig))
            value = jnp.where(hidden, 0.0, value).astype(BF16)
            pre_grad[t, :, parity * half : (parity + 1) * half] = value
    rows = inner - 2
    grads = [pre_grad[t, 1 : rows + 1].reshape(rows * width, chans) for t in range(frames)]
    grad = jnp.concatenate(grads, axis=0)
    field = jnp.concatenate(
        [
            jnp.concatenate(
                [
                    stacked_a[t, kh + 1 : kh + 1 + rows].reshape(rows * width, 3 * chans)
                    for t in (0, core)
                ],
                axis=0,
            )
            for kh in range(3)
        ],
        axis=1,
    )
    total = mm(grad.T, field)
    for k in range(9):
        total_a[k] = total[:, k * chans : (k + 1) * chans].T
    emit(total_a, pieces)


def output_kernel(stacked_b, pre_grad, weight_a, weight_b, encoded, frames_grad, flat):
    core, side, _ = position()
    place = 2 * side + core
    frames, _, _, half, _ = stacked_b.shape
    rows, width, chans = frames_grad.shape[1:]
    short = rows // 2
    wide = encoded.shape[-1]
    count = short * half
    shared = jnp.zeros((count, wide), F32)
    latest = jnp.zeros((frames * count, wide), F32)
    for kh in range(3):
        lo, parity = divmod(kh, 2)
        piece = [
            stacked_b[t, pl.ds(short * place + lo, short), parity].reshape(count, 3 * chans)
            for t in range(frames)
        ]
        shared += mm(piece[0], weight_b[0, kh]) + mm(piece[0], weight_b[1, kh])
        latest += mm(jnp.concatenate(piece, axis=0), weight_b[2, kh])
    for t in range(frames):
        value = shared + latest[t * count : (t + 1) * count]
        encoded[t] = value.astype(BF16).reshape(short, half, wide)

    ext = rows + 2
    own = pre_grad[:, pl.ds(rows * place, ext)].astype(F32)
    even = own[:, :, 0:half].reshape(frames * ext, half, chans)
    odd = own[:, :, half:width].reshape(frames * ext, half, chans)
    before = shifted(odd, 1, half).astype(BF16)
    after = shifted(even, -1, half).astype(BF16)
    even_16, odd_16 = (even.astype(BF16), odd.astype(BF16))
    stacked = jnp.stack(
        [
            jnp.concatenate([odd_16, even_16, before], axis=-1),
            jnp.concatenate([after, odd_16, even_16], axis=-1),
        ],
        axis=1,
    ).reshape(frames, ext, width, 3 * chans)
    early = jnp.zeros((frames * rows * width, chans), F32)
    late = jnp.zeros((frames * rows * width, chans), F32)
    for kh in range(3):
        piece = stacked[:, 2 - kh : 2 - kh + rows].reshape(frames * rows * width, 3 * chans)
        for kt in range(3):
            taps = jnp.concatenate([weight_a[kt, kh, kw] for kw in range(3)], axis=1)
            if kt == 2:
                late += mm_nt(piece, taps)
            else:
                early += mm_nt(piece, taps)
    early = early.reshape(frames, rows, 2, half, chans)
    late = late.reshape(frames, rows, 2, half, chans)
    even = even.reshape(frames, ext, half, chans)[:, 1 : rows + 1]
    odd = odd.reshape(frames, ext, half, chans)[:, 1 : rows + 1]
    size = rows * half
    for t in range(frames):
        total = late[t]
        if t == 0:
            total = total + (early[0] + early[1])
        for parity, value in ((0, even), (1, odd)):
            summed = value[t] + total[:, parity]
            flat[pl.ds(t * 2 * size + parity, size, stride=2), :] = summed.reshape(size, chans)
    frames_grad[...] = flat[...].reshape(frames_grad.shape).astype(BF16)


def finish_kernel(scale, *refs):
    half = len(refs) // 2
    chans = refs[0].shape[-1]

    def total(parts):
        value = parts[0][...].astype(F32)
        for part in parts[1:]:
            value = value + part[...].astype(F32)
        return (value * scale).astype(BF16)

    refs[-1][:, :, 0:chans] = total(refs[:half])
    refs[-1][:, :, chans:] = total(refs[half:-1])


def assemble_kernel(places, planes, *refs):
    pieces, (out_a, out_b) = (refs[:-2], refs[-2:])
    core, side, plane = position()
    chans = out_a.shape[-1]
    rows = pieces[0].shape[1]
    for piece, (flip_core, flip_side, step) in zip(pieces, places, strict=True):
        tap = core ^ flip_core
        source = (plane - step + planes) % planes
        at = pl.multiple_of((side ^ flip_side) * (chans // 2) + source * rows, rows)
        for slot in (2 * tap, 1 + tap):
            out_a[slot, :, pl.ds(at, rows)] = piece[:, :, 0:chans]
            out_b[slot, :, pl.ds(at, rows)] = piece[:, :, chans:]


def call(body, outs, args, scratch=(), flops=0, whole=False, limit=VMEM_LIMIT):
    extra = {}
    if whole:
        extra["in_specs"] = [pl.BlockSpec(memory_space=pl.ANY)] * len(args)
    return pl.pallas_call(
        body,
        out_shape=outs,
        scratch_shapes=scratch,
        compiler_params=pltpu.CompilerParams(vmem_limit_bytes=limit),
        cost_estimate=pl.CostEstimate(flops=flops, bytes_accessed=10**4, transcendentals=0),
        **extra,
    )(*args)


def on_device(frames, weight_a, weight_b, cotangent):
    count, rows, width, chans = frames.shape
    assert count == 2
    wide = weight_b.shape[-1]
    half = width // 2
    n = lax.axis_size(AXIS)
    planes = n // 4
    core, side, plane = position()
    shape = jax.ShapeDtypeStruct

    def send(value, pairs):
        return lax.ppermute(value, AXIS, pairs)

    swap_core = [(i, i ^ 1) for i in range(n)]
    swap_side = [(i, i ^ 2) for i in range(n)]
    along = []
    for k in range(0, n - 4, 4):
        along += [(k + 2, k + 6), (k + 3, k + 4), (k + 4, k + 3), (k + 5, k + 1)]

    pack, edge = call(
        edge_kernel,
        (
            shape((count, rows + rows // 2, width, chans), BF16),
            shape((count, 3, width, chans), BF16),
        ),
        (frames, cotangent),
        [pltpu.SemaphoreType.DMA((6,))],
        whole=True,
        limit=None,
        flops=4 * 10**9,
    )
    outer = jnp.where(core == side, edge, send(edge, swap_core))
    packs = [send(pack, swap_core), send(pack, swap_side), None]
    edges = [send(outer, along), None]
    edges[1] = send(edges[0], swap_core)
    packs[1], edges[0] = lax.optimization_barrier((packs[1], edges[0]))
    packs[2] = send(packs[1], swap_core)
    staged_a, staged_b = (weight_a, weight_b)

    inner = 4 * rows + 2
    kernel_a = staged_a.reshape(3, 3, 3 * chans, chans)
    kernel_b = staged_b.reshape(3, 3, 3 * chans, wide)
    part = chans // 2
    split = planes if part % (8 * planes) == 0 else 1

    def pieces_of(outputs):
        own = (9, part // split, outputs)
        return (shape(own, F32),) + (shape(own, BF16),) * (split - 1)

    def forward(*refs):
        forward_kernel(split, *refs)

    def backward(*refs):
        backward_kernel(planes - 1, *refs)

    *pieces_b, pre, stacked_a, stacked_b, cot = call(
        forward,
        pieces_of(wide)
        + (
            shape((count, inner, width, chans), F32),
            shape((count, inner + 2, width, 3 * chans), BF16),
            shape((count, inner // 2, 2, half, 3 * chans), BF16),
            shape((count, 2 * rows + 2, half, wide), BF16),
        ),
        (frames, cotangent, *packs, *edges, kernel_a),
        [
            pltpu.VMEM((count * (inner + 2) * width, chans), F32),
            pltpu.VMEM((9, chans, wide), F32),
        ],
        flops=10**7,
    )
    *pieces_a, pre_grad = call(
        backward,
        pieces_of(chans) + (shape((count, inner, width, chans), BF16),),
        (cot, pre, stacked_a, staged_b),
        [pltpu.VMEM((9, chans, chans), F32)],
        flops=10**7,
    )
    def outputs(stacked_b):
        return call(
            output_kernel,
            (shape(cotangent.shape, BF16), shape(frames.shape, BF16)),
            (stacked_b, pre_grad, staged_a, kernel_b),
            [pltpu.VMEM((count * rows * width, chans), F32)],
            flops=10**7,
        )

    scale = (count * rows * n * width) ** (-0.5)
    if split != planes:
        encoded, frames_grad = outputs(stacked_b)
        taps = jnp.arange(2)[:, None, None, None, None] == core
        sides = jnp.arange(2)[None, None, :, None, None] == side
        both = []
        for value in (pieces_a[0], pieces_b[0]):
            slots = jnp.where(taps & sides, value[None, :, None], 0.0)
            total = lax.psum(slots, AXIS) * scale
            total = total.astype(BF16).reshape(2, 3, 3, chans, -1)
            both.append(jnp.concatenate([total[:1], total], axis=0))
        return (encoded, frames_grad, both[0], both[1])

    rotations = [[(i, (i + 4 * step) % n) for i in range(n)] for step in range(planes)]
    got_b = [send(pieces_b[step], rotations[step]) for step in range(1, planes)]
    gate = lax.optimization_barrier((*got_b[:1], *pieces_a[1:]))
    got_b[:1] = gate[:1]
    pieces_a[1:] = gate[1:]
    got_a = [send(pieces_a[step], rotations[step]) for step in range(1, planes)]

    def finish(*refs):
        finish_kernel(scale, *refs)

    piece = shape((9, part // planes, chans + wide), BF16)
    (own,) = call(finish, (piece,), (pieces_a[0], *got_a, pieces_b[0], *got_b))
    own, stacked_b = lax.optimization_barrier((own, stacked_b))
    column = {(0, 0, 0): own}
    order = sorted(range(1, planes), key=lambda step: -min(step, planes - step))
    for step in order:
        column[0, 0, step] = send(own, rotations[step])
    first = (0, 0, order[-1] if order else 0)
    encoded, frames_grad = outputs(stacked_b)
    held = lax.optimization_barrier((column[first], encoded, frames_grad))
    column[first], encoded, frames_grad = held
    for step in (*order, 0):
        column[0, 1, step] = send(column[0, 0, step], swap_side)
    for (_, flip, step), value in list(column.items()):
        column[1, flip, step] = send(value, swap_core)
    places = tuple(column)

    def assemble(*refs):
        assemble_kernel(places, planes, *refs)

    grad_a, grad_b = call(
        assemble,
        (shape((3, 9, chans, chans), BF16), shape((3, 9, chans, wide), BF16)),
        tuple(column.values()),
    )
    return (encoded, frames_grad, grad_a.reshape(weight_a.shape), grad_b.reshape(weight_b.shape))


def solution(mesh):
    in_specs = (P("groups", "height", None, None), P(), P(), P("groups", "height", None, None))
    out_specs = (
        P("groups", "height", None, None),
        P("groups", "height", None, None),
        P("groups", None, None, None, None),
        P("groups", None, None, None, None),
    )
    return jax.shard_map(
        on_device, mesh=mesh, in_specs=in_specs, out_specs=out_specs, check_vma=False
    )
```

```python
import jax
import jax.numpy as jnp
from jax import lax
from jax.experimental import pallas as pl
from jax.experimental.pallas import tpu as pltpu
from jax.sharding import PartitionSpec as P

F32 = jnp.float32
BF16 = jnp.bfloat16
AXIS = "height"
VMEM_LIMIT = 24 * 1024 * 1024


def position():
    index = lax.axis_index(AXIS)
    return (index % 2, (index // 2) % 2, index // 4)


def emit(total, outs):
    _, side, plane = position()
    part = total.shape[1] // 2
    count = len(outs)
    rows = part // count
    for step, out in enumerate(outs):
        owner = (plane + step) % count if count > 1 else 0
        at = pl.multiple_of(side * part + owner * rows, rows)
        value = total[:, pl.ds(at, rows)].astype(out.dtype)
        out[:, :, 0 : value.shape[-1]] = value


def mm(a, b):
    return lax.dot_general(a, b, (((1,), (0,)), ((), ())), preferred_element_type=F32)


def mm_nt(a, b):
    return lax.dot_general(a, b, (((1,), (1,)), ((), ())), preferred_element_type=F32)


def mm_tn(a, b):
    return lax.dot_general(a, b, (((0,), (0,)), ((), ())), preferred_element_type=F32)


def shifted(field, by, half):
    rows, _, chans = field.shape
    flat = field.reshape(rows * half, chans)
    column = lax.broadcasted_iota(jnp.int32, flat.shape, 0) % half
    moved = pltpu.roll(flat, by % (rows * half), axis=0)
    edge = 0 if by > 0 else half - 1
    return jnp.where(column == edge, 0.0, moved).reshape(field.shape)


def wide_pair(even, odd, half):
    before = shifted(odd, 1, half).astype(BF16)
    after = shifted(even, -1, half).astype(BF16)
    even, odd = (even.astype(BF16), odd.astype(BF16))
    return (
        jnp.concatenate([before, even, odd], axis=-1),
        jnp.concatenate([even, odd, after], axis=-1),
    )


def edge_kernel(frames, cot, pack, edge, sems):
    core, _, _ = position()
    rows, width = frames.shape[1:3]
    short, half = cot.shape[1:3]
    chans = frames.shape[-1]
    first = pl.ds(core * (rows - 2), 2)
    only = pl.ds(core * (short - 1), 1)
    moves = [(frames.at[:, first], edge.at[:, 0:2]), (frames, pack.at[:, 0:rows])]
    for k in range(2):
        lanes = slice(k * chans, (k + 1) * chans)
        columns = slice(k * half, (k + 1) * half)
        moves.append((cot.at[:, only, :, lanes], edge.at[:, 2:3, columns]))
        moves.append((cot.at[:, :, :, lanes], pack.at[:, rows:, columns]))
    copies = [pltpu.make_async_copy(*move, sems.at[k]) for k, move in enumerate(moves)]
    for copy in copies:
        copy.start()
    for copy in copies:
        copy.wait()


def forward_kernel(split, *refs):
    own_f, own_g, packs, edges, weight_a = (*refs[0:2], refs[2:5], refs[5:7], refs[7])
    outs, flat, total_b = (refs[8:-2], refs[-2], refs[-1])
    pieces, (pre_ref, stacked_a, stacked_b, cot_ref) = (outs[:split], outs[split:])
    core, side, plane = position()
    place = 2 * side + core
    frames, rows, width, chans = own_f.shape
    short = rows // 2
    half = width // 2
    ext = 4 * rows + 4
    block = rows * width

    def edge(t, own):
        chosen = jnp.where(core == own, edges[0][t].astype(F32), edges[1][t].astype(F32))
        cot = jnp.concatenate([chosen[2, 0:half], chosen[2, half:]], axis=-1)
        return (chosen[0:2].reshape(2 * width, chans), cot.astype(BF16))

    for t in range(frames):
        base = t * ext * width
        flat[base : base + 2 * width], cot_ref[t, 0] = edge(t, 0)
        low = base + (ext - 2) * width
        flat[low : low + 2 * width], cot_ref[t, 4 * short + 1] = edge(t, 1)
        for k in range(4):
            at = pl.multiple_of(base + 2 * width + (place ^ k) * block, 2 * width)
            spot = pl.ds(1 + (place ^ k) * short, short)
            if k == 0:
                field, cot = (own_f[t], own_g[t])
            else:
                pack = packs[k - 1]
                cot = (pack[t, rows:, 0:half], pack[t, rows:, half:])
                field, cot = (pack[t, 0:rows], jnp.concatenate(cot, axis=-1))
            flat[pl.ds(at, block)] = field.astype(F32).reshape(block, chans)
            cot_ref[t, spot] = cot
    count = frames * ext
    even = flat[pl.ds(0, count * half, stride=2), :].reshape(count, half, chans)
    odd = flat[pl.ds(1, count * half, stride=2), :].reshape(count, half, chans)
    taps_even, taps_odd = wide_pair(even, odd, half)
    stacked_a[:, :, 0:half] = taps_even.reshape(frames, ext, half, 3 * chans)
    stacked_a[:, :, half:width] = taps_odd.reshape(frames, ext, half, 3 * chans)

    inner = ext - 2
    taps = [
        jnp.concatenate([weight_a[kt, kh] for kh in range(3)], axis=0) for kt in range(3)
    ]
    fields = [
        jnp.concatenate(
            [
                stacked_a[t, kh : kh + inner].reshape(inner * width, 3 * chans)
                for kh in range(3)
            ],
            axis=1,
        )
        for t in range(2)
    ]
    early = mm(fields[0], jnp.concatenate(taps[:2], axis=1))
    shared = early[:, :chans] + early[:, chans:]
    latest = [mm(field, taps[2]) for field in fields]
    even = even.reshape(frames, ext, half, chans)
    odd = odd.reshape(frames, ext, half, chans)
    outside = plane == 0
    row = lax.broadcasted_iota(jnp.int32, (inner, half, chans), 0)
    hidden = outside & (row == 0)
    for t in range(frames):
        conv = (shared + latest[t]).reshape(inner, 2, half, chans)
        pre_even = even[t, 1 : ext - 1] + conv[:, 0]
        pre_odd = odd[t, 1 : ext - 1] + conv[:, 1]
        pre_ref[t, :, 0:half] = pre_even
        pre_ref[t, :, half:width] = pre_odd
        act_even = jnp.where(hidden, 0.0, pre_even * jax.nn.sigmoid(pre_even))
        act_odd = jnp.where(hidden, 0.0, pre_odd * jax.nn.sigmoid(pre_odd))
        stacked_b[t] = jnp.concatenate(
            [
                shifted(act_odd, 1, half).astype(BF16),
                act_even.astype(BF16),
                act_odd.astype(BF16),
            ],
            axis=-1,
        ).reshape(inner // 2, 2, half, 3 * chans)
    wide = cot_ref.shape[-1]
    tall = 4 * short
    grads = [cot_ref[t, 1 : tall + 1].reshape(tall * half, wide) for t in range(frames)]
    grad = jnp.concatenate(grads, axis=0)
    for kh in range(3):
        lo, parity = divmod(kh, 2)
        piece = [
            stacked_b[t, lo : lo + tall, parity].reshape(tall * half, 3 * chans)
            for t in (0, core)
        ]
        total = mm_tn(jnp.concatenate(piece, axis=0), grad)
        total_b[3 * kh : 3 * kh + 3] = total.reshape(3, chans, wide)
    emit(total_b, pieces)


def backward_kernel(last, join, cot_ref, pre_ref, stacked_a, weight_b, *refs):
    if join:
        refs[1 + join][:, :, weight_b.shape[3] :] = refs[0][...]
        refs = refs[1:]
    pieces, (pre_grad, total_a) = (refs[:-2], refs[-2:])
    core, side, plane = position()
    frames, ext_g, half, wide = cot_ref.shape
    chans = weight_b.shape[3]
    inner = pre_ref.shape[1]
    width = 2 * half
    mid = inner // 2
    cot = cot_ref[...].reshape(frames * ext_g, half, wide)
    ahead = shifted(cot.astype(F32), -1, half).astype(BF16)
    both = jnp.concatenate([cot, ahead], axis=-1).reshape(frames, ext_g, half, 2 * wide)
    later = both[:, 1:].reshape(frames * mid * half, 2 * wide)
    sooner = both[:, :-1].reshape(frames * mid * half, 2 * wide)
    zero = jnp.zeros((chans, wide), BF16)

    def taps(kt, kh):
        return jnp.concatenate(
            [
                jnp.concatenate([weight_b[kt, kh, 1], zero], axis=1),
                jnp.concatenate([weight_b[kt, kh, 2], weight_b[kt, kh, 0]], axis=1),
            ],
            axis=0,
        )

    def rows_of(kt):
        even = mm_nt(later, taps(kt, 1))
        odd = mm_nt(later, taps(kt, 0)) + mm_nt(sooner, taps(kt, 2))
        shape = (frames, mid, half, 2 * chans)
        return (even.reshape(shape), odd.reshape(shape))

    copies = [rows_of(kt) for kt in range(3)]
    row = lax.broadcasted_iota(jnp.int32, (inner, half, chans), 0)
    hidden = ((plane == 0) & (row == 0)) | ((plane == last) & (row == inner - 1))
    for t in range(frames):
        sums = []
        for parity in range(2):
            total = copies[2][parity][t]
            if t == 0:
                total = total + (copies[0][parity][0] + copies[1][parity][0])
                total = total + (copies[0][parity][1] + copies[1][parity][1])
            sums.append(total)
        grad = jnp.stack([sums[1], sums[0]], axis=1).reshape(inner, half, 2 * chans)
        for parity in range(2):
            act_grad = grad[:, :, parity * chans : (parity + 1) * chans]
            pre = pre_ref[t, :, parity * half : (parity + 1) * half]
            sig = jax.nn.sigmoid(pre)
            value = act_grad * sig * (1.0 + pre * (1.0 - sig))
            value = jnp.where(hidden, 0.0, value).astype(BF16)
            pre_grad[t, :, parity * half : (parity + 1) * half] = value
    rows = inner - 2
    grads = [pre_grad[t, 1 : rows + 1].reshape(rows * width, chans) for t in range(frames)]
    grad = jnp.concatenate(grads, axis=0)
    field = jnp.concatenate(
        [
            jnp.concatenate(
                [
                    stacked_a[t, kh + 1 : kh + 1 + rows].reshape(rows * width, 3 * chans)
                    for t in (0, core)
                ],
                axis=0,
            )
            for kh in range(3)
        ],
        axis=1,
    )
    total = mm(grad.T, field)
    for k in range(9):
        total_a[k] = total[:, k * chans : (k + 1) * chans].T
    emit(total_a, pieces)


def output_kernel(stacked_b, pre_grad, weight_a, weight_b, encoded, frames_grad, flat):
    core, side, _ = position()
    place = 2 * side + core
    frames, _, _, half, _ = stacked_b.shape
    rows, width, chans = frames_grad.shape[1:]
    short = rows // 2
    wide = encoded.shape[-1]
    count = short * half
    shared = jnp.zeros((count, wide), F32)
    latest = jnp.zeros((frames * count, wide), F32)
    for kh in range(3):
        lo, parity = divmod(kh, 2)
        piece = [
            stacked_b[t, pl.ds(short * place + lo, short), parity].reshape(count, 3 * chans)
            for t in range(frames)
        ]
        shared += mm(piece[0], weight_b[0, kh]) + mm(piece[0], weight_b[1, kh])
        latest += mm(jnp.concatenate(piece, axis=0), weight_b[2, kh])
    for t in range(frames):
        value = shared + latest[t * count : (t + 1) * count]
        encoded[t] = value.astype(BF16).reshape(short, half, wide)

    ext = rows + 2
    own = pre_grad[:, pl.ds(rows * place, ext)].astype(F32)
    even = own[:, :, 0:half].reshape(frames * ext, half, chans)
    odd = own[:, :, half:width].reshape(frames * ext, half, chans)
    before = shifted(odd, 1, half).astype(BF16)
    after = shifted(even, -1, half).astype(BF16)
    even_16, odd_16 = (even.astype(BF16), odd.astype(BF16))
    stacked = jnp.stack(
        [
            jnp.concatenate([odd_16, even_16, before], axis=-1),
            jnp.concatenate([after, odd_16, even_16], axis=-1),
        ],
        axis=1,
    ).reshape(frames, ext, width, 3 * chans)
    early = jnp.zeros((frames * rows * width, chans), F32)
    late = jnp.zeros((frames * rows * width, chans), F32)
    for kh in range(3):
        piece = stacked[:, 2 - kh : 2 - kh + rows].reshape(frames * rows * width, 3 * chans)
        for kt in range(3):
            taps = jnp.concatenate([weight_a[kt, kh, kw] for kw in range(3)], axis=1)
            if kt == 2:
                late += mm_nt(piece, taps)
            else:
                early += mm_nt(piece, taps)
    early = early.reshape(frames, rows, 2, half, chans)
    late = late.reshape(frames, rows, 2, half, chans)
    even = even.reshape(frames, ext, half, chans)[:, 1 : rows + 1]
    odd = odd.reshape(frames, ext, half, chans)[:, 1 : rows + 1]
    size = rows * half
    for t in range(frames):
        total = late[t]
        if t == 0:
            total = total + (early[0] + early[1])
        for parity, value in ((0, even), (1, odd)):
            summed = value[t] + total[:, parity]
            flat[pl.ds(t * 2 * size + parity, size, stride=2), :] = summed.reshape(size, chans)
    frames_grad[...] = flat[...].reshape(frames_grad.shape).astype(BF16)


def finish_kernel(scale, count, *refs):
    chans = refs[0].shape[-1]
    shared, out = (refs[2 * count : -1], refs[-1])

    def total(parts, lanes):
        value = parts[0][...].astype(F32)
        for part in parts[1:]:
            value = value + part[...].astype(F32)
        for part in shared:
            value = value + part[:, :, lanes].astype(F32)
        return (value * scale).astype(BF16)

    out[:, :, 0:chans] = total(refs[:count], slice(0, chans))
    out[:, :, chans:] = total(refs[count : 2 * count], slice(chans, None))


def assemble_kernel(places, planes, *refs):
    pieces, (out_a, out_b) = (refs[:-2], refs[-2:])
    core, side, plane = position()
    chans = out_a.shape[-1]
    rows = pieces[0].shape[1]
    for piece, (flip_core, flip_side, step) in zip(pieces, places, strict=True):
        tap = core ^ flip_core
        source = (plane - step + planes) % planes
        at = pl.multiple_of((side ^ flip_side) * (chans // 2) + source * rows, rows)
        for slot in (2 * tap, 1 + tap):
            out_a[slot, :, pl.ds(at, rows)] = piece[:, :, 0:chans]
            out_b[slot, :, pl.ds(at, rows)] = piece[:, :, chans:]


def append_kernel(places, planes, old_a, old_b, *refs):
    del old_a, old_b
    count = len(places)
    pieces, (out_a, out_b, sems) = (refs[:count], refs[count:])
    core, side, plane = position()
    chans = out_a.shape[-1]
    rows = pieces[0].shape[1]

    def each(act):
        for index, (flip_core, flip_side, step) in enumerate(places):
            tap = core ^ flip_core
            source = (plane - step + planes) % planes
            at = pl.multiple_of((side ^ flip_side) * (chans // 2) + source * rows, rows)
            for k, out in enumerate((out_a, out_b)):
                lanes = slice(0, chans) if k == 0 else slice(chans, None)
                piece = pieces[index].at[:, :, lanes]
                move = pltpu.make_async_copy(
                    piece, out.at[tap * 2, :, pl.ds(at, rows)], sems.at[index, k]
                )
                twin = pltpu.make_async_copy(
                    piece, out.at[1, :, pl.ds(at, rows)], sems.at[index, 2 + k]
                )
                act(move)
                pl.when(tap == 0)(lambda twin=twin: act(twin))

    each(lambda copy: copy.start())
    each(lambda copy: copy.wait())


def call(
    body, outs, args, scratch=(), flops=0, whole=0, limit=VMEM_LIMIT, aliases=None, size=10**4
):
    extra = {}
    if whole:
        held = pl.BlockSpec(memory_space=pl.ANY)
        inside = pl.BlockSpec(memory_space=pltpu.VMEM)
        extra["in_specs"] = [held] * whole + [inside] * (len(args) - whole)
    if aliases:
        extra["out_specs"] = (held,) * len(outs)
        extra["input_output_aliases"] = aliases
    return pl.pallas_call(
        body,
        out_shape=outs,
        scratch_shapes=scratch,
        compiler_params=pltpu.CompilerParams(vmem_limit_bytes=limit),
        cost_estimate=pl.CostEstimate(flops=flops, bytes_accessed=size, transcendentals=0),
        **extra,
    )(*args)


def on_device(frames, weight_a, weight_b, cotangent):
    count, rows, width, chans = frames.shape
    assert count == 2
    wide = weight_b.shape[-1]
    half = width // 2
    n = lax.axis_size(AXIS)
    planes = n // 4
    core, side, plane = position()
    shape = jax.ShapeDtypeStruct

    def send(value, pairs):
        return lax.ppermute(value, AXIS, pairs)

    swap_core = [(i, i ^ 1) for i in range(n)]
    swap_side = [(i, i ^ 2) for i in range(n)]
    along = []
    for k in range(0, n - 4, 4):
        along += [(k + 2, k + 6), (k + 3, k + 4), (k + 4, k + 3), (k + 5, k + 1)]

    pack, edge = call(
        edge_kernel,
        (
            shape((count, rows + rows // 2, width, chans), BF16),
            shape((count, 3, width, chans), BF16),
        ),
        (frames, cotangent),
        [pltpu.SemaphoreType.DMA((6,))],
        whole=2,
        limit=None,
        flops=4 * 10**9,
    )
    outer = jnp.where(core == side, edge, send(edge, swap_core))
    packs = [send(pack, swap_core), send(pack, swap_side), None]
    edges = [send(outer, along), None]
    edges[1] = send(edges[0], swap_core)
    packs[1], edges[0] = lax.optimization_barrier((packs[1], edges[0]))
    packs[2] = send(packs[1], swap_core)
    staged_a, staged_b = (weight_a, weight_b)

    inner = 4 * rows + 2
    kernel_a = staged_a.reshape(3, 3, 3 * chans, chans)
    kernel_b = staged_b.reshape(3, 3, 3 * chans, wide)
    part = chans // 2
    split = planes if part % (8 * planes) == 0 else 1

    def pieces_of(outputs):
        own = (9, part // split, outputs)
        return (shape(own, F32),) + (shape(own, BF16),) * (split - 1)

    def forward(*refs):
        forward_kernel(split, *refs)

    join = split // 2 if split > 2 else 0

    def backward(*refs):
        backward_kernel(planes - 1, join, *refs)

    *pieces_b, pre, stacked_a, stacked_b, cot = call(
        forward,
        pieces_of(wide)
        + (
            shape((count, inner, width, chans), F32),
            shape((count, inner + 2, width, 3 * chans), BF16),
            shape((count, inner // 2, 2, half, 3 * chans), BF16),
            shape((count, 2 * rows + 2, half, wide), BF16),
        ),
        (frames, cotangent, *packs, *edges, kernel_a),
        [
            pltpu.VMEM((count * (inner + 2) * width, chans), F32),
            pltpu.VMEM((9, chans, wide), F32),
        ],
        flops=10**7,
    )
    shapes_a = list(pieces_of(chans))
    joined = ()
    if join:
        shapes_a[join] = shape((9, part // split, chans + wide), BF16)
        joined = (pieces_b[join],)
    *pieces_a, pre_grad = call(
        backward,
        (*shapes_a, shape((count, inner, width, chans), BF16)),
        (cot, pre, stacked_a, staged_b, *joined),
        [pltpu.VMEM((9, chans, chans), F32)],
        flops=10**7,
    )
    def outputs(stacked_b):
        return call(
            output_kernel,
            (shape(cotangent.shape, BF16), shape(frames.shape, BF16)),
            (stacked_b, pre_grad, staged_a, kernel_b),
            [pltpu.VMEM((count * rows * width, chans), F32)],
            flops=10**7,
        )

    scale = (count * rows * n * width) ** (-0.5)
    if split != planes:
        encoded, frames_grad = outputs(stacked_b)
        taps = jnp.arange(2)[:, None, None, None, None] == core
        sides = jnp.arange(2)[None, None, :, None, None] == side
        both = []
        for value in (pieces_a[0], pieces_b[0]):
            slots = jnp.where(taps & sides, value[None, :, None], 0.0)
            total = lax.psum(slots, AXIS) * scale
            total = total.astype(BF16).reshape(2, 3, 3, chans, -1)
            both.append(jnp.concatenate([total[:1], total], axis=0))
        return (encoded, frames_grad, both[0], both[1])

    rotations = [[(i, (i + 4 * step) % n) for i in range(n)] for step in range(planes)]
    close = [step for step in range(1, planes) if step != join]
    got_b = [send(pieces_b[step], rotations[step]) for step in close]
    if join:
        gate = lax.optimization_barrier((*got_b, pieces_a[close[-1]]))
        *got_b, pieces_a[close[-1]] = gate
    got_a = [send(pieces_a[step], rotations[step]) for step in close]
    both = [send(pieces_a[join], rotations[join])] if join else []

    def finish(*refs):
        finish_kernel(scale, 1 + len(close), *refs)

    encoded, frames_grad = outputs(stacked_b)
    held = lax.optimization_barrier((pieces_a[0], encoded, frames_grad))
    pieces_a[0], encoded, frames_grad = held
    piece = shape((9, part // planes, chans + wide), BF16)
    (own,) = call(finish, (piece,), (pieces_a[0], *got_a, pieces_b[0], *got_b, *both))
    column = {(0, 0, 0): own}
    order = sorted(range(1, planes), key=lambda step: min(step, planes - step))
    for step in order[:-1]:
        column[0, 0, step] = send(own, rotations[step])
    if planes == 1:
        column[0, 1, 0] = send(own, swap_side)
    else:
        far = (0, 0, order[-1])
        column[far] = send(own, rotations[order[-1]])
        for step in (0, *order[:-1]):
            column[0, 1, step] = send(column[0, 0, step], swap_side)
        if len(order) > 1:
            key = (0, 1, order[0])
            column[far], column[key] = lax.optimization_barrier((column[far], column[key]))
        column[0, 1, far[2]] = send(column[far], swap_side)
    last = (0, 1, order[-1] if order else 0)
    for (_, flip, step), value in list(column.items()):
        if (0, flip, step) != last:
            column[1, flip, step] = send(value, swap_core)
    slow = column.pop(last)
    tail = {key: column.pop(key) for key in list(column) if key[1] and key[2]}
    places = tuple(column)

    def assemble(*refs):
        assemble_kernel(places, planes, *refs)

    grads = call(
        assemble,
        (shape((3, 9, chans, chans), BF16), shape((3, 9, chans, wide), BF16)),
        tuple(column.values()),
    )
    slow, *grads = lax.optimization_barrier((slow, *grads))
    tail[last] = slow
    tail[1, *last[1:]] = send(slow, swap_core)
    ends = tuple(tail)

    def append(*refs):
        append_kernel(ends, planes, *refs)

    grad_a, grad_b = call(
        append,
        tuple(shape(x.shape, x.dtype) for x in grads),
        (*grads, *tail.values()),
        [pltpu.SemaphoreType.DMA((len(ends), 4))],
        whole=2,
        aliases={0: 0, 1: 1},
    )
    return (encoded, frames_grad, grad_a.reshape(weight_a.shape), grad_b.reshape(weight_b.shape))


def solution(mesh):
    in_specs = (P("groups", "height", None, None), P(), P(), P("groups", "height", None, None))
    out_specs = (
        P("groups", "height", None, None),
        P("groups", "height", None, None),
        P("groups", None, None, None, None),
        P("groups", None, None, None, None),
    )
    return jax.shard_map(
        on_device, mesh=mesh, in_specs=in_specs, out_specs=out_specs, check_vma=False
    )
```

```python
import jax
import jax.numpy as jnp
from jax import lax
from jax.experimental import pallas as pl
from jax.experimental.pallas import tpu as pltpu
from jax.sharding import PartitionSpec as P

F32 = jnp.float32
BF16 = jnp.bfloat16
AXIS = "height"
VMEM_LIMIT = 24 * 1024 * 1024


def position():
    index = lax.axis_index(AXIS)
    return (index % 2, (index // 2) % 2, index // 4)


def folded(weight, kt, *taps):
    if kt:
        return weight[(2, *taps)]
    return (weight[(0, *taps)].astype(F32) + weight[(1, *taps)].astype(F32)).astype(BF16)


def emit(total, outs):
    _, side, plane = position()
    part = total.shape[1] // 2
    count = len(outs)
    rows = part // count
    for step, out in enumerate(outs):
        owner = (plane + step) % count if count > 1 else 0
        at = pl.multiple_of(side * part + owner * rows, rows)
        value = total[:, pl.ds(at, rows)].astype(out.dtype)
        out[:, :, 0 : value.shape[-1]] = value


def mm(a, b):
    return lax.dot_general(a, b, (((1,), (0,)), ((), ())), preferred_element_type=F32)


def mm_nt(a, b):
    return lax.dot_general(a, b, (((1,), (1,)), ((), ())), preferred_element_type=F32)


def mm_tn(a, b):
    return lax.dot_general(a, b, (((0,), (0,)), ((), ())), preferred_element_type=F32)


def shifted(field, by, half):
    rows, _, chans = field.shape
    flat = field.reshape(rows * half, chans)
    column = lax.broadcasted_iota(jnp.int32, flat.shape, 0) % half
    moved = pltpu.roll(flat, by % (rows * half), axis=0)
    edge = 0 if by > 0 else half - 1
    return jnp.where(column == edge, 0.0, moved).reshape(field.shape)


def wide_pair(even, odd, half):
    before = shifted(odd, 1, half).astype(BF16)
    after = shifted(even, -1, half).astype(BF16)
    even, odd = (even.astype(BF16), odd.astype(BF16))
    return (
        jnp.concatenate([before, even, odd], axis=-1),
        jnp.concatenate([even, odd, after], axis=-1),
    )


def edge_kernel(frames, cot, pack, edge, sems):
    core, _, _ = position()
    rows, width = frames.shape[1:3]
    short, half = cot.shape[1:3]
    chans = frames.shape[-1]
    first = pl.ds(core * (rows - 2), 2)
    only = pl.ds(core * (short - 1), 1)
    moves = [(frames.at[:, first], edge.at[:, 0:2]), (frames, pack.at[:, 0:rows])]
    for k in range(2):
        lanes = slice(k * chans, (k + 1) * chans)
        columns = slice(k * half, (k + 1) * half)
        moves.append((cot.at[:, only, :, lanes], edge.at[:, 2:3, columns]))
        moves.append((cot.at[:, :, :, lanes], pack.at[:, rows:, columns]))
    copies = [pltpu.make_async_copy(*move, sems.at[k]) for k, move in enumerate(moves)]
    for copy in copies:
        copy.start()
    for copy in copies:
        copy.wait()


def forward_kernel(split, *refs):
    own_f, own_g, packs, edges, weight_a = (*refs[0:2], refs[2:5], refs[5:7], refs[7])
    outs, flat, total_b = (refs[8:-2], refs[-2], refs[-1])
    pieces, (pre_ref, stacked_a, stacked_b, cot_ref) = (outs[:split], outs[split:])
    core, side, plane = position()
    place = 2 * side + core
    frames, rows, width, chans = own_f.shape
    short = rows // 2
    half = width // 2
    ext = 4 * rows + 4
    block = rows * width

    def edge(t, own):
        chosen = jnp.where(core == own, edges[0][t].astype(F32), edges[1][t].astype(F32))
        cot = jnp.concatenate([chosen[2, 0:half], chosen[2, half:]], axis=-1)
        return (chosen[0:2].reshape(2 * width, chans), cot.astype(BF16))

    for t in range(frames):
        base = t * ext * width
        flat[base : base + 2 * width], cot_ref[t, 0] = edge(t, 0)
        low = base + (ext - 2) * width
        flat[low : low + 2 * width], cot_ref[t, 4 * short + 1] = edge(t, 1)
        for k in range(4):
            at = pl.multiple_of(base + 2 * width + (place ^ k) * block, 2 * width)
            spot = pl.ds(1 + (place ^ k) * short, short)
            if k == 0:
                field, cot = (own_f[t], own_g[t])
            else:
                pack = packs[k - 1]
                cot = (pack[t, rows:, 0:half], pack[t, rows:, half:])
                field, cot = (pack[t, 0:rows], jnp.concatenate(cot, axis=-1))
            flat[pl.ds(at, block)] = field.astype(F32).reshape(block, chans)
            cot_ref[t, spot] = cot
    count = frames * ext
    even = flat[pl.ds(0, count * half, stride=2), :].reshape(count, half, chans)
    odd = flat[pl.ds(1, count * half, stride=2), :].reshape(count, half, chans)
    taps_even, taps_odd = wide_pair(even, odd, half)
    stacked_a[:, :, 0:half] = taps_even.reshape(frames, ext, half, 3 * chans)
    stacked_a[:, :, half:width] = taps_odd.reshape(frames, ext, half, 3 * chans)

    inner = ext - 2
    taps = [
        jnp.concatenate([folded(weight_a, kt, kh) for kh in range(3)], axis=0) for kt in range(2)
    ]
    fields = [
        jnp.concatenate(
            [
                stacked_a[t, kh : kh + inner].reshape(inner * width, 3 * chans)
                for kh in range(3)
            ],
            axis=1,
        )
        for t in range(2)
    ]
    early = mm(fields[0], jnp.concatenate(taps, axis=1))
    shared = early[:, :chans]
    latest = [early[:, chans:], mm(fields[1], taps[1])]
    even = even.reshape(frames, ext, half, chans)
    odd = odd.reshape(frames, ext, half, chans)
    outside = plane == 0
    row = lax.broadcasted_iota(jnp.int32, (inner, half, chans), 0)
    hidden = outside & (row == 0)
    for t in range(frames):
        conv = (shared + latest[t]).reshape(inner, 2, half, chans)
        pre_even = even[t, 1 : ext - 1] + conv[:, 0]
        pre_odd = odd[t, 1 : ext - 1] + conv[:, 1]
        pre_ref[t, :, 0:half] = pre_even
        pre_ref[t, :, half:width] = pre_odd
        act_even = jnp.where(hidden, 0.0, pre_even * jax.nn.sigmoid(pre_even))
        act_odd = jnp.where(hidden, 0.0, pre_odd * jax.nn.sigmoid(pre_odd))
        stacked_b[t] = jnp.concatenate(
            [
                shifted(act_odd, 1, half).astype(BF16),
                act_even.astype(BF16),
                act_odd.astype(BF16),
            ],
            axis=-1,
        ).reshape(inner // 2, 2, half, 3 * chans)
    wide = cot_ref.shape[-1]
    tall = 4 * short
    grads = [cot_ref[t, 1 : tall + 1].reshape(tall * half, wide) for t in range(frames)]
    grad = jnp.concatenate(grads, axis=0)
    for kh in range(3):
        lo, parity = divmod(kh, 2)
        piece = [
            stacked_b[t, lo : lo + tall, parity].reshape(tall * half, 3 * chans)
            for t in (0, core)
        ]
        total = mm_tn(jnp.concatenate(piece, axis=0), grad)
        total_b[3 * kh : 3 * kh + 3] = total.reshape(3, chans, wide)
    emit(total_b, pieces)


def backward_kernel(last, join, cot_ref, pre_ref, stacked_a, weight_b, *refs):
    if join:
        refs[1 + join][:, :, weight_b.shape[3] :] = refs[0][...]
        refs = refs[1:]
    pieces, (pre_grad, total_a) = (refs[:-2], refs[-2:])
    core, side, plane = position()
    frames, ext_g, half, wide = cot_ref.shape
    chans = weight_b.shape[3]
    inner = pre_ref.shape[1]
    width = 2 * half
    mid = inner // 2
    cot = cot_ref[...].reshape(frames * ext_g, half, wide)
    ahead = shifted(cot.astype(F32), -1, half).astype(BF16)
    both = jnp.concatenate([cot, ahead], axis=-1).reshape(frames, ext_g, half, 2 * wide)
    later = both[:, 1:].reshape(frames * mid * half, 2 * wide)
    sooner = both[:, :-1].reshape(frames * mid * half, 2 * wide)
    zero = jnp.zeros((chans, wide), BF16)

    def taps(kt, kh):
        left, mid, right = (folded(weight_b, kt, kh, kw) for kw in range(3))
        return jnp.concatenate(
            [
                jnp.concatenate([mid, zero], axis=1),
                jnp.concatenate([right, left], axis=1),
            ],
            axis=0,
        )

    def rows_of(kt):
        even = mm_nt(later, taps(kt, 1))
        odd = mm_nt(later, taps(kt, 0)) + mm_nt(sooner, taps(kt, 2))
        shape = (frames, mid, half, 2 * chans)
        return (even.reshape(shape), odd.reshape(shape))

    copies = [rows_of(kt) for kt in range(2)]
    row = lax.broadcasted_iota(jnp.int32, (inner, half, chans), 0)
    hidden = ((plane == 0) & (row == 0)) | ((plane == last) & (row == inner - 1))
    for t in range(frames):
        sums = []
        for parity in range(2):
            total = copies[1][parity][t]
            if t == 0:
                total = total + (copies[0][parity][0] + copies[0][parity][1])
            sums.append(total)
        grad = jnp.stack([sums[1], sums[0]], axis=1).reshape(inner, half, 2 * chans)
        for parity in range(2):
            act_grad = grad[:, :, parity * chans : (parity + 1) * chans]
            pre = pre_ref[t, :, parity * half : (parity + 1) * half]
            sig = jax.nn.sigmoid(pre)
            value = act_grad * sig * (1.0 + pre * (1.0 - sig))
            value = jnp.where(hidden, 0.0, value).astype(BF16)
            pre_grad[t, :, parity * half : (parity + 1) * half] = value
    rows = inner - 2
    grads = [pre_grad[t, 1 : rows + 1].reshape(rows * width, chans) for t in range(frames)]
    grad = jnp.concatenate(grads, axis=0)
    field = jnp.concatenate(
        [
            jnp.concatenate(
                [
                    stacked_a[t, kh + 1 : kh + 1 + rows].reshape(rows * width, 3 * chans)
                    for t in (0, core)
                ],
                axis=0,
            )
            for kh in range(3)
        ],
        axis=1,
    )
    total = mm(grad.T, field)
    for k in range(9):
        total_a[k] = total[:, k * chans : (k + 1) * chans].T
    emit(total_a, pieces)


def output_kernel(stacked_b, pre_grad, weight_a, weight_b, encoded, frames_grad, flat):
    core, side, _ = position()
    place = 2 * side + core
    frames, _, _, half, _ = stacked_b.shape
    rows, width, chans = frames_grad.shape[1:]
    short = rows // 2
    wide = encoded.shape[-1]
    count = short * half
    shared = jnp.zeros((count, wide), F32)
    latest = jnp.zeros((frames * count, wide), F32)
    for kh in range(3):
        lo, parity = divmod(kh, 2)
        piece = [
            stacked_b[t, pl.ds(short * place + lo, short), parity].reshape(count, 3 * chans)
            for t in range(frames)
        ]
        shared += mm(piece[0], weight_b[0, kh]) + mm(piece[0], weight_b[1, kh])
        latest += mm(jnp.concatenate(piece, axis=0), weight_b[2, kh])
    for t in range(frames):
        value = shared + latest[t * count : (t + 1) * count]
        encoded[t] = value.astype(BF16).reshape(short, half, wide)

    ext = rows + 2
    own = pre_grad[:, pl.ds(rows * place, ext)].astype(F32)
    even = own[:, :, 0:half].reshape(frames * ext, half, chans)
    odd = own[:, :, half:width].reshape(frames * ext, half, chans)
    before = shifted(odd, 1, half).astype(BF16)
    after = shifted(even, -1, half).astype(BF16)
    even_16, odd_16 = (even.astype(BF16), odd.astype(BF16))
    stacked = jnp.stack(
        [
            jnp.concatenate([odd_16, even_16, before], axis=-1),
            jnp.concatenate([after, odd_16, even_16], axis=-1),
        ],
        axis=1,
    ).reshape(frames, ext, width, 3 * chans)
    early = jnp.zeros((frames * rows * width, chans), F32)
    late = jnp.zeros((frames * rows * width, chans), F32)
    for kh in range(3):
        piece = stacked[:, 2 - kh : 2 - kh + rows].reshape(frames * rows * width, 3 * chans)
        for kt in range(3):
            taps = jnp.concatenate([weight_a[kt, kh, kw] for kw in range(3)], axis=1)
            if kt == 2:
                late += mm_nt(piece, taps)
            else:
                early += mm_nt(piece, taps)
    early = early.reshape(frames, rows, 2, half, chans)
    late = late.reshape(frames, rows, 2, half, chans)
    even = even.reshape(frames, ext, half, chans)[:, 1 : rows + 1]
    odd = odd.reshape(frames, ext, half, chans)[:, 1 : rows + 1]
    size = rows * half
    for t in range(frames):
        total = late[t]
        if t == 0:
            total = total + (early[0] + early[1])
        for parity, value in ((0, even), (1, odd)):
            summed = value[t] + total[:, parity]
            flat[pl.ds(t * 2 * size + parity, size, stride=2), :] = summed.reshape(size, chans)
    frames_grad[...] = flat[...].reshape(frames_grad.shape).astype(BF16)


def finish_kernel(scale, count, *refs):
    chans = refs[0].shape[-1]
    shared, out = (refs[2 * count : -1], refs[-1])

    def total(parts, lanes):
        value = parts[0][...].astype(F32)
        for part in parts[1:]:
            value = value + part[...].astype(F32)
        for part in shared:
            value = value + part[:, :, lanes].astype(F32)
        return (value * scale).astype(BF16)

    out[:, :, 0:chans] = total(refs[:count], slice(0, chans))
    out[:, :, chans:] = total(refs[count : 2 * count], slice(chans, None))


def assemble_kernel(places, planes, *refs):
    pieces, (out_a, out_b) = (refs[:-2], refs[-2:])
    core, side, plane = position()
    chans = out_a.shape[-1]
    rows = pieces[0].shape[1]
    for piece, (flip_core, flip_side, step) in zip(pieces, places, strict=True):
        tap = core ^ flip_core
        source = (plane - step + planes) % planes
        at = pl.multiple_of((side ^ flip_side) * (chans // 2) + source * rows, rows)
        for slot in (2 * tap, 1 + tap):
            out_a[slot, :, pl.ds(at, rows)] = piece[:, :, 0:chans]
            out_b[slot, :, pl.ds(at, rows)] = piece[:, :, chans:]


def append_kernel(places, planes, old_a, old_b, *refs):
    del old_a, old_b
    count = len(places)
    pieces, (out_a, out_b, sems) = (refs[:count], refs[count:])
    core, side, plane = position()
    chans = out_a.shape[-1]
    rows = pieces[0].shape[1]

    def each(act):
        for index, (flip_core, flip_side, step) in enumerate(places):
            tap = core ^ flip_core
            source = (plane - step + planes) % planes
            at = pl.multiple_of((side ^ flip_side) * (chans // 2) + source * rows, rows)
            for k, out in enumerate((out_a, out_b)):
                lanes = slice(0, chans) if k == 0 else slice(chans, None)
                piece = pieces[index].at[:, :, lanes]
                move = pltpu.make_async_copy(
                    piece, out.at[tap * 2, :, pl.ds(at, rows)], sems.at[index, k]
                )
                twin = pltpu.make_async_copy(
                    piece, out.at[1, :, pl.ds(at, rows)], sems.at[index, 2 + k]
                )
                act(move)
                pl.when(tap == 0)(lambda twin=twin: act(twin))

    each(lambda copy: copy.start())
    each(lambda copy: copy.wait())


def call(
    body, outs, args, scratch=(), flops=0, whole=0, limit=VMEM_LIMIT, aliases=None, size=10**4
):
    extra = {}
    if whole:
        held = pl.BlockSpec(memory_space=pl.ANY)
        inside = pl.BlockSpec(memory_space=pltpu.VMEM)
        extra["in_specs"] = [held] * whole + [inside] * (len(args) - whole)
    if aliases:
        extra["out_specs"] = (held,) * len(outs)
        extra["input_output_aliases"] = aliases
    return pl.pallas_call(
        body,
        out_shape=outs,
        scratch_shapes=scratch,
        compiler_params=pltpu.CompilerParams(vmem_limit_bytes=limit),
        cost_estimate=pl.CostEstimate(flops=flops, bytes_accessed=size, transcendentals=0),
        **extra,
    )(*args)


def on_device(frames, weight_a, weight_b, cotangent):
    count, rows, width, chans = frames.shape
    assert count == 2
    wide = weight_b.shape[-1]
    half = width // 2
    n = lax.axis_size(AXIS)
    planes = n // 4
    core, side, plane = position()
    shape = jax.ShapeDtypeStruct

    def send(value, pairs):
        return lax.ppermute(value, AXIS, pairs)

    swap_core = [(i, i ^ 1) for i in range(n)]
    swap_side = [(i, i ^ 2) for i in range(n)]
    along = []
    for k in range(0, n - 4, 4):
        along += [(k + 2, k + 6), (k + 3, k + 4), (k + 4, k + 3), (k + 5, k + 1)]

    pack, edge = call(
        edge_kernel,
        (
            shape((count, rows + rows // 2, width, chans), BF16),
            shape((count, 3, width, chans), BF16),
        ),
        (frames, cotangent),
        [pltpu.SemaphoreType.DMA((6,))],
        whole=2,
        limit=None,
        flops=4 * 10**9,
    )
    outer = jnp.where(core == side, edge, send(edge, swap_core))
    packs = [send(pack, swap_core), send(pack, swap_side), None]
    edges = [send(outer, along), None]
    edges[1] = send(edges[0], swap_core)
    packs[1], edges[0] = lax.optimization_barrier((packs[1], edges[0]))
    packs[2] = send(packs[1], swap_core)
    staged_a, staged_b = (weight_a, weight_b)

    inner = 4 * rows + 2
    kernel_a = staged_a.reshape(3, 3, 3 * chans, chans)
    kernel_b = staged_b.reshape(3, 3, 3 * chans, wide)
    part = chans // 2
    split = planes if part % (8 * planes) == 0 else 1

    def pieces_of(outputs):
        own = (9, part // split, outputs)
        return (shape(own, F32),) + (shape(own, BF16),) * (split - 1)

    def forward(*refs):
        forward_kernel(split, *refs)

    join = split // 2 if split > 2 else 0

    def backward(*refs):
        backward_kernel(planes - 1, join, *refs)

    *pieces_b, pre, stacked_a, stacked_b, cot = call(
        forward,
        pieces_of(wide)
        + (
            shape((count, inner, width, chans), F32),
            shape((count, inner + 2, width, 3 * chans), BF16),
            shape((count, inner // 2, 2, half, 3 * chans), BF16),
            shape((count, 2 * rows + 2, half, wide), BF16),
        ),
        (frames, cotangent, *packs, *edges, kernel_a),
        [
            pltpu.VMEM((count * (inner + 2) * width, chans), F32),
            pltpu.VMEM((9, chans, wide), F32),
        ],
        flops=10**7,
    )
    shapes_a = list(pieces_of(chans))
    joined = ()
    if join:
        shapes_a[join] = shape((9, part // split, chans + wide), BF16)
        joined = (pieces_b[join],)
    *pieces_a, pre_grad = call(
        backward,
        (*shapes_a, shape((count, inner, width, chans), BF16)),
        (cot, pre, stacked_a, staged_b, *joined),
        [pltpu.VMEM((9, chans, chans), F32)],
        flops=10**7,
    )
    def outputs(stacked_b):
        return call(
            output_kernel,
            (shape(cotangent.shape, BF16), shape(frames.shape, BF16)),
            (stacked_b, pre_grad, staged_a, kernel_b),
            [pltpu.VMEM((count * rows * width, chans), F32)],
            flops=10**7,
        )

    scale = (count * rows * n * width) ** (-0.5)
    if split != planes:
        encoded, frames_grad = outputs(stacked_b)
        taps = jnp.arange(2)[:, None, None, None, None] == core
        sides = jnp.arange(2)[None, None, :, None, None] == side
        both = []
        for value in (pieces_a[0], pieces_b[0]):
            slots = jnp.where(taps & sides, value[None, :, None], 0.0)
            total = lax.psum(slots, AXIS) * scale
            total = total.astype(BF16).reshape(2, 3, 3, chans, -1)
            both.append(jnp.concatenate([total[:1], total], axis=0))
        return (encoded, frames_grad, both[0], both[1])

    rotations = [[(i, (i + 4 * step) % n) for i in range(n)] for step in range(planes)]
    close = [step for step in range(1, planes) if step != join]
    got_b = [send(pieces_b[step], rotations[step]) for step in close]
    if join:
        gate = lax.optimization_barrier((*got_b, pieces_a[close[-1]]))
        *got_b, pieces_a[close[-1]] = gate
    got_a = [send(pieces_a[step], rotations[step]) for step in close]
    both = [send(pieces_a[join], rotations[join])] if join else []

    def finish(*refs):
        finish_kernel(scale, 1 + len(close), *refs)

    encoded, frames_grad = outputs(stacked_b)
    held = lax.optimization_barrier((pieces_a[0], encoded, frames_grad))
    pieces_a[0], encoded, frames_grad = held
    piece = shape((9, part // planes, chans + wide), BF16)
    (own,) = call(finish, (piece,), (pieces_a[0], *got_a, pieces_b[0], *got_b, *both))
    column = {(0, 0, 0): own}
    order = sorted(range(1, planes), key=lambda step: min(step, planes - step))
    for step in order[:-1]:
        column[0, 0, step] = send(own, rotations[step])
    if planes == 1:
        column[0, 1, 0] = send(own, swap_side)
    else:
        far = (0, 0, order[-1])
        column[far] = send(own, rotations[order[-1]])
        for step in (0, *order[:-1]):
            column[0, 1, step] = send(column[0, 0, step], swap_side)
        if len(order) > 1:
            key = (0, 1, order[0])
            column[far], column[key] = lax.optimization_barrier((column[far], column[key]))
        column[0, 1, far[2]] = send(column[far], swap_side)
    last = (0, 1, order[-1] if order else 0)
    for (_, flip, step), value in list(column.items()):
        if (0, flip, step) != last:
            column[1, flip, step] = send(value, swap_core)
    slow = column.pop(last)
    tail = {key: column.pop(key) for key in list(column) if key[1] and key[2]}
    places = tuple(column)

    def assemble(*refs):
        assemble_kernel(places, planes, *refs)

    grads = call(
        assemble,
        (shape((3, 9, chans, chans), BF16), shape((3, 9, chans, wide), BF16)),
        tuple(column.values()),
    )
    slow, *grads = lax.optimization_barrier((slow, *grads))
    tail[last] = slow
    tail[1, *last[1:]] = send(slow, swap_core)
    ends = tuple(tail)

    def append(*refs):
        append_kernel(ends, planes, *refs)

    grad_a, grad_b = call(
        append,
        tuple(shape(x.shape, x.dtype) for x in grads),
        (*grads, *tail.values()),
        [pltpu.SemaphoreType.DMA((len(ends), 4))],
        whole=2,
        aliases={0: 0, 1: 1},
    )
    return (encoded, frames_grad, grad_a.reshape(weight_a.shape), grad_b.reshape(weight_b.shape))


def solution(mesh):
    in_specs = (P("groups", "height", None, None), P(), P(), P("groups", "height", None, None))
    out_specs = (
        P("groups", "height", None, None),
        P("groups", "height", None, None),
        P("groups", None, None, None, None),
        P("groups", None, None, None, None),
    )
    return jax.shard_map(
        on_device, mesh=mesh, in_specs=in_specs, out_specs=out_specs, check_vma=False
    )
```

```python
import jax
import jax.numpy as jnp
from jax import lax
from jax.experimental import pallas as pl
from jax.experimental.pallas import tpu as pltpu
from jax.sharding import PartitionSpec as P

F32 = jnp.float32
BF16 = jnp.bfloat16
AXIS = "height"
VMEM_LIMIT = 24 * 1024 * 1024


def position():
    index = lax.axis_index(AXIS)
    return (index % 2, (index // 2) % 2, index // 4)


def folded(weight, kt, *taps):
    if kt:
        return weight[(2, *taps)]
    return (weight[(0, *taps)].astype(F32) + weight[(1, *taps)].astype(F32)).astype(BF16)


def emit(total, outs):
    _, side, plane = position()
    part = total.shape[1] // 2
    count = len(outs)
    rows = part // count
    for step, out in enumerate(outs):
        owner = (plane + step) % count if count > 1 else 0
        at = pl.multiple_of(side * part + owner * rows, rows)
        value = total[:, pl.ds(at, rows)].astype(out.dtype)
        out[:, :, 0 : value.shape[-1]] = value


def mm(a, b):
    return lax.dot_general(a, b, (((1,), (0,)), ((), ())), preferred_element_type=F32)


def mm_nt(a, b):
    return lax.dot_general(a, b, (((1,), (1,)), ((), ())), preferred_element_type=F32)


def mm_tn(a, b):
    return lax.dot_general(a, b, (((0,), (0,)), ((), ())), preferred_element_type=F32)


def shifted(field, by, half):
    rows, _, chans = field.shape
    flat = field.reshape(rows * half, chans)
    column = lax.broadcasted_iota(jnp.int32, flat.shape, 0) % half
    moved = pltpu.roll(flat, by % (rows * half), axis=0)
    edge = 0 if by > 0 else half - 1
    return jnp.where(column == edge, 0.0, moved).reshape(field.shape)


def wide_pair(even, odd, half):
    before = shifted(odd, 1, half).astype(BF16)
    after = shifted(even, -1, half).astype(BF16)
    even, odd = (even.astype(BF16), odd.astype(BF16))
    return (
        jnp.concatenate([before, even, odd], axis=-1),
        jnp.concatenate([even, odd, after], axis=-1),
    )


def edge_kernel(frames, cot, pack, edge, sems):
    core, _, _ = position()
    rows, width = frames.shape[1:3]
    short, half = cot.shape[1:3]
    chans = frames.shape[-1]
    first = pl.ds(core * (rows - 2), 2)
    only = pl.ds(core * (short - 1), 1)
    moves = [(frames.at[:, first], edge.at[:, 0:2]), (frames, pack.at[:, 0:rows])]
    for k in range(2):
        lanes = slice(k * chans, (k + 1) * chans)
        columns = slice(k * half, (k + 1) * half)
        moves.append((cot.at[:, only, :, lanes], edge.at[:, 2:3, columns]))
        moves.append((cot.at[:, :, :, lanes], pack.at[:, rows:, columns]))
    copies = [pltpu.make_async_copy(*move, sems.at[k]) for k, move in enumerate(moves)]
    for copy in copies:
        copy.start()
    for copy in copies:
        copy.wait()


def forward_kernel(split, *refs):
    own_f, own_g, packs, edges, weight_a = (*refs[0:2], refs[2:5], refs[5:7], refs[7])
    outs, flat, total_b = (refs[8:-2], refs[-2], refs[-1])
    pieces, (pre_ref, stacked_a, stacked_b, cot_ref) = (outs[:split], outs[split:])
    core, side, plane = position()
    place = 2 * side + core
    frames, rows, width, chans = own_f.shape
    short = rows // 2
    half = width // 2
    ext = 4 * rows + 4
    block = rows * width

    def edge(t, own):
        chosen = jnp.where(core == own, edges[0][t].astype(F32), edges[1][t].astype(F32))
        cot = jnp.concatenate([chosen[2, 0:half], chosen[2, half:]], axis=-1)
        return (chosen[0:2].reshape(2 * width, chans), cot.astype(BF16))

    for t in range(frames):
        base = t * ext * width
        flat[base : base + 2 * width], cot_ref[t, 0] = edge(t, 0)
        low = base + (ext - 2) * width
        flat[low : low + 2 * width], cot_ref[t, 4 * short + 1] = edge(t, 1)
        for k in range(4):
            at = pl.multiple_of(base + 2 * width + (place ^ k) * block, 2 * width)
            spot = pl.ds(1 + (place ^ k) * short, short)
            if k == 0:
                field, cot = (own_f[t], own_g[t])
            else:
                pack = packs[k - 1]
                cot = (pack[t, rows:, 0:half], pack[t, rows:, half:])
                field, cot = (pack[t, 0:rows], jnp.concatenate(cot, axis=-1))
            flat[pl.ds(at, block)] = field.astype(F32).reshape(block, chans)
            cot_ref[t, spot] = cot
    count = frames * ext
    even = flat[pl.ds(0, count * half, stride=2), :].reshape(count, half, chans)
    odd = flat[pl.ds(1, count * half, stride=2), :].reshape(count, half, chans)
    taps_even, taps_odd = wide_pair(even, odd, half)
    stacked_a[:, :, 0:half] = taps_even.reshape(frames, ext, half, 3 * chans)
    stacked_a[:, :, half:width] = taps_odd.reshape(frames, ext, half, 3 * chans)

    inner = ext - 2
    taps = [
        jnp.concatenate([folded(weight_a, kt, kh) for kh in range(3)], axis=0) for kt in range(2)
    ]
    fields = [
        jnp.concatenate(
            [
                stacked_a[t, kh : kh + inner].reshape(inner * width, 3 * chans)
                for kh in range(3)
            ],
            axis=1,
        )
        for t in range(2)
    ]
    early = mm(fields[0], jnp.concatenate(taps, axis=1))
    shared = early[:, :chans]
    latest = [early[:, chans:], mm(fields[1], taps[1])]
    even = even.reshape(frames, ext, half, chans)
    odd = odd.reshape(frames, ext, half, chans)
    outside = plane == 0
    row = lax.broadcasted_iota(jnp.int32, (inner, half, chans), 0)
    hidden = outside & (row == 0)
    for t in range(frames):
        conv = (shared + latest[t]).reshape(inner, 2, half, chans)
        pre_even = even[t, 1 : ext - 1] + conv[:, 0]
        pre_odd = odd[t, 1 : ext - 1] + conv[:, 1]
        pre_ref[t, :, 0:half] = pre_even
        pre_ref[t, :, half:width] = pre_odd
        act_even = jnp.where(hidden, 0.0, pre_even * jax.nn.sigmoid(pre_even))
        act_odd = jnp.where(hidden, 0.0, pre_odd * jax.nn.sigmoid(pre_odd))
        stacked_b[t] = jnp.concatenate(
            [
                shifted(act_odd, 1, half).astype(BF16),
                act_even.astype(BF16),
                act_odd.astype(BF16),
            ],
            axis=-1,
        ).reshape(inner // 2, 2, half, 3 * chans)
    wide = cot_ref.shape[-1]
    tall = 4 * short
    grads = [cot_ref[t, 1 : tall + 1].reshape(tall * half, wide) for t in range(frames)]
    grad = jnp.concatenate(grads, axis=0)
    for kh in range(3):
        lo, parity = divmod(kh, 2)
        piece = [
            stacked_b[t, lo : lo + tall, parity].reshape(tall * half, 3 * chans)
            for t in (0, core)
        ]
        total = mm_tn(jnp.concatenate(piece, axis=0), grad)
        total_b[3 * kh : 3 * kh + 3] = total.reshape(3, chans, wide)
    emit(total_b, pieces)


def backward_kernel(last, joins, cot_ref, pre_ref, stacked_a, weight_b, *refs):
    given, refs = (refs[: len(joins)], refs[len(joins) :])
    for step, piece in zip(joins, given, strict=True):
        refs[step][:, :, weight_b.shape[3] :] = piece[...]
    pieces, (pre_grad, total_a) = (refs[:-2], refs[-2:])
    core, side, plane = position()
    frames, ext_g, half, wide = cot_ref.shape
    chans = weight_b.shape[3]
    inner = pre_ref.shape[1]
    width = 2 * half
    mid = inner // 2
    cot = cot_ref[...].reshape(frames * ext_g, half, wide)
    ahead = shifted(cot.astype(F32), -1, half).astype(BF16)
    both = jnp.concatenate([cot, ahead], axis=-1).reshape(frames, ext_g, half, 2 * wide)
    later = both[:, 1:].reshape(frames * mid * half, 2 * wide)
    sooner = both[:, :-1].reshape(frames * mid * half, 2 * wide)
    zero = jnp.zeros((chans, wide), BF16)

    def taps(kt, kh):
        left, mid, right = (folded(weight_b, kt, kh, kw) for kw in range(3))
        return jnp.concatenate(
            [
                jnp.concatenate([mid, zero], axis=1),
                jnp.concatenate([right, left], axis=1),
            ],
            axis=0,
        )

    def rows_of(kt):
        even = mm_nt(later, taps(kt, 1))
        odd = mm_nt(later, taps(kt, 0)) + mm_nt(sooner, taps(kt, 2))
        shape = (frames, mid, half, 2 * chans)
        return (even.reshape(shape), odd.reshape(shape))

    copies = [rows_of(kt) for kt in range(2)]
    row = lax.broadcasted_iota(jnp.int32, (inner, half, chans), 0)
    hidden = ((plane == 0) & (row == 0)) | ((plane == last) & (row == inner - 1))
    for t in range(frames):
        sums = []
        for parity in range(2):
            total = copies[1][parity][t]
            if t == 0:
                total = total + (copies[0][parity][0] + copies[0][parity][1])
            sums.append(total)
        grad = jnp.stack([sums[1], sums[0]], axis=1).reshape(inner, half, 2 * chans)
        for parity in range(2):
            act_grad = grad[:, :, parity * chans : (parity + 1) * chans]
            pre = pre_ref[t, :, parity * half : (parity + 1) * half]
            sig = jax.nn.sigmoid(pre)
            value = act_grad * sig * (1.0 + pre * (1.0 - sig))
            value = jnp.where(hidden, 0.0, value).astype(BF16)
            pre_grad[t, :, parity * half : (parity + 1) * half] = value
    rows = inner - 2
    grads = [pre_grad[t, 1 : rows + 1].reshape(rows * width, chans) for t in range(frames)]
    grad = jnp.concatenate(grads, axis=0)
    field = jnp.concatenate(
        [
            jnp.concatenate(
                [
                    stacked_a[t, kh + 1 : kh + 1 + rows].reshape(rows * width, 3 * chans)
                    for t in (0, core)
                ],
                axis=0,
            )
            for kh in range(3)
        ],
        axis=1,
    )
    total = mm(grad.T, field)
    for k in range(9):
        total_a[k] = total[:, k * chans : (k + 1) * chans].T
    emit(total_a, pieces)


def output_kernel(stacked_b, pre_grad, weight_a, weight_b, encoded, frames_grad, flat):
    core, side, _ = position()
    place = 2 * side + core
    frames, _, _, half, _ = stacked_b.shape
    rows, width, chans = frames_grad.shape[1:]
    short = rows // 2
    wide = encoded.shape[-1]
    count = short * half
    shared = jnp.zeros((count, wide), F32)
    latest = jnp.zeros((frames * count, wide), F32)
    for kh in range(3):
        lo, parity = divmod(kh, 2)
        piece = [
            stacked_b[t, pl.ds(short * place + lo, short), parity].reshape(count, 3 * chans)
            for t in range(frames)
        ]
        shared += mm(piece[0], weight_b[0, kh]) + mm(piece[0], weight_b[1, kh])
        latest += mm(jnp.concatenate(piece, axis=0), weight_b[2, kh])
    for t in range(frames):
        value = shared + latest[t * count : (t + 1) * count]
        encoded[t] = value.astype(BF16).reshape(short, half, wide)

    ext = rows + 2
    own = pre_grad[:, pl.ds(rows * place, ext)].astype(F32)
    even = own[:, :, 0:half].reshape(frames * ext, half, chans)
    odd = own[:, :, half:width].reshape(frames * ext, half, chans)
    before = shifted(odd, 1, half).astype(BF16)
    after = shifted(even, -1, half).astype(BF16)
    even_16, odd_16 = (even.astype(BF16), odd.astype(BF16))
    stacked = jnp.stack(
        [
            jnp.concatenate([odd_16, even_16, before], axis=-1),
            jnp.concatenate([after, odd_16, even_16], axis=-1),
        ],
        axis=1,
    ).reshape(frames, ext, width, 3 * chans)
    early = jnp.zeros((frames * rows * width, chans), F32)
    late = jnp.zeros((frames * rows * width, chans), F32)
    for kh in range(3):
        piece = stacked[:, 2 - kh : 2 - kh + rows].reshape(frames * rows * width, 3 * chans)
        for kt in range(3):
            taps = jnp.concatenate([weight_a[kt, kh, kw] for kw in range(3)], axis=1)
            if kt == 2:
                late += mm_nt(piece, taps)
            else:
                early += mm_nt(piece, taps)
    early = early.reshape(frames, rows, 2, half, chans)
    late = late.reshape(frames, rows, 2, half, chans)
    even = even.reshape(frames, ext, half, chans)[:, 1 : rows + 1]
    odd = odd.reshape(frames, ext, half, chans)[:, 1 : rows + 1]
    size = rows * half
    for t in range(frames):
        total = late[t]
        if t == 0:
            total = total + (early[0] + early[1])
        for parity, value in ((0, even), (1, odd)):
            summed = value[t] + total[:, parity]
            flat[pl.ds(t * 2 * size + parity, size, stride=2), :] = summed.reshape(size, chans)
    frames_grad[...] = flat[...].reshape(frames_grad.shape).astype(BF16)


def finish_kernel(scale, count, *refs):
    chans = refs[0].shape[-1]
    shared, out = (refs[2 * count : -1], refs[-1])

    def total(parts, lanes):
        value = parts[0][...].astype(F32)
        for part in parts[1:]:
            value = value + part[...].astype(F32)
        for part in shared:
            value = value + part[:, :, lanes].astype(F32)
        return (value * scale).astype(BF16)

    out[:, :, 0:chans] = total(refs[:count], slice(0, chans))
    out[:, :, chans:] = total(refs[count : 2 * count], slice(chans, None))


def assemble_kernel(places, planes, *refs):
    pieces, (out_a, out_b) = (refs[:-2], refs[-2:])
    core, side, plane = position()
    chans = out_a.shape[-1]
    rows = pieces[0].shape[1]
    for piece, (flip_core, flip_side, step) in zip(pieces, places, strict=True):
        tap = core ^ flip_core
        source = (plane - step + planes) % planes
        at = pl.multiple_of((side ^ flip_side) * (chans // 2) + source * rows, rows)
        for slot in (2 * tap, 1 + tap):
            out_a[slot, :, pl.ds(at, rows)] = piece[:, :, 0:chans]
            out_b[slot, :, pl.ds(at, rows)] = piece[:, :, chans:]


def append_kernel(places, planes, old_a, old_b, *refs):
    del old_a, old_b
    count = len(places)
    pieces, (out_a, out_b, sems) = (refs[:count], refs[count:])
    core, side, plane = position()
    chans = out_a.shape[-1]
    rows = pieces[0].shape[1]

    def each(act):
        for index, (flip_core, flip_side, step) in enumerate(places):
            tap = core ^ flip_core
            source = (plane - step + planes) % planes
            at = pl.multiple_of((side ^ flip_side) * (chans // 2) + source * rows, rows)
            for k, out in enumerate((out_a, out_b)):
                lanes = slice(0, chans) if k == 0 else slice(chans, None)
                piece = pieces[index].at[:, :, lanes]
                move = pltpu.make_async_copy(
                    piece, out.at[tap * 2, :, pl.ds(at, rows)], sems.at[index, k]
                )
                twin = pltpu.make_async_copy(
                    piece, out.at[1, :, pl.ds(at, rows)], sems.at[index, 2 + k]
                )
                act(move)
                pl.when(tap == 0)(lambda twin=twin: act(twin))

    each(lambda copy: copy.start())
    each(lambda copy: copy.wait())


def call(
    body, outs, args, scratch=(), flops=0, whole=0, limit=VMEM_LIMIT, aliases=None, size=10**4
):
    extra = {}
    if whole:
        held = pl.BlockSpec(memory_space=pl.ANY)
        inside = pl.BlockSpec(memory_space=pltpu.VMEM)
        extra["in_specs"] = [held] * whole + [inside] * (len(args) - whole)
    if aliases:
        extra["out_specs"] = (held,) * len(outs)
        extra["input_output_aliases"] = aliases
    return pl.pallas_call(
        body,
        out_shape=outs,
        scratch_shapes=scratch,
        compiler_params=pltpu.CompilerParams(vmem_limit_bytes=limit),
        cost_estimate=pl.CostEstimate(flops=flops, bytes_accessed=size, transcendentals=0),
        **extra,
    )(*args)


def on_device(frames, weight_a, weight_b, cotangent):
    count, rows, width, chans = frames.shape
    assert count == 2
    wide = weight_b.shape[-1]
    half = width // 2
    n = lax.axis_size(AXIS)
    planes = n // 4
    core, side, plane = position()
    shape = jax.ShapeDtypeStruct

    def send(value, pairs):
        return lax.ppermute(value, AXIS, pairs)

    swap_core = [(i, i ^ 1) for i in range(n)]
    swap_side = [(i, i ^ 2) for i in range(n)]
    along = []
    for k in range(0, n - 4, 4):
        along += [(k + 2, k + 6), (k + 3, k + 4), (k + 4, k + 3), (k + 5, k + 1)]

    pack, edge = call(
        edge_kernel,
        (
            shape((count, rows + rows // 2, width, chans), BF16),
            shape((count, 3, width, chans), BF16),
        ),
        (frames, cotangent),
        [pltpu.SemaphoreType.DMA((6,))],
        whole=2,
        limit=None,
        flops=4 * 10**9,
    )
    outer = jnp.where(core == side, edge, send(edge, swap_core))
    packs = [send(pack, swap_core), send(pack, swap_side), None]
    edges = [send(outer, along), None]
    edges[1] = send(edges[0], swap_core)
    packs[1], edges[0] = lax.optimization_barrier((packs[1], edges[0]))
    packs[2] = send(packs[1], swap_core)
    staged_a, staged_b = (weight_a, weight_b)

    inner = 4 * rows + 2
    kernel_a = staged_a.reshape(3, 3, 3 * chans, chans)
    kernel_b = staged_b.reshape(3, 3, 3 * chans, wide)
    part = chans // 2
    split = planes if part % (8 * planes) == 0 else 1

    def pieces_of(outputs):
        own = (9, part // split, outputs)
        return (shape(own, F32),) + (shape(own, BF16),) * (split - 1)

    def forward(*refs):
        forward_kernel(split, *refs)

    far = split // 2
    joins = tuple(step for step in range(1, split) if step != far)

    def backward(*refs):
        backward_kernel(planes - 1, joins, *refs)

    *pieces_b, pre, stacked_a, stacked_b, cot = call(
        forward,
        pieces_of(wide)
        + (
            shape((count, inner, width, chans), F32),
            shape((count, inner + 2, width, 3 * chans), BF16),
            shape((count, inner // 2, 2, half, 3 * chans), BF16),
            shape((count, 2 * rows + 2, half, wide), BF16),
        ),
        (frames, cotangent, *packs, *edges, kernel_a),
        [
            pltpu.VMEM((count * (inner + 2) * width, chans), F32),
            pltpu.VMEM((9, chans, wide), F32),
        ],
        flops=10**7,
    )
    shapes_a = list(pieces_of(chans))
    for step in joins:
        shapes_a[step] = shape((9, part // split, chans + wide), BF16)
    joined = tuple(pieces_b[step] for step in joins)
    *pieces_a, pre_grad = call(
        backward,
        (*shapes_a, shape((count, inner, width, chans), BF16)),
        (cot, pre, stacked_a, staged_b, *joined),
        [pltpu.VMEM((9, chans, chans), F32)],
        flops=10**7,
    )
    def outputs(stacked_b):
        return call(
            output_kernel,
            (shape(cotangent.shape, BF16), shape(frames.shape, BF16)),
            (stacked_b, pre_grad, staged_a, kernel_b),
            [pltpu.VMEM((count * rows * width, chans), F32)],
            flops=10**7,
        )

    scale = (count * rows * n * width) ** (-0.5)
    if split != planes:
        encoded, frames_grad = outputs(stacked_b)
        taps = jnp.arange(2)[:, None, None, None, None] == core
        sides = jnp.arange(2)[None, None, :, None, None] == side
        both = []
        for value in (pieces_a[0], pieces_b[0]):
            slots = jnp.where(taps & sides, value[None, :, None], 0.0)
            total = lax.psum(slots, AXIS) * scale
            total = total.astype(BF16).reshape(2, 3, 3, chans, -1)
            both.append(jnp.concatenate([total[:1], total], axis=0))
        return (encoded, frames_grad, both[0], both[1])

    rotations = [[(i, (i + 4 * step) % n) for i in range(n)] for step in range(planes)]
    alone_a, alone_b = (pieces_a[:1], pieces_b[:1])
    if far:
        alone_b.append(send(pieces_b[far], rotations[far]))
        gate = lax.optimization_barrier((alone_b[1], pieces_a[far]))
        alone_b[1], pieces_a[far] = gate
        alone_a.append(send(pieces_a[far], rotations[far]))
    both = [send(pieces_a[step], rotations[step]) for step in joins]

    def finish(*refs):
        finish_kernel(scale, len(alone_a), *refs)

    encoded, frames_grad = outputs(stacked_b)
    held = lax.optimization_barrier((alone_a[0], encoded, frames_grad))
    alone_a[0], encoded, frames_grad = held
    piece = shape((9, part // planes, chans + wide), BF16)
    (own,) = call(finish, (piece,), (*alone_a, *alone_b, *both))
    column = {(0, 0, 0): own}
    order = sorted(range(1, planes), key=lambda step: min(step, planes - step))
    for step in order[:-1]:
        column[0, 0, step] = send(own, rotations[step])
    if planes == 1:
        column[0, 1, 0] = send(own, swap_side)
    else:
        distant = (0, 0, order[-1])
        column[distant] = send(own, rotations[order[-1]])
        for step in (0, *order[:-1]):
            column[0, 1, step] = send(column[0, 0, step], swap_side)
        if len(order) > 1:
            key = (0, 1, order[0])
            column[distant], column[key] = lax.optimization_barrier((column[distant], column[key]))
        column[0, 1, distant[2]] = send(column[distant], swap_side)
    last = (0, 1, order[-1] if order else 0)
    for (_, flip, step), value in list(column.items()):
        if (0, flip, step) != last:
            column[1, flip, step] = send(value, swap_core)
    slow = column.pop(last)
    tail = {key: column.pop(key) for key in list(column) if key[1] and key[2]}
    places = tuple(column)

    def assemble(*refs):
        assemble_kernel(places, planes, *refs)

    grads = call(
        assemble,
        (shape((3, 9, chans, chans), BF16), shape((3, 9, chans, wide), BF16)),
        tuple(column.values()),
    )
    slow, *grads = lax.optimization_barrier((slow, *grads))
    tail[last] = slow
    tail[1, *last[1:]] = send(slow, swap_core)
    ends = tuple(tail)

    def append(*refs):
        append_kernel(ends, planes, *refs)

    grad_a, grad_b = call(
        append,
        tuple(shape(x.shape, x.dtype) for x in grads),
        (*grads, *tail.values()),
        [pltpu.SemaphoreType.DMA((len(ends), 4))],
        whole=2,
        aliases={0: 0, 1: 1},
    )
    return (encoded, frames_grad, grad_a.reshape(weight_a.shape), grad_b.reshape(weight_b.shape))


def solution(mesh):
    in_specs = (P("groups", "height", None, None), P(), P(), P("groups", "height", None, None))
    out_specs = (
        P("groups", "height", None, None),
        P("groups", "height", None, None),
        P("groups", None, None, None, None),
        P("groups", None, None, None, None),
    )
    return jax.shard_map(
        on_device, mesh=mesh, in_specs=in_specs, out_specs=out_specs, check_vma=False
    )
```

```python
import jax
import jax.numpy as jnp
from jax import lax
from jax.experimental import pallas as pl
from jax.experimental.pallas import tpu as pltpu
from jax.sharding import PartitionSpec as P

F32 = jnp.float32
BF16 = jnp.bfloat16
AXIS = "height"
VMEM_LIMIT = 24 * 1024 * 1024


def position():
    index = lax.axis_index(AXIS)
    return (index % 2, (index // 2) % 2, index // 4)


def folded(weight, kt, *taps):
    if kt:
        return weight[(2, *taps)]
    return (weight[(0, *taps)].astype(F32) + weight[(1, *taps)].astype(F32)).astype(BF16)


def emit(total, outs):
    _, side, plane = position()
    part = total.shape[1] // 2
    count = len(outs)
    rows = part // count
    for step, out in enumerate(outs):
        owner = (plane + step) % count if count > 1 else 0
        at = pl.multiple_of(side * part + owner * rows, rows)
        value = total[:, pl.ds(at, rows)].astype(out.dtype)
        out[:, :, 0 : value.shape[-1]] = value


def mm(a, b):
    return lax.dot_general(a, b, (((1,), (0,)), ((), ())), preferred_element_type=F32)


def mm_nt(a, b):
    return lax.dot_general(a, b, (((1,), (1,)), ((), ())), preferred_element_type=F32)


def mm_tn(a, b):
    return lax.dot_general(a, b, (((0,), (0,)), ((), ())), preferred_element_type=F32)


def shifted(field, by, half):
    rows, _, chans = field.shape
    flat = field.reshape(rows * half, chans)
    column = lax.broadcasted_iota(jnp.int32, flat.shape, 0) % half
    moved = pltpu.roll(flat, by % (rows * half), axis=0)
    edge = 0 if by > 0 else half - 1
    return jnp.where(column == edge, 0.0, moved).reshape(field.shape)


def wide_pair(even, odd, half):
    before = shifted(odd, 1, half).astype(BF16)
    after = shifted(even, -1, half).astype(BF16)
    even, odd = (even.astype(BF16), odd.astype(BF16))
    return (
        jnp.concatenate([before, even, odd], axis=-1),
        jnp.concatenate([even, odd, after], axis=-1),
    )


def edge_kernel(frames, cot, pack, edge, sems):
    core, _, _ = position()
    rows, width = frames.shape[1:3]
    short, half = cot.shape[1:3]
    chans = frames.shape[-1]
    first = pl.ds(core * (rows - 2), 2)
    only = pl.ds(core * (short - 1), 1)
    moves = [(frames.at[:, first], edge.at[:, 0:2]), (frames, pack.at[:, 0:rows])]
    for k in range(2):
        lanes = slice(k * chans, (k + 1) * chans)
        columns = slice(k * half, (k + 1) * half)
        moves.append((cot.at[:, only, :, lanes], edge.at[:, 2:3, columns]))
        moves.append((cot.at[:, :, :, lanes], pack.at[:, rows:, columns]))
    copies = [pltpu.make_async_copy(*move, sems.at[k]) for k, move in enumerate(moves)]
    for copy in copies:
        copy.start()
    for copy in copies:
        copy.wait()


def forward_kernel(split, *refs):
    own_f, own_g, packs, edges, weight_a = (*refs[0:2], refs[2:5], refs[5:7], refs[7])
    outs, flat, total_b = (refs[8:-2], refs[-2], refs[-1])
    pieces, (pre_ref, stacked_a, stacked_b, cot_ref) = (outs[:split], outs[split:])
    core, side, plane = position()
    place = 2 * side + core
    frames, rows, width, chans = own_f.shape
    short = rows // 2
    half = width // 2
    ext = 4 * rows + 4
    block = rows * width

    def edge(t, own):
        chosen = jnp.where(core == own, edges[0][t].astype(F32), edges[1][t].astype(F32))
        cot = jnp.concatenate([chosen[2, 0:half], chosen[2, half:]], axis=-1)
        return (chosen[0:2].reshape(2 * width, chans), cot.astype(BF16))

    for t in range(frames):
        base = t * ext * width
        flat[base : base + 2 * width], cot_ref[t, 0] = edge(t, 0)
        low = base + (ext - 2) * width
        flat[low : low + 2 * width], cot_ref[t, 4 * short + 1] = edge(t, 1)
        for k in range(4):
            at = pl.multiple_of(base + 2 * width + (place ^ k) * block, 2 * width)
            spot = pl.ds(1 + (place ^ k) * short, short)
            if k == 0:
                field, cot = (own_f[t], own_g[t])
            else:
                pack = packs[k - 1]
                cot = (pack[t, rows:, 0:half], pack[t, rows:, half:])
                field, cot = (pack[t, 0:rows], jnp.concatenate(cot, axis=-1))
            flat[pl.ds(at, block)] = field.astype(F32).reshape(block, chans)
            cot_ref[t, spot] = cot
    count = frames * ext
    even = flat[pl.ds(0, count * half, stride=2), :].reshape(count, half, chans)
    odd = flat[pl.ds(1, count * half, stride=2), :].reshape(count, half, chans)
    taps_even, taps_odd = wide_pair(even, odd, half)
    stacked_a[:, :, 0:half] = taps_even.reshape(frames, ext, half, 3 * chans)
    stacked_a[:, :, half:width] = taps_odd.reshape(frames, ext, half, 3 * chans)

    inner = ext - 2
    taps = [
        jnp.concatenate([folded(weight_a, kt, kh) for kh in range(3)], axis=0) for kt in range(2)
    ]
    fields = [
        jnp.concatenate(
            [
                stacked_a[t, kh : kh + inner].reshape(inner * width, 3 * chans)
                for kh in range(3)
            ],
            axis=1,
        )
        for t in range(2)
    ]
    early = mm(fields[0], jnp.concatenate(taps, axis=1))
    shared = early[:, :chans]
    latest = [early[:, chans:], mm(fields[1], taps[1])]
    even = even.reshape(frames, ext, half, chans)
    odd = odd.reshape(frames, ext, half, chans)
    outside = plane == 0
    row = lax.broadcasted_iota(jnp.int32, (inner, half, chans), 0)
    hidden = outside & (row == 0)
    for t in range(frames):
        conv = (shared + latest[t]).reshape(inner, 2, half, chans)
        pre_even = even[t, 1 : ext - 1] + conv[:, 0]
        pre_odd = odd[t, 1 : ext - 1] + conv[:, 1]
        pre_ref[t, :, 0:half] = pre_even
        pre_ref[t, :, half:width] = pre_odd
        act_even = jnp.where(hidden, 0.0, pre_even * jax.nn.sigmoid(pre_even))
        act_odd = jnp.where(hidden, 0.0, pre_odd * jax.nn.sigmoid(pre_odd))
        stacked_b[t] = jnp.concatenate(
            [
                shifted(act_odd, 1, half).astype(BF16),
                act_even.astype(BF16),
                act_odd.astype(BF16),
            ],
            axis=-1,
        ).reshape(inner // 2, 2, half, 3 * chans)
    wide = cot_ref.shape[-1]
    tall = 4 * short
    grads = [cot_ref[t, 1 : tall + 1].reshape(tall * half, wide) for t in range(frames)]
    grad = jnp.concatenate(grads, axis=0)
    for kh in range(3):
        lo, parity = divmod(kh, 2)
        piece = [
            stacked_b[t, lo : lo + tall, parity].reshape(tall * half, 3 * chans)
            for t in (0, core)
        ]
        total = mm_tn(jnp.concatenate(piece, axis=0), grad)
        total_b[3 * kh : 3 * kh + 3] = total.reshape(3, chans, wide)
    emit(total_b, pieces)


def backward_kernel(last, joins, cot_ref, pre_ref, stacked_a, weight_b, *refs):
    given, refs = (refs[: len(joins)], refs[len(joins) :])
    for step, piece in zip(joins, given, strict=True):
        refs[step][:, :, weight_b.shape[3] :] = piece[...]
    pieces, (pre_grad, total_a) = (refs[:-2], refs[-2:])
    core, side, plane = position()
    frames, ext_g, half, wide = cot_ref.shape
    chans = weight_b.shape[3]
    inner = pre_ref.shape[1]
    width = 2 * half
    mid = inner // 2
    cot = cot_ref[...].reshape(frames * ext_g, half, wide)
    ahead = shifted(cot.astype(F32), -1, half).astype(BF16)
    both = jnp.concatenate([cot, ahead], axis=-1).reshape(frames, ext_g, half, 2 * wide)
    later = both[:, 1:].reshape(frames * mid * half, 2 * wide)
    sooner = both[:, :-1].reshape(frames * mid * half, 2 * wide)
    zero = jnp.zeros((chans, wide), BF16)

    def taps(kt, kh):
        left, mid, right = (folded(weight_b, kt, kh, kw) for kw in range(3))
        return jnp.concatenate(
            [
                jnp.concatenate([mid, zero], axis=1),
                jnp.concatenate([right, left], axis=1),
            ],
            axis=0,
        )

    def rows_of(kt):
        even = mm_nt(later, taps(kt, 1))
        odd = mm_nt(later, taps(kt, 0)) + mm_nt(sooner, taps(kt, 2))
        shape = (frames, mid, half, 2 * chans)
        return (even.reshape(shape), odd.reshape(shape))

    copies = [rows_of(kt) for kt in range(2)]
    row = lax.broadcasted_iota(jnp.int32, (inner, half, chans), 0)
    hidden = ((plane == 0) & (row == 0)) | ((plane == last) & (row == inner - 1))
    for t in range(frames):
        sums = []
        for parity in range(2):
            total = copies[1][parity][t]
            if t == 0:
                total = total + (copies[0][parity][0] + copies[0][parity][1])
            sums.append(total)
        grad = jnp.stack([sums[1], sums[0]], axis=1).reshape(inner, half, 2 * chans)
        for parity in range(2):
            act_grad = grad[:, :, parity * chans : (parity + 1) * chans]
            pre = pre_ref[t, :, parity * half : (parity + 1) * half]
            sig = jax.nn.sigmoid(pre)
            value = act_grad * sig * (1.0 + pre * (1.0 - sig))
            value = jnp.where(hidden, 0.0, value).astype(BF16)
            pre_grad[t, :, parity * half : (parity + 1) * half] = value
    rows = inner - 2
    grads = [pre_grad[t, 1 : rows + 1].reshape(rows * width, chans) for t in range(frames)]
    grad = jnp.concatenate(grads, axis=0)
    field = jnp.concatenate(
        [
            jnp.concatenate(
                [
                    stacked_a[t, kh + 1 : kh + 1 + rows].reshape(rows * width, 3 * chans)
                    for t in (0, core)
                ],
                axis=0,
            )
            for kh in range(3)
        ],
        axis=1,
    )
    total = mm(grad.T, field)
    for k in range(9):
        total_a[k] = total[:, k * chans : (k + 1) * chans].T
    emit(total_a, pieces)


def output_kernel(stacked_b, pre_grad, weight_a, weight_b, encoded, frames_grad, flat):
    core, side, _ = position()
    place = 2 * side + core
    frames, _, _, half, _ = stacked_b.shape
    rows, width, chans = frames_grad.shape[1:]
    short = rows // 2
    wide = encoded.shape[-1]
    count = short * half
    shared = jnp.zeros((count, wide), F32)
    latest = jnp.zeros((frames * count, wide), F32)
    for kh in range(3):
        lo, parity = divmod(kh, 2)
        piece = [
            stacked_b[t, pl.ds(short * place + lo, short), parity].reshape(count, 3 * chans)
            for t in range(frames)
        ]
        shared += mm(piece[0], weight_b[0, kh]) + mm(piece[0], weight_b[1, kh])
        latest += mm(jnp.concatenate(piece, axis=0), weight_b[2, kh])
    for t in range(frames):
        value = shared + latest[t * count : (t + 1) * count]
        encoded[t] = value.astype(BF16).reshape(short, half, wide)

    ext = rows + 2
    own = pre_grad[:, pl.ds(rows * place, ext)].astype(F32)
    even = own[:, :, 0:half].reshape(frames * ext, half, chans)
    odd = own[:, :, half:width].reshape(frames * ext, half, chans)
    before = shifted(odd, 1, half).astype(BF16)
    after = shifted(even, -1, half).astype(BF16)
    even_16, odd_16 = (even.astype(BF16), odd.astype(BF16))
    stacked = jnp.stack(
        [
            jnp.concatenate([odd_16, even_16, before], axis=-1),
            jnp.concatenate([after, odd_16, even_16], axis=-1),
        ],
        axis=1,
    ).reshape(frames, ext, width, 3 * chans)
    early = jnp.zeros((frames * rows * width, chans), F32)
    late = jnp.zeros((frames * rows * width, chans), F32)
    for kh in range(3):
        piece = stacked[:, 2 - kh : 2 - kh + rows].reshape(frames * rows * width, 3 * chans)
        for kt in range(3):
            taps = jnp.concatenate([weight_a[kt, kh, kw] for kw in range(3)], axis=1)
            if kt == 2:
                late += mm_nt(piece, taps)
            else:
                early += mm_nt(piece, taps)
    early = early.reshape(frames, rows, 2, half, chans)
    late = late.reshape(frames, rows, 2, half, chans)
    even = even.reshape(frames, ext, half, chans)[:, 1 : rows + 1]
    odd = odd.reshape(frames, ext, half, chans)[:, 1 : rows + 1]
    size = rows * half
    for t in range(frames):
        total = late[t]
        if t == 0:
            total = total + (early[0] + early[1])
        for parity, value in ((0, even), (1, odd)):
            summed = value[t] + total[:, parity]
            flat[pl.ds(t * 2 * size + parity, size, stride=2), :] = summed.reshape(size, chans)
    frames_grad[...] = flat[...].reshape(frames_grad.shape).astype(BF16)


def finish_kernel(scale, count, *refs):
    chans = refs[0].shape[-1]
    shared, out = (refs[2 * count : -1], refs[-1])

    def total(parts, lanes):
        value = parts[0][...].astype(F32)
        for part in parts[1:]:
            value = value + part[...].astype(F32)
        for part in shared:
            value = value + part[:, :, lanes].astype(F32)
        return (value * scale).astype(BF16)

    out[:, :, 0:chans] = total(refs[:count], slice(0, chans))
    out[:, :, chans:] = total(refs[count : 2 * count], slice(chans, None))


def assemble_kernel(places, planes, *refs):
    pieces, (out_a, out_b) = (refs[:-2], refs[-2:])
    core, side, plane = position()
    chans = out_a.shape[-1]
    rows = pieces[0].shape[1]
    for piece, (flip_core, flip_side, step) in zip(pieces, places, strict=True):
        tap = core ^ flip_core
        source = (plane - step + planes) % planes
        at = pl.multiple_of((side ^ flip_side) * (chans // 2) + source * rows, rows)
        for slot in (2 * tap, 1 + tap):
            out_a[slot, :, pl.ds(at, rows)] = piece[:, :, 0:chans]
            out_b[slot, :, pl.ds(at, rows)] = piece[:, :, chans:]


def append_kernel(places, planes, old_a, old_b, *refs):
    del old_a, old_b
    count = len(places)
    pieces, (out_a, out_b, sems) = (refs[:count], refs[count:])
    core, side, plane = position()
    chans = out_a.shape[-1]
    rows = pieces[0].shape[1]

    def each(act):
        for index, (flip_core, flip_side, step) in enumerate(places):
            tap = core ^ flip_core
            source = (plane - step + planes) % planes
            at = pl.multiple_of((side ^ flip_side) * (chans // 2) + source * rows, rows)
            for k, out in enumerate((out_a, out_b)):
                lanes = slice(0, chans) if k == 0 else slice(chans, None)
                piece = pieces[index].at[:, :, lanes]
                move = pltpu.make_async_copy(
                    piece, out.at[tap * 2, :, pl.ds(at, rows)], sems.at[index, k]
                )
                twin = pltpu.make_async_copy(
                    piece, out.at[1, :, pl.ds(at, rows)], sems.at[index, 2 + k]
                )
                act(move)
                pl.when(tap == 0)(lambda twin=twin: act(twin))

    each(lambda copy: copy.start())
    each(lambda copy: copy.wait())


def call(
    body, outs, args, scratch=(), flops=0, whole=0, limit=VMEM_LIMIT, aliases=None, size=10**4
):
    extra = {}
    if whole:
        held = pl.BlockSpec(memory_space=pl.ANY)
        inside = pl.BlockSpec(memory_space=pltpu.VMEM)
        extra["in_specs"] = [held] * whole + [inside] * (len(args) - whole)
    if aliases:
        extra["out_specs"] = (held,) * len(outs)
        extra["input_output_aliases"] = aliases
    return pl.pallas_call(
        body,
        out_shape=outs,
        scratch_shapes=scratch,
        compiler_params=pltpu.CompilerParams(vmem_limit_bytes=limit),
        cost_estimate=pl.CostEstimate(flops=flops, bytes_accessed=size, transcendentals=0),
        **extra,
    )(*args)


def on_device(frames, weight_a, weight_b, cotangent):
    count, rows, width, chans = frames.shape
    assert count == 2
    wide = weight_b.shape[-1]
    half = width // 2
    n = lax.axis_size(AXIS)
    planes = n // 4
    core, side, plane = position()
    shape = jax.ShapeDtypeStruct

    def send(value, pairs):
        return lax.ppermute(value, AXIS, pairs)

    swap_core = [(i, i ^ 1) for i in range(n)]
    swap_side = [(i, i ^ 2) for i in range(n)]
    along = []
    for k in range(0, n - 4, 4):
        along += [(k + 2, k + 6), (k + 3, k + 4), (k + 4, k + 3), (k + 5, k + 1)]

    pack, edge = call(
        edge_kernel,
        (
            shape((count, rows + rows // 2, width, chans), BF16),
            shape((count, 3, width, chans), BF16),
        ),
        (frames, cotangent),
        [pltpu.SemaphoreType.DMA((6,))],
        whole=2,
        limit=None,
        flops=4 * 10**9,
    )
    outer = jnp.where(core == side, edge, send(edge, swap_core))
    packs = [send(pack, swap_core), send(pack, swap_side), None]
    edges = [send(outer, along), None]
    edges[1] = send(edges[0], swap_core)
    packs[1], edges[0] = lax.optimization_barrier((packs[1], edges[0]))
    packs[2] = send(packs[1], swap_core)
    staged_a, staged_b = (weight_a, weight_b)

    inner = 4 * rows + 2
    kernel_a = staged_a.reshape(3, 3, 3 * chans, chans)
    kernel_b = staged_b.reshape(3, 3, 3 * chans, wide)
    part = chans // 2
    split = planes if part % (8 * planes) == 0 else 1

    def pieces_of(outputs):
        own = (9, part // split, outputs)
        return (shape(own, F32),) + (shape(own, BF16),) * (split - 1)

    def forward(*refs):
        forward_kernel(split, *refs)

    far = split // 2
    joins = tuple(step for step in range(1, split) if step != far)

    def backward(*refs):
        backward_kernel(planes - 1, joins, *refs)

    *pieces_b, pre, stacked_a, stacked_b, cot = call(
        forward,
        pieces_of(wide)
        + (
            shape((count, inner, width, chans), F32),
            shape((count, inner + 2, width, 3 * chans), BF16),
            shape((count, inner // 2, 2, half, 3 * chans), BF16),
            shape((count, 2 * rows + 2, half, wide), BF16),
        ),
        (frames, cotangent, *packs, *edges, kernel_a),
        [
            pltpu.VMEM((count * (inner + 2) * width, chans), F32),
            pltpu.VMEM((9, chans, wide), F32),
        ],
        flops=10**7,
    )
    shapes_a = list(pieces_of(chans))
    for step in joins:
        shapes_a[step] = shape((9, part // split, chans + wide), BF16)
    joined = tuple(pieces_b[step] for step in joins)
    *pieces_a, pre_grad = call(
        backward,
        (*shapes_a, shape((count, inner, width, chans), BF16)),
        (cot, pre, stacked_a, staged_b, *joined),
        [pltpu.VMEM((9, chans, chans), F32)],
        flops=10**7,
    )
    def outputs(stacked_b):
        return call(
            output_kernel,
            (shape(cotangent.shape, BF16), shape(frames.shape, BF16)),
            (stacked_b, pre_grad, staged_a, kernel_b),
            [pltpu.VMEM((count * rows * width, chans), F32)],
            flops=10**7,
        )

    scale = (count * rows * n * width) ** (-0.5)
    if split != planes:
        encoded, frames_grad = outputs(stacked_b)
        taps = jnp.arange(2)[:, None, None, None, None] == core
        sides = jnp.arange(2)[None, None, :, None, None] == side
        both = []
        for value in (pieces_a[0], pieces_b[0]):
            slots = jnp.where(taps & sides, value[None, :, None], 0.0)
            total = lax.psum(slots, AXIS) * scale
            total = total.astype(BF16).reshape(2, 3, 3, chans, -1)
            both.append(jnp.concatenate([total[:1], total], axis=0))
        return (encoded, frames_grad, both[0], both[1])

    rotations = [[(i, (i + 4 * step) % n) for i in range(n)] for step in range(planes)]
    alone_a, alone_b = (pieces_a[:1], pieces_b[:1])
    if far:
        alone_b.append(send(pieces_b[far], rotations[far]))
        gate = lax.optimization_barrier((alone_b[1], pieces_a[far]))
        alone_b[1], pieces_a[far] = gate
        alone_a.append(send(pieces_a[far], rotations[far]))
    both = [send(pieces_a[step], rotations[step]) for step in joins]

    def finish(*refs):
        finish_kernel(scale, len(alone_a), *refs)

    encoded, frames_grad = outputs(stacked_b)
    held = lax.optimization_barrier((alone_a[0], encoded, frames_grad))
    alone_a[0], encoded, frames_grad = held
    piece = shape((9, part // planes, chans + wide), BF16)
    (own,) = call(finish, (piece,), (*alone_a, *alone_b, *both))
    column = {(0, 0, 0): own}
    order = sorted(range(1, planes), key=lambda step: min(step, planes - step))
    for step in order[:-1]:
        column[0, 0, step] = send(own, rotations[step])
    if planes == 1:
        column[0, 1, 0] = send(own, swap_side)
    else:
        distant = (0, 0, order[-1])
        column[distant] = send(own, rotations[order[-1]])
        for step in (0, *order[:-1]):
            column[0, 1, step] = send(column[0, 0, step], swap_side)
        if len(order) > 1:
            key = (0, 1, order[0])
            column[distant], column[key] = lax.optimization_barrier((column[distant], column[key]))
        column[0, 1, distant[2]] = send(column[distant], swap_side)
    last = (0, 1, order[-1] if order else 0)
    for (_, flip, step), value in list(column.items()):
        if (0, flip, step) != last:
            column[1, flip, step] = send(value, swap_core)
    slow = column.pop(last)
    tail = {key: column.pop(key) for key in list(column) if key[1] and key[2]}
    places = tuple(column)

    def assemble(*refs):
        assemble_kernel(places, planes, *refs)

    grads = call(
        assemble,
        (shape((3, 9, chans, chans), BF16), shape((3, 9, chans, wide), BF16)),
        tuple(column.values()),
        flops=4 * 10**9,
    )

    def append(grads, pieces):
        ends = tuple(pieces)

        def body(*refs):
            append_kernel(ends, planes, *refs)

        return call(
            body,
            tuple(shape(x.shape, x.dtype) for x in grads),
            (*grads, *pieces.values()),
            [pltpu.SemaphoreType.DMA((len(ends), 4))],
            whole=2,
            aliases={0: 0, 1: 1},
        )

    if tail:
        grads = append(grads, tail)
    slow, *grads = lax.optimization_barrier((slow, *grads))
    grad_a, grad_b = append(grads, {last: slow, (1, *last[1:]): send(slow, swap_core)})
    return (encoded, frames_grad, grad_a.reshape(weight_a.shape), grad_b.reshape(weight_b.shape))


def solution(mesh):
    in_specs = (P("groups", "height", None, None), P(), P(), P("groups", "height", None, None))
    out_specs = (
        P("groups", "height", None, None),
        P("groups", "height", None, None),
        P("groups", None, None, None, None),
        P("groups", None, None, None, None),
    )
    return jax.shard_map(
        on_device, mesh=mesh, in_specs=in_specs, out_specs=out_specs, check_vma=False
    )
```

```python
import jax
import jax.numpy as jnp
from jax import lax
from jax.experimental import pallas as pl
from jax.experimental.pallas import tpu as pltpu
from jax.sharding import PartitionSpec as P

F32 = jnp.float32
BF16 = jnp.bfloat16
AXIS = "height"
VMEM_LIMIT = 24 * 1024 * 1024


def position():
    index = lax.axis_index(AXIS)
    return (index % 2, (index // 2) % 2, index // 4)


def folded(weight, kt, *taps):
    if kt:
        return weight[(2, *taps)]
    return (weight[(0, *taps)].astype(F32) + weight[(1, *taps)].astype(F32)).astype(BF16)


def emit(total, outs):
    _, side, plane = position()
    part = total.shape[1] // 2
    count = len(outs)
    rows = part // count
    for step, out in enumerate(outs):
        owner = (plane + step) % count if count > 1 else 0
        at = pl.multiple_of(side * part + owner * rows, rows)
        value = total[:, pl.ds(at, rows)].astype(out.dtype)
        out[:, :, 0 : value.shape[-1]] = value


def mm(a, b):
    return lax.dot_general(a, b, (((1,), (0,)), ((), ())), preferred_element_type=F32)


def mm_nt(a, b):
    return lax.dot_general(a, b, (((1,), (1,)), ((), ())), preferred_element_type=F32)


def mm_tn(a, b):
    return lax.dot_general(a, b, (((0,), (0,)), ((), ())), preferred_element_type=F32)


def shifted(field, by, half):
    rows, _, chans = field.shape
    flat = field.reshape(rows * half, chans)
    column = lax.broadcasted_iota(jnp.int32, flat.shape, 0) % half
    moved = pltpu.roll(flat, by % (rows * half), axis=0)
    edge = 0 if by > 0 else half - 1
    return jnp.where(column == edge, 0.0, moved).reshape(field.shape)


def wide_pair(even, odd, half):
    before = shifted(odd, 1, half).astype(BF16)
    after = shifted(even, -1, half).astype(BF16)
    even, odd = (even.astype(BF16), odd.astype(BF16))
    return (
        jnp.concatenate([before, even, odd], axis=-1),
        jnp.concatenate([even, odd, after], axis=-1),
    )


def edge_kernel(frames, cot, pack, edge, sems):
    core, _, _ = position()
    rows, width = frames.shape[1:3]
    short, half = cot.shape[1:3]
    chans = frames.shape[-1]
    first = pl.ds(core * (rows - 2), 2)
    only = pl.ds(core * (short - 1), 1)
    moves = [(frames.at[:, first], edge.at[:, 0:2]), (frames, pack.at[:, 0:rows])]
    for k in range(2):
        lanes = slice(k * chans, (k + 1) * chans)
        columns = slice(k * half, (k + 1) * half)
        moves.append((cot.at[:, only, :, lanes], edge.at[:, 2:3, columns]))
        moves.append((cot.at[:, :, :, lanes], pack.at[:, rows:, columns]))
    copies = [pltpu.make_async_copy(*move, sems.at[k]) for k, move in enumerate(moves)]
    for copy in copies:
        copy.start()
    for copy in copies:
        copy.wait()


def forward_kernel(split, *refs):
    own_f, own_g, packs, edges, weight_a = (*refs[0:2], refs[2:5], refs[5:7], refs[7])
    outs, flat, total_b = (refs[8:-2], refs[-2], refs[-1])
    pieces, (pre_ref, stacked_a, stacked_b, cot_ref) = (outs[:split], outs[split:])
    core, side, plane = position()
    place = 2 * side + core
    frames, rows, width, chans = own_f.shape
    short = rows // 2
    half = width // 2
    ext = 4 * rows + 4
    block = rows * width

    def edge(t, own):
        chosen = jnp.where(core == own, edges[0][t].astype(F32), edges[1][t].astype(F32))
        cot = jnp.concatenate([chosen[2, 0:half], chosen[2, half:]], axis=-1)
        return (chosen[0:2].reshape(2 * width, chans), cot.astype(BF16))

    for t in range(frames):
        base = t * ext * width
        flat[base : base + 2 * width], cot_ref[t, 0] = edge(t, 0)
        low = base + (ext - 2) * width
        flat[low : low + 2 * width], cot_ref[t, 4 * short + 1] = edge(t, 1)
        for k in range(4):
            at = pl.multiple_of(base + 2 * width + (place ^ k) * block, 2 * width)
            spot = pl.ds(1 + (place ^ k) * short, short)
            if k == 0:
                field, cot = (own_f[t], own_g[t])
            else:
                pack = packs[k - 1]
                cot = (pack[t, rows:, 0:half], pack[t, rows:, half:])
                field, cot = (pack[t, 0:rows], jnp.concatenate(cot, axis=-1))
            flat[pl.ds(at, block)] = field.astype(F32).reshape(block, chans)
            cot_ref[t, spot] = cot
    count = frames * ext
    even = flat[pl.ds(0, count * half, stride=2), :].reshape(count, half, chans)
    odd = flat[pl.ds(1, count * half, stride=2), :].reshape(count, half, chans)
    taps_even, taps_odd = wide_pair(even, odd, half)
    stacked_a[:, :, 0:half] = taps_even.reshape(frames, ext, half, 3 * chans)
    stacked_a[:, :, half:width] = taps_odd.reshape(frames, ext, half, 3 * chans)

    inner = ext - 2
    taps = [
        jnp.concatenate([folded(weight_a, kt, kh) for kh in range(3)], axis=0) for kt in range(2)
    ]
    fields = [
        jnp.concatenate(
            [
                stacked_a[t, kh : kh + inner].reshape(inner * width, 3 * chans)
                for kh in range(3)
            ],
            axis=1,
        )
        for t in range(2)
    ]
    early = mm(fields[0], jnp.concatenate(taps, axis=1))
    shared = early[:, :chans]
    latest = [early[:, chans:], mm(fields[1], taps[1])]
    even = even.reshape(frames, ext, half, chans)
    odd = odd.reshape(frames, ext, half, chans)
    outside = plane == 0
    row = lax.broadcasted_iota(jnp.int32, (inner, half, chans), 0)
    hidden = outside & (row == 0)
    for t in range(frames):
        conv = (shared + latest[t]).reshape(inner, 2, half, chans)
        pre_even = even[t, 1 : ext - 1] + conv[:, 0]
        pre_odd = odd[t, 1 : ext - 1] + conv[:, 1]
        pre_ref[t, :, 0:half] = pre_even
        pre_ref[t, :, half:width] = pre_odd
        act_even = jnp.where(hidden, 0.0, pre_even * jax.nn.sigmoid(pre_even))
        act_odd = jnp.where(hidden, 0.0, pre_odd * jax.nn.sigmoid(pre_odd))
        stacked_b[t] = jnp.concatenate(
            [
                shifted(act_odd, 1, half).astype(BF16),
                act_even.astype(BF16),
                act_odd.astype(BF16),
            ],
            axis=-1,
        ).reshape(inner // 2, 2, half, 3 * chans)
    wide = cot_ref.shape[-1]
    tall = 4 * short
    grads = [cot_ref[t, 1 : tall + 1].reshape(tall * half, wide) for t in range(frames)]
    grad = jnp.concatenate(grads, axis=0)
    for kh in range(3):
        lo, parity = divmod(kh, 2)
        piece = [
            stacked_b[t, lo : lo + tall, parity].reshape(tall * half, 3 * chans)
            for t in (0, core)
        ]
        total = mm_tn(jnp.concatenate(piece, axis=0), grad)
        total_b[3 * kh : 3 * kh + 3] = total.reshape(3, chans, wide)
    emit(total_b, pieces)


def backward_kernel(last, joins, cot_ref, pre_ref, stacked_a, weight_b, *refs):
    given, refs = (refs[: len(joins)], refs[len(joins) :])
    for step, piece in zip(joins, given, strict=True):
        refs[step][:, :, weight_b.shape[3] :] = piece[...]
    pieces, (pre_grad, total_a) = (refs[:-2], refs[-2:])
    core, side, plane = position()
    frames, ext_g, half, wide = cot_ref.shape
    chans = weight_b.shape[3]
    inner = pre_ref.shape[1]
    width = 2 * half
    mid = inner // 2
    cot = cot_ref[...].reshape(frames * ext_g, half, wide)
    ahead = shifted(cot.astype(F32), -1, half).astype(BF16)
    both = jnp.concatenate([cot, ahead], axis=-1).reshape(frames, ext_g, half, 2 * wide)
    later = both[:, 1:].reshape(frames * mid * half, 2 * wide)
    sooner = both[:, :-1].reshape(frames * mid * half, 2 * wide)
    zero = jnp.zeros((chans, wide), BF16)

    def taps(kt, kh):
        left, mid, right = (folded(weight_b, kt, kh, kw) for kw in range(3))
        return jnp.concatenate(
            [
                jnp.concatenate([mid, zero], axis=1),
                jnp.concatenate([right, left], axis=1),
            ],
            axis=0,
        )

    def rows_of(kt):
        even = mm_nt(later, taps(kt, 1))
        odd = mm_nt(later, taps(kt, 0)) + mm_nt(sooner, taps(kt, 2))
        shape = (frames, mid, half, 2 * chans)
        return (even.reshape(shape), odd.reshape(shape))

    copies = [rows_of(kt) for kt in range(2)]
    row = lax.broadcasted_iota(jnp.int32, (inner, half, chans), 0)
    hidden = ((plane == 0) & (row == 0)) | ((plane == last) & (row == inner - 1))
    for t in range(frames):
        sums = []
        for parity in range(2):
            total = copies[1][parity][t]
            if t == 0:
                total = total + (copies[0][parity][0] + copies[0][parity][1])
            sums.append(total)
        grad = jnp.stack([sums[1], sums[0]], axis=1).reshape(inner, half, 2 * chans)
        for parity in range(2):
            act_grad = grad[:, :, parity * chans : (parity + 1) * chans]
            pre = pre_ref[t, :, parity * half : (parity + 1) * half]
            sig = jax.nn.sigmoid(pre)
            value = act_grad * sig * (1.0 + pre * (1.0 - sig))
            value = jnp.where(hidden, 0.0, value).astype(BF16)
            pre_grad[t, :, parity * half : (parity + 1) * half] = value
    rows = inner - 2
    grads = [pre_grad[t, 1 : rows + 1].reshape(rows * width, chans) for t in range(frames)]
    grad = jnp.concatenate(grads, axis=0)
    field = jnp.concatenate(
        [
            jnp.concatenate(
                [
                    stacked_a[t, kh + 1 : kh + 1 + rows].reshape(rows * width, 3 * chans)
                    for t in (0, core)
                ],
                axis=0,
            )
            for kh in range(3)
        ],
        axis=1,
    )
    total = mm(grad.T, field)
    for k in range(9):
        total_a[k] = total[:, k * chans : (k + 1) * chans].T
    emit(total_a, pieces)


def output_kernel(stacked_b, pre_grad, weight_a, weight_b, encoded, frames_grad, flat):
    core, side, _ = position()
    place = 2 * side + core
    frames, _, _, half, _ = stacked_b.shape
    rows, width, chans = frames_grad.shape[1:]
    short = rows // 2
    wide = encoded.shape[-1]
    count = short * half
    shared = jnp.zeros((count, wide), F32)
    latest = jnp.zeros((frames * count, wide), F32)
    for kh in range(3):
        lo, parity = divmod(kh, 2)
        piece = [
            stacked_b[t, pl.ds(short * place + lo, short), parity].reshape(count, 3 * chans)
            for t in range(frames)
        ]
        shared += mm(piece[0], weight_b[0, kh]) + mm(piece[0], weight_b[1, kh])
        latest += mm(jnp.concatenate(piece, axis=0), weight_b[2, kh])
    for t in range(frames):
        value = shared + latest[t * count : (t + 1) * count]
        encoded[t] = value.astype(BF16).reshape(short, half, wide)

    ext = rows + 2
    own = pre_grad[:, pl.ds(rows * place, ext)].astype(F32)
    even = own[:, :, 0:half].reshape(frames * ext, half, chans)
    odd = own[:, :, half:width].reshape(frames * ext, half, chans)
    before = shifted(odd, 1, half).astype(BF16)
    after = shifted(even, -1, half).astype(BF16)
    even_16, odd_16 = (even.astype(BF16), odd.astype(BF16))
    stacked = jnp.stack(
        [
            jnp.concatenate([odd_16, even_16, before], axis=-1),
            jnp.concatenate([after, odd_16, even_16], axis=-1),
        ],
        axis=1,
    ).reshape(frames, ext, width, 3 * chans)
    early = jnp.zeros((frames * rows * width, chans), F32)
    late = jnp.zeros((frames * rows * width, chans), F32)
    for kh in range(3):
        piece = stacked[:, 2 - kh : 2 - kh + rows].reshape(frames * rows * width, 3 * chans)
        for kt in range(3):
            taps = jnp.concatenate([weight_a[kt, kh, kw] for kw in range(3)], axis=1)
            if kt == 2:
                late += mm_nt(piece, taps)
            else:
                early += mm_nt(piece, taps)
    early = early.reshape(frames, rows, 2, half, chans)
    late = late.reshape(frames, rows, 2, half, chans)
    even = even.reshape(frames, ext, half, chans)[:, 1 : rows + 1]
    odd = odd.reshape(frames, ext, half, chans)[:, 1 : rows + 1]
    size = rows * half
    for t in range(frames):
        total = late[t]
        if t == 0:
            total = total + (early[0] + early[1])
        for parity, value in ((0, even), (1, odd)):
            summed = value[t] + total[:, parity]
            flat[pl.ds(t * 2 * size + parity, size, stride=2), :] = summed.reshape(size, chans)
    frames_grad[...] = flat[...].reshape(frames_grad.shape).astype(BF16)


def finish_kernel(scale, count, *refs):
    chans = refs[0].shape[-1]
    shared, out = (refs[2 * count : -1], refs[-1])

    def total(parts, lanes):
        value = parts[0][...].astype(F32)
        for part in parts[1:]:
            value = value + part[...].astype(F32)
        for part in shared:
            value = value + part[:, :, lanes].astype(F32)
        return (value * scale).astype(BF16)

    out[:, :, 0:chans] = total(refs[:count], slice(0, chans))
    out[:, :, chans:] = total(refs[count : 2 * count], slice(chans, None))


def assemble_kernel(places, planes, *refs):
    pieces, (out_a, out_b) = (refs[:-2], refs[-2:])
    core, side, plane = position()
    chans = out_a.shape[-1]
    rows = pieces[0].shape[1]
    for piece, (flip_core, flip_side, step) in zip(pieces, places, strict=True):
        tap = core ^ flip_core
        source = (plane - step + planes) % planes
        at = pl.multiple_of((side ^ flip_side) * (chans // 2) + source * rows, rows)
        for slot in (2 * tap, 1 + tap):
            out_a[slot, :, pl.ds(at, rows)] = piece[:, :, 0:chans]
            out_b[slot, :, pl.ds(at, rows)] = piece[:, :, chans:]


def append_kernel(places, planes, old_a, old_b, *refs):
    del old_a, old_b
    count = len(places)
    pieces, (out_a, out_b, sems) = (refs[:count], refs[count:])
    core, side, plane = position()
    chans = out_a.shape[-1]
    rows = pieces[0].shape[1]

    def each(act):
        for index, (flip_core, flip_side, step) in enumerate(places):
            tap = core ^ flip_core
            source = (plane - step + planes) % planes
            at = pl.multiple_of((side ^ flip_side) * (chans // 2) + source * rows, rows)
            for k, out in enumerate((out_a, out_b)):
                lanes = slice(0, chans) if k == 0 else slice(chans, None)
                piece = pieces[index].at[:, :, lanes]
                move = pltpu.make_async_copy(
                    piece, out.at[tap * 2, :, pl.ds(at, rows)], sems.at[index, k]
                )
                twin = pltpu.make_async_copy(
                    piece, out.at[1, :, pl.ds(at, rows)], sems.at[index, 2 + k]
                )
                act(move)
                pl.when(tap == 0)(lambda twin=twin: act(twin))

    each(lambda copy: copy.start())
    each(lambda copy: copy.wait())


def call(
    body, outs, args, scratch=(), flops=0, whole=0, limit=VMEM_LIMIT, aliases=None, size=10**4
):
    extra = {}
    if whole:
        held = pl.BlockSpec(memory_space=pl.ANY)
        inside = pl.BlockSpec(memory_space=pltpu.VMEM)
        extra["in_specs"] = [held] * whole + [inside] * (len(args) - whole)
    if aliases:
        extra["out_specs"] = (held,) * len(outs)
        extra["input_output_aliases"] = aliases
    return pl.pallas_call(
        body,
        out_shape=outs,
        scratch_shapes=scratch,
        compiler_params=pltpu.CompilerParams(vmem_limit_bytes=limit),
        cost_estimate=pl.CostEstimate(flops=flops, bytes_accessed=size, transcendentals=0),
        **extra,
    )(*args)


def on_device(frames, weight_a, weight_b, cotangent):
    count, rows, width, chans = frames.shape
    assert count == 2
    wide = weight_b.shape[-1]
    half = width // 2
    n = lax.axis_size(AXIS)
    planes = n // 4
    core, side, plane = position()
    shape = jax.ShapeDtypeStruct

    def send(value, pairs):
        return lax.ppermute(value, AXIS, pairs)

    swap_core = [(i, i ^ 1) for i in range(n)]
    swap_side = [(i, i ^ 2) for i in range(n)]
    along = []
    for k in range(0, n - 4, 4):
        along += [(k + 2, k + 6), (k + 3, k + 4), (k + 4, k + 3), (k + 5, k + 1)]

    pack, edge = call(
        edge_kernel,
        (
            shape((count, rows + rows // 2, width, chans), BF16),
            shape((count, 3, width, chans), BF16),
        ),
        (frames, cotangent),
        [pltpu.SemaphoreType.DMA((6,))],
        whole=2,
        limit=None,
        flops=4 * 10**9,
    )
    outer = jnp.where(core == side, edge, send(edge, swap_core))
    packs = [send(pack, swap_core), send(pack, swap_side), None]
    edges = [send(outer, along), None]
    edges[1] = send(edges[0], swap_core)
    packs[1], edges[0] = lax.optimization_barrier((packs[1], edges[0]))
    packs[2] = send(packs[1], swap_core)
    staged_a, staged_b = (weight_a, weight_b)

    inner = 4 * rows + 2
    kernel_a = staged_a.reshape(3, 3, 3 * chans, chans)
    kernel_b = staged_b.reshape(3, 3, 3 * chans, wide)
    part = chans // 2
    split = planes if part % (8 * planes) == 0 else 1

    def pieces_of(outputs):
        own = (9, part // split, outputs)
        return (shape(own, F32),) + (shape(own, BF16),) * (split - 1)

    def forward(*refs):
        forward_kernel(split, *refs)

    far = split // 2
    joins = tuple(step for step in range(1, split) if step != far)

    def backward(*refs):
        backward_kernel(planes - 1, joins, *refs)

    *pieces_b, pre, stacked_a, stacked_b, cot = call(
        forward,
        pieces_of(wide)
        + (
            shape((count, inner, width, chans), F32),
            shape((count, inner + 2, width, 3 * chans), BF16),
            shape((count, inner // 2, 2, half, 3 * chans), BF16),
            shape((count, 2 * rows + 2, half, wide), BF16),
        ),
        (frames, cotangent, *packs, *edges, kernel_a),
        [
            pltpu.VMEM((count * (inner + 2) * width, chans), F32),
            pltpu.VMEM((9, chans, wide), F32),
        ],
        flops=10**7,
    )
    shapes_a = list(pieces_of(chans))
    for step in joins:
        shapes_a[step] = shape((9, part // split, chans + wide), BF16)
    joined = tuple(pieces_b[step] for step in joins)
    *pieces_a, pre_grad = call(
        backward,
        (*shapes_a, shape((count, inner, width, chans), BF16)),
        (cot, pre, stacked_a, staged_b, *joined),
        [pltpu.VMEM((9, chans, chans), F32)],
        flops=10**7,
    )
    def outputs(stacked_b):
        return call(
            output_kernel,
            (shape(cotangent.shape, BF16), shape(frames.shape, BF16)),
            (stacked_b, pre_grad, staged_a, kernel_b),
            [pltpu.VMEM((count * rows * width, chans), F32)],
            flops=10**7,
        )

    scale = (count * rows * n * width) ** (-0.5)
    if split != planes:
        encoded, frames_grad = outputs(stacked_b)
        taps = jnp.arange(2)[:, None, None, None, None] == core
        sides = jnp.arange(2)[None, None, :, None, None] == side
        both = []
        for value in (pieces_a[0], pieces_b[0]):
            slots = jnp.where(taps & sides, value[None, :, None], 0.0)
            total = lax.psum(slots, AXIS) * scale
            total = total.astype(BF16).reshape(2, 3, 3, chans, -1)
            both.append(jnp.concatenate([total[:1], total], axis=0))
        return (encoded, frames_grad, both[0], both[1])

    rotations = [[(i, (i + 4 * step) % n) for i in range(n)] for step in range(planes)]
    alone_a, alone_b = (pieces_a[:1], pieces_b[:1])
    if far:
        alone_b.append(send(pieces_b[far], rotations[far]))
        gate = lax.optimization_barrier((alone_b[1], pieces_a[far]))
        alone_b[1], pieces_a[far] = gate
        alone_a.append(send(pieces_a[far], rotations[far]))
    both = [send(pieces_a[step], rotations[step]) for step in joins]

    def finish(*refs):
        finish_kernel(scale, len(alone_a), *refs)

    encoded, frames_grad = outputs(stacked_b)
    held = lax.optimization_barrier((alone_a[0], encoded, frames_grad))
    alone_a[0], encoded, frames_grad = held
    piece = shape((9, part // planes, chans + wide), BF16)
    (own,) = call(finish, (piece,), (*alone_a, *alone_b, *both))
    column = {(0, 0, 0): own}
    order = sorted(range(planes - 1, 0, -1), key=lambda step: min(step, planes - step))
    for step in order[:-1]:
        column[0, 0, step] = send(own, rotations[step])
    if planes == 1:
        column[0, 1, 0] = send(own, swap_side)
    else:
        distant = (0, 0, order[-1])
        column[distant] = send(own, rotations[order[-1]])
        for step in (0, *order[:-1]):
            column[0, 1, step] = send(column[0, 0, step], swap_side)
        if len(order) > 1:
            key = (0, 1, order[0])
            column[distant], column[key] = lax.optimization_barrier((column[distant], column[key]))
        column[0, 1, distant[2]] = send(column[distant], swap_side)
    last = (0, 1, order[-1] if order else 0)
    for (_, flip, step), value in list(column.items()):
        if (0, flip, step) != last:
            column[1, flip, step] = send(value, swap_core)
    slow = column.pop(last)
    tail = {key: column.pop(key) for key in list(column) if key[1] and key[2]}
    places = tuple(column)

    def assemble(*refs):
        assemble_kernel(places, planes, *refs)

    grads = call(
        assemble,
        (shape((3, 9, chans, chans), BF16), shape((3, 9, chans, wide), BF16)),
        tuple(column.values()),
        flops=4 * 10**9,
    )

    def append(grads, pieces):
        ends = tuple(pieces)

        def body(*refs):
            append_kernel(ends, planes, *refs)

        return call(
            body,
            tuple(shape(x.shape, x.dtype) for x in grads),
            (*grads, *pieces.values()),
            [pltpu.SemaphoreType.DMA((len(ends), 4))],
            whole=2,
            aliases={0: 0, 1: 1},
        )

    if tail:
        grads = append(grads, tail)
    slow, *grads = lax.optimization_barrier((slow, *grads))
    grad_a, grad_b = append(grads, {last: slow, (1, *last[1:]): send(slow, swap_core)})
    return (encoded, frames_grad, grad_a.reshape(weight_a.shape), grad_b.reshape(weight_b.shape))


def solution(mesh):
    in_specs = (P("groups", "height", None, None), P(), P(), P("groups", "height", None, None))
    out_specs = (
        P("groups", "height", None, None),
        P("groups", "height", None, None),
        P("groups", None, None, None, None),
        P("groups", None, None, None, None),
    )
    return jax.shard_map(
        on_device, mesh=mesh, in_specs=in_specs, out_specs=out_specs, check_vma=False
    )
```
